32 devices in a mesh: grp: 2 (over y), kz: 4 (over z), coil: 2 (over x), kx: 2 (over core).
Axes of the slice: x: 2, y: 2, z: 4, core: 2. Of those that a mesh axis runs over, the one named last changes fastest.
Arguments:
- measured: float32 [2, 64, 32, 32, 32], P(None, ('grp', 'coil'), 'kx', 'kz'), parts along dimension 1, may hold values from -6 to 6
- mask: int32 [64, 32, 32], P(('grp', 'kx'), 'kz'), parts along dimension 0, may hold values 0 or 1
- kernel: float32 [27, 2, 32, 64], P(None, None, 'coil'), may hold values from -0.109375 to 0.109375
Outputs:
- restored: float32 [2, 64, 32, 32, 32], P(None, ('grp', 'coil'), 'kx', 'kz'), parts along dimension 1
The draws below stay inside these ranges and needn't reach their ends.
There are 2 independent parts, one for each index of `grp`. The reference program is written for one: setup_inputs(seed, part) draws one part's arguments, and reference() takes and returns one part's arrays. A program takes and returns all parts, laid end to end along the dimension named above; an argument that names none is the same for every part. Nothing has to cross between parts.
All inputs are finite; a program needn't handle non-finite values. No bound on the sum of `mask` on one device may be relied on, other than what follows from the above.
Results may differ from the reference program's by a relative error of at most 0.0001.
Values sent between devices are 32-bit elements; how exact they have to be, the bound alone decides.
A program may use at most 128 MiB of HBM per device.

```python
import jax
import jax.numpy as jnp
from jax import lax

COILS = 32
KX = 32
KY = 32
ITERS = 2
TAPS = 27
KZ = 32


def touch_ends(drawn, rng, low, largest):
    longest = drawn.shape.index(max(drawn.shape))
    spots = []
    for shift in (0, 1):
        where = [jax.random.randint(jax.random.fold_in(rng, axis), (), 0, length) for axis, length in enumerate(drawn.shape)]
        where[longest] = (where[longest] + shift) % drawn.shape[longest]
        spots.append(tuple(where))
    return drawn.at[spots[0]].set(low).at[spots[1]].set(largest)


def steps_of(own_key, shape, shards, low, high):
    loudness = 1.0
    for position, parts in shards:
        heights = jax.random.uniform(jax.random.fold_in(jax.random.fold_in(own_key, 6), position), (parts,), jnp.float32, low / len(shards), high / len(shards))
        loudness = loudness * jnp.repeat(jnp.exp(heights), shape[position] // parts).reshape((-1,) + (1,) * (len(shape) - 1 - position))
    return loudness


def bell_draw(key, extent, width, bound, shards=(), kind=jnp.bfloat16):
    entries = jax.random.normal(key, extent, jnp.float32) * width
    if len(shards) > 0:
        entries = steps_of(key, extent, shards, -0.22, 0.18) * entries
    return jnp.clip(entries, min=-bound, max=bound).astype(kind)


def setup_inputs(seed: int = 0, part: int = 0) -> dict:
    key_list = jax.random.split(jax.random.key(seed), 4)
    part_keys = jax.random.split(jax.random.fold_in(key_list[3], part), 4)
    measured = bell_draw(part_keys[0], (2, COILS, KX, KZ, KY), 1.0, 6.0, ((1, 2), (2, 2), (3, 4)), jnp.float32)
    mask = touch_ends((jax.random.randint(part_keys[1], (KX, KZ, KY), 0, 2) < 1).astype(jnp.int32), jax.random.fold_in(part_keys[1], 1), 0, 1)
    kernel = bell_draw(key_list[2], (TAPS, 2, COILS, 2 * COILS), (108 * COILS) ** -0.5, 0.109375, ((2, 2),), jnp.float32)
    return {"measured": measured, "mask": mask, "kernel": kernel}


def reference(measured, mask, kernel):
    sampled = (mask == 1)[None, None]
    state = jnp.where(sampled, measured, jnp.zeros_like(measured))
    real_k = kernel[:, 0]
    imag_k = kernel[:, 1]
    weights = jnp.concatenate([jnp.concatenate([real_k, -imag_k], 2), jnp.concatenate([imag_k, real_k], 2)], 1)
    sign = jnp.array([1.0, -1.0], jnp.float32).reshape(2, 1, 1, 1, 1)
    for step in range(ITERS):
        virtual = jnp.flip(state, (2, 3, 4)) * sign
        stacked = jnp.concatenate([state, virtual], 1)
        padded = jnp.pad(stacked, ((0, 0), (0, 0), (1, 1), (1, 1), (1, 1)))
        result = jnp.zeros(state.shape, jnp.float32)
        for first in range(3):
            for second in range(3):
                for third in range(3):
                    window = padded[:, :, first:first + KX, third:third + KZ, second:second + KY]
                    window = window.reshape(4 * COILS, -1)
                    term = jnp.dot(weights[9 * first + 3 * second + third], window, precision=lax.Precision.HIGHEST)
                    result = result + term.reshape(state.shape)
        state = jnp.where(sampled, measured, result)
    return state
```

```python
import functools

import jax
import jax.numpy as jnp
from jax import lax
from jax.experimental import pallas as pl
from jax.experimental.pallas import tpu as pltpu
from jax.sharding import PartitionSpec as P

ITERS = 2
TAPS = 27
CHUNK = 2
MESH = pl.DeviceIdType.MESH
F32, BF16 = jnp.float32, jnp.bfloat16
NT = (((1,), (1,)), ((), ()))


def split(x):
    hi = x.astype(BF16)
    return hi, (x - hi.astype(F32)).astype(BF16)


def reversal(n):
    i = lax.broadcasted_iota(jnp.int32, (n, n), 0) + lax.broadcasted_iota(jnp.int32, (n, n), 1)
    return jnp.where(i == n - 1, 1.0, 0.0).astype(BF16)


def body(sizes, measured, mask, kernel, out, hd, hm, rb, mb, kb, w, st, mt, xb, hz, hg, hq, ob, fr,
         s_send, s_recv, v_send, v_recv, k_send, k_recv, m_send, m_recv, h_send, h_recv, os_send, os_recv, ov_send, ov_recv):
    nz, nc = sizes
    _, coils, depth_x, planes, row = measured.shape
    half = nz // 2
    groups = 2 * nc
    g = depth_x // groups
    lanes = g * row
    band = nc * coils
    chans = 4 * band
    wide = 2 * chans

    z, c, h = lax.axis_index("kz"), lax.axis_index("coil"), lax.axis_index("kx")
    side = lax.div(z, half)
    far = nz - 1 - z
    eq = lax.rem(side + h + 1, 2)

    def pos(zz, cx):
        turn = lax.rem(lax.min(zz, nz - 1 - zz), 2)
        return turn * (nc - 1 - cx) + (1 - turn) * cx

    cc = pos(z, c)

    def own_group(at):
        return eq * at + (1 - eq) * (groups - 1 - at)

    def coil_at(d):
        return lax.rem(c + d, nc)

    def neighbour(dz, dc):
        zt = z + dz
        good = (zt >= 0) & (zt < nz)
        zt = lax.max(lax.min(zt, nz - 1), 0)
        over = lax.rem(lax.div(zt, half) + side, 2)
        inter = lax.div(cc + 1, nc) if dc > 0 else 0
        core = 1 - lax.min(cc, 1) if dc < 0 else 0
        if dc < 0:
            good = good & ((side == 1) | (cc > 0))
        flip = lax.rem(over + inter, 2)
        tz = flip * (nz - 1 - zt) + (1 - flip) * zt
        tcc = cc + dc - inter + core
        th = lax.rem(h + flip + core, 2)
        sz, sc = (dz + 1) // 2, (dc + 1) // 2
        stay = inter + core
        tsz = flip * sz + (1 - flip) * (1 - sz)
        tsc = stay * sc + (1 - stay) * (1 - sc)
        alone = (over * core == 1) & good
        return dict(good=good & jnp.logical_not(alone), alone=alone, flip=flip,
                    device={"kz": tz, "coil": pos(tz, tcc), "kx": th}, sz=sz, sc=sc, tsz=tsz, tsc=tsc)

    dirs = [(dz, dc) for dz in (-1, 0, 1) for dc in (-1, 0, 1) if dz or dc]
    near = {d: neighbour(*d) for d in dirs}
    maybe_alone = [(-1, -1), (1, -1)]

    barrier = pltpu.get_barrier_semaphore()
    for d in range(nc):
        if d:
            pl.semaphore_signal(barrier, inc=1, device_id={"coil": coil_at(d)}, device_id_type=MESH)
        pl.semaphore_signal(barrier, inc=1, device_id={"kz": far, "coil": coil_at(d), "kx": 1 - h}, device_id_type=MESH)
    count = 2 * nc - 1
    for d in dirs:
        @pl.when(near[d]["good"])
        def _():
            pl.semaphore_signal(barrier, inc=1, device_id=near[d]["device"], device_id_type=MESH)
        count = count + near[d]["good"].astype(jnp.int32)
    pl.semaphore_wait(barrier, count)

    def remote(src, dst, send, recv, device):
        return pltpu.make_async_remote_copy(
            src_ref=src, dst_ref=dst, send_sem=send, recv_sem=recv, device_id=device, device_id_type=MESH)

    def same_copy(d):
        return remote(hd.at[own_group(pos(z, coil_at(d)))], rb.at[:, :, 0, c], s_send.at[d], s_recv.at[d],
                      {"coil": coil_at(d)})

    def far_copy(d):
        return remote(hd.at[groups - 1 - own_group(pos(z, coil_at(d)))], rb.at[:, :, 1, c], v_send.at[d], v_recv.at[d],
                      {"kz": far, "coil": coil_at(d), "kx": 1 - h})

    def kernel_copy(d):
        return remote(kb.at[c], kb.at[c], k_send.at[d], k_recv.at[d], {"coil": coil_at(d)})

    mask_copy = remote(hm.at[groups - 1 - own_group(cc)], mb.at[1], m_send, m_recv,
                       {"kz": far, "kx": 1 - h})

    hd_rows = hd.reshape(groups * planes * 2 * coils, lanes)
    fr_rows = fr.reshape(groups * planes * 2 * coils, lanes)

    def pack(m):
        keep = jnp.concatenate([mask[m * g + i] for i in range(g)], 1) == 1
        hm[m] = jnp.where(keep, 1.0, 0.0)
        for ri in range(2):
            for coil in range(coils):
                value = jnp.concatenate([measured[ri, coil, m * g + i] for i in range(g)], 1)
                hd_rows[pl.ds(m * planes * 2 * coils + ri * coils + coil, planes, stride=2 * coils), :] = jnp.where(keep, value, 0.0)

    def pack_far(d, _):
        pack(groups - 1 - own_group(pos(z, coil_at(d))))
        far_copy(d).start()
        return 0

    lax.fori_loop(0, nc, pack_far, 0)
    mask_copy.start()
    kb[c] = jnp.concatenate([kernel[:, 0], kernel[:, 1]], 2)
    for d in range(1, nc):
        kernel_copy(d).start()

    def pack_same(d, _):
        pack(own_group(pos(z, coil_at(d))))

        @pl.when(d > 0)
        def _():
            same_copy(d).start()

        return 0

    lax.fori_loop(0, nc, pack_same, 0)
    mine = own_group(cc)
    rb[:, :, 0, c] = hd[mine]
    mb[0] = hm[mine]

    for step in range(ITERS):
        for sz in range(2):
            @pl.when(jnp.logical_not(near[(2 * sz - 1, 0)]["good"]))
            def _():
                hz[step, sz] = jnp.zeros(hz.shape[2:], F32)
            for sc in range(2):
                @pl.when(jnp.logical_not(near[(2 * sz - 1, 2 * sc - 1)]["good"]))
                def _():
                    hq[step, sz, sc] = jnp.zeros(hq.shape[3:], F32)
        @pl.when(jnp.logical_not(near[(0, -1)]["good"]))
        def _():
            hg[step, 0] = jnp.zeros(hg.shape[2:], F32)

    for d in range(1, nc):
        kernel_copy(d).wait_recv()
    lane = lax.broadcasted_iota(jnp.int32, (1, chans), 1)
    first = lax.rem(lax.div(lane, band), 2) == 0
    upper = lane >= 2 * band

    def swap(x):
        return jnp.where(first, pltpu.roll(x, chans - band, 1), pltpu.roll(x, band, 1))

    def sign(s):
        return jnp.where(upper, jnp.where(first, s, -s), 1.0)

    def weights(t, _):
        plain = kb[:, t].reshape(band, chans)
        turned = swap(kb[:, TAPS - 1 - t].reshape(band, chans))
        rows = (plain * sign(-1.0), turned * sign(1.0),
                pltpu.roll(plain, 2 * band, 1) * sign(1.0), pltpu.roll(turned, 2 * band, 1) * sign(-1.0))
        for n, value in enumerate(rows):
            hi, lo = split(value)
            w[t, n * band:(n + 1) * band, :] = jnp.concatenate([hi, hi], 1)
            w[t, chans + n * band:chans + (n + 1) * band, :] = jnp.concatenate([lo, jnp.zeros_like(lo)], 1)
        return 0

    lax.fori_loop(0, TAPS, weights, 0)

    turn = reversal(lanes)
    eye = (lax.broadcasted_iota(jnp.int32, (lanes, lanes), 0) == lax.broadcasted_iota(jnp.int32, (lanes, lanes), 1))
    both = jnp.concatenate([jnp.where(eye, 1.0, 0.0).astype(BF16), turn], 1)
    is_state = lax.rem(lax.div(lax.broadcasted_iota(jnp.int32, (chans, 1), 0), band), 2) == 0

    def put(step, x, k, r, n, m):
        rows = n * m * row
        j = lax.rem(lax.broadcasted_iota(jnp.int32, (rows, 1), 0), row)
        for b in range(3):
            y = x
            if b == 0:
                y = jnp.where(j > 0, pltpu.roll(x, 1, 0), 0.0)
            if b == 2:
                y = jnp.where(j < row - 1, pltpu.roll(x, rows - 1, 0), 0.0)
            hi, lo = split(y)
            xb[step, b, pl.ds(k, n), pl.ds(r, m)] = jnp.concatenate([hi, lo], 1).reshape(n, m, row, wide)

    for d in range(nc):
        if d:
            same_copy(d).wait_recv()
        far_copy(d).wait_recv()
    mask_copy.wait_recv()

    def transpose_in(k, _):
        kv = planes - 1 - k
        xs, xv = rb[k].reshape(chans, lanes), rb[kv].reshape(chans, lanes)
        cat = jnp.concatenate([jnp.where(is_state, xs, 0.0), jnp.where(is_state, 0.0, xv)], 1)
        hi, lo = split(cat)
        ms = jnp.broadcast_to(mb[0, pl.ds(k, 1)], (chans, lanes))
        mv = jnp.broadcast_to(mb[1, pl.ds(kv, 1)], (chans, lanes))
        mk = jnp.concatenate([jnp.where(is_state, ms, 0.0), jnp.where(is_state, 0.0, mv)], 1).astype(BF16)
        t = lax.dot_general(both, jnp.concatenate([hi, lo, mk], 0), NT, preferred_element_type=F32)
        x = t[:, :chans] + t[:, chans:2 * chans]
        mt[k] = t[:, 2 * chans:]
        st[0, k] = x.reshape(g, row, chans)
        put(0, x, k + 1, 1, 1, g)
        return 0

    lax.fori_loop(0, planes, transpose_in, 0)

    def edge(sc, inner):
        up = eq * sc + (1 - eq) * (1 - sc)
        return up * (g - 1) if inner else up * (g + 1)

    def halo_copy(step, d):
        v = near[d]
        n = dirs.index(d)
        plane = planes - 1 if d[0] > 0 else 0
        sem = 0
        if d[1] == 0:
            src, dst = st.at[step, plane], hz.at[step, v["tsz"]]
            sem = v["tsz"]
        elif d[0] == 0:
            src, dst = st.at[step, :, edge(v["sc"], True)], hg.at[step, v["tsc"]]
            sem = 2 + v["tsc"]
        else:
            src, dst = st.at[step, plane, edge(v["sc"], True)], hq.at[step, v["tsz"], v["tsc"]]
            sem = 4 + 2 * v["tsz"] + v["tsc"]
        return remote(src, dst, h_send.at[step, n], h_recv.at[step, sem], v["device"])

    def halo_land(step, d):
        v = near[d]
        if d[1] == 0:
            return hz.at[step, v["sz"]], v["sz"]
        if d[0] == 0:
            return hg.at[step, v["sc"]], 2 + v["sc"]
        return hq.at[step, v["sz"], v["sc"]], 4 + 2 * v["sz"] + v["sc"]

    order = [(0, 1), (0, -1), (1, 0), (-1, 0), (1, 1), (-1, 1), (1, -1), (-1, -1)]

    def start_halo(step):
        for d in order:
            @pl.when(near[d]["good"])
            def _():
                halo_copy(step, d).start()
        for d in maybe_alone:
            @pl.when(near[d]["alone"])
            def _():
                v = near[d]
                hq[step, v["sz"], v["sc"]] = st[step, planes - 1 if d[0] > 0 else 0, edge(v["sc"], True)]

    def flipped(x, rows):
        hi, lo = split(x)
        y = jnp.dot(reversal(rows), jnp.concatenate([hi, lo], 1), preferred_element_type=F32)
        return swap(y[:, :chans] + y[:, chans:])

    def take_halo(step):
        for d in order[2:4] + order[:2] + order[4:]:
            v = near[d]
            buf, sem = halo_land(step, d)

            @pl.when(v["good"])
            def _():
                remote(buf, buf, h_send.at[step, dirs.index(d)], h_recv.at[step, sem], v["device"]).wait_recv()

            n = planes if d[0] == 0 else 1
            m = g if d[1] == 0 else 1
            rows = n * m * row
            x = buf[...].reshape(rows, chans)
            x = jnp.where(v["flip"] == 1, flipped(x, rows), x)
            k = 1 if d[0] == 0 else (planes + 1 if d[0] > 0 else 0)
            r = 1 if d[1] == 0 else edge(v["sc"], False)
            put(step, x, k, r, n, m)

    def convolve(step, k):
        x = jnp.concatenate([xb[step, (t // 3) % 3, pl.ds(k + t % 3, CHUNK), pl.ds(t // 9, g)].reshape(CHUNK * lanes, wide)
                             for t in range(TAPS)], 1)
        p = lax.dot_general(x, jnp.concatenate([w[t] for t in range(TAPS)], 1), NT, preferred_element_type=F32)
        return p[:, :chans] + p[:, chans:]

    start_halo(0)
    take_halo(0)

    for step in range(ITERS - 1):
        def iterate(n, _):
            result = convolve(step, n * CHUNK)
            for i in range(CHUNK):
                k = n * CHUNK + i
                x = jnp.where(mt[k] > 0.5, st[0, k].reshape(lanes, chans), result[i * lanes:(i + 1) * lanes])
                st[step + 1, k] = x.reshape(g, row, chans)
                put(step + 1, x, k + 1, 1, 1, g)
            return 0

        lax.fori_loop(0, planes // CHUNK, iterate, 0)
        start_halo(step + 1)
        take_halo(step + 1)

    def same_back(d, n):
        k = pl.ds(n * CHUNK, CHUNK)
        return remote(ob.at[k, :, 0, coil_at(d)], fr.at[mine, k], os_send.at[d, n], os_recv.at[d, n],
                      {"coil": coil_at(d)})

    def far_back(d, n):
        k = pl.ds(planes - (n + 1) * CHUNK, CHUNK)
        return remote(ob.at[k, :, 1, coil_at(d)], fr.at[groups - 1 - mine, k], ov_send.at[d, n], ov_recv.at[d, n],
                      {"kz": far, "coil": coil_at(d), "kx": 1 - h})

    turn2 = jnp.concatenate([turn, turn], 1)

    def finish(n, _):
        result = convolve(ITERS - 1, n * CHUNK)
        for i in range(CHUNK):
            k = n * CHUNK + i
            r = result[i * lanes:(i + 1) * lanes]
            hi, lo = split(r)
            back = jnp.dot(turn2, jnp.concatenate([hi, lo], 0), preferred_element_type=F32)
            y = jnp.where(first, r, back).T.reshape(2, 2, nc, coils, lanes)
            ob[k, :, 0] = y[:, 0]
            ob[planes - 1 - k, :, 1] = y[:, 1]
        for d in range(nc):
            far_back(d, n).start()
        for d in range(1, nc):
            same_back(d, n).start()
        return 0

    lax.fori_loop(0, planes // CHUNK, finish, 0)
    fr[mine] = ob[:, :, 0, c]

    def unpack(m):
        keep = hm[m] > 0.5
        for ri in range(2):
            for coil in range(coils):
                at = pl.ds(m * planes * 2 * coils + ri * coils + coil, planes, stride=2 * coils)
                value = jnp.where(keep, hd_rows[at, :], fr_rows[at, :])
                for i in range(g):
                    out[ri, coil, m * g + i] = value[:, i * row:(i + 1) * row]

    def landed(send, recv, m, d, n):
        k = pl.ds(n * CHUNK, CHUNK)
        remote(ob.at[k, :, 0, 0], fr.at[m, k], send.at[d, n], recv.at[d, n], {"coil": coil_at(1)}).wait_recv()

    def same_home(d, _):
        m = own_group(pos(z, lax.rem(c + nc - d, nc)))

        @pl.when(d > 0)
        def _():
            for n in range(planes // CHUNK):
                landed(os_send, os_recv, m, d, n)

        unpack(m)
        return 0

    def far_home(d, _):
        m = groups - 1 - own_group(pos(z, lax.rem(c + nc - d, nc)))
        for n in range(planes // CHUNK):
            landed(ov_send, ov_recv, m, d, n)
        unpack(m)
        return 0

    lax.fori_loop(0, nc, same_home, 0)
    lax.fori_loop(0, nc, far_home, 0)

    for d in range(nc):
        far_copy(d).wait_send()
        if d:
            same_copy(d).wait_send()
            kernel_copy(d).wait_send()
        for n in range(planes // CHUNK):
            far_back(d, n).wait_send()
            if d:
                same_back(d, n).wait_send()
    mask_copy.wait_send()
    for step in range(ITERS):
        for d in dirs:
            @pl.when(near[d]["good"])
            def _():
                halo_copy(step, d).wait_send()


def on_device(sizes, measured, mask, kernel):
    nz, nc = sizes
    _, coils, depth_x, planes, row = measured.shape
    groups = 2 * nc
    g = depth_x // groups
    lanes = g * row
    chans = 4 * nc * coils
    parts = planes // CHUNK
    vmem = pl.BlockSpec(memory_space=pltpu.VMEM)
    dma = pltpu.SemaphoreType.DMA
    return pl.pallas_call(
        functools.partial(body, sizes),
        out_shape=jax.ShapeDtypeStruct(measured.shape, F32),
        in_specs=[vmem] * 3,
        out_specs=vmem,
        scratch_shapes=[
            pltpu.VMEM((groups, planes, 2, coils, lanes), F32),
            pltpu.VMEM((groups, planes, lanes), F32),
            pltpu.VMEM((planes, 2, 2, nc, coils, lanes), F32),
            pltpu.VMEM((2, planes, lanes), F32),
            pltpu.VMEM((nc, TAPS, coils, chans), F32),
            pltpu.VMEM((TAPS, 2 * chans, 2 * chans), BF16),
            pltpu.VMEM((ITERS, planes, g, row, chans), F32),
            pltpu.VMEM((planes, lanes, chans), F32),
            pltpu.VMEM((ITERS, 3, planes + 2, g + 2, row, 2 * chans), BF16),
            pltpu.VMEM((ITERS, 2, g, row, chans), F32),
            pltpu.VMEM((ITERS, 2, planes, row, chans), F32),
            pltpu.VMEM((ITERS, 2, 2, row, chans), F32),
            pltpu.VMEM((planes, 2, 2, nc, coils, lanes), F32),
            pltpu.VMEM((groups, planes, 2, coils, lanes), F32),
            dma((nc,)), dma((nc,)), dma((nc,)), dma((nc,)), dma((nc,)), dma((nc,)), dma, dma,
            dma((ITERS, 8)), dma((ITERS, 8)),
            dma((nc, parts)), dma((nc, parts)), dma((nc, parts)), dma((nc, parts)),
        ],
        compiler_params=pltpu.CompilerParams(collective_id=0, has_side_effects=True, vmem_limit_bytes=56 << 20),
    )(measured, mask, kernel)


def solution(mesh):
    placed = (
        P(None, ("grp", "coil"), "kx", "kz", None),
        P(("grp", "kx"), "kz", None),
        P(None, None, "coil", None),
    )
    return jax.shard_map(
        functools.partial(on_device, (mesh.shape["kz"], mesh.shape["coil"])),
        mesh=mesh,
        in_specs=placed,
        out_specs=P(None, ("grp", "coil"), "kx", "kz", None),
        check_vma=False,
    )
```

```python
import functools

import jax
import jax.numpy as jnp
from jax import lax
from jax.experimental import pallas as pl
from jax.experimental.pallas import tpu as pltpu
from jax.sharding import PartitionSpec as P

ITERS = 2
TAPS = 27
CHUNK = 2
MESH = pl.DeviceIdType.MESH
F32, BF16 = jnp.float32, jnp.bfloat16
NT = (((1,), (1,)), ((), ()))


def split(x):
    hi = x.astype(BF16)
    return hi, (x - hi.astype(F32)).astype(BF16)


def reversal(n):
    i = lax.broadcasted_iota(jnp.int32, (n, n), 0) + lax.broadcasted_iota(jnp.int32, (n, n), 1)
    return jnp.where(i == n - 1, 1.0, 0.0).astype(BF16)


def body(sizes, measured_hbm, mask_hbm, kernel_hbm, out, measured, mask, kernel, hd, hm, rb, mb, kb, w, st, mt, xb, hz, hg, hq, acc, ob, fr,
         in_sem, s_send, s_recv, v_send, v_recv, k_send, k_recv, f_send, f_recv, m_send, m_recv,
         hz_send, hz_recv, hg_send, hg_recv, hq_send, hq_recv, os_send, os_recv, ov_send, ov_recv):
    nz, nc = sizes
    _, coils, depth_x, planes, row = measured.shape
    half = nz // 2
    groups = 2 * nc
    g = depth_x // groups
    lanes = g * row
    band = nc * coils
    chans = 4 * band
    wide = 2 * chans
    parts = planes // CHUNK

    z, c, h = lax.axis_index("kz"), lax.axis_index("coil"), lax.axis_index("kx")
    side = lax.div(z, half)
    far = nz - 1 - z

    def owner(tz, thalf, place):
        q = lax.rem(thalf + lax.div(tz, half), 2)
        return {"kz": tz, "coil": q * (nc // 2) + lax.div(place, 2), "kx": lax.rem(place, 2)}

    kxh = lax.rem(lax.div(c, nc // 2) + side, 2)
    cc = lax.rem(c, nc // 2) * 2 + h
    stays = kxh == h

    def group_of(khalf, place):
        even = lax.rem(side + khalf + 1, 2)
        return even * place + (1 - even) * (groups - 1 - place)

    eq = lax.rem(side + kxh + 1, 2)
    mine = group_of(kxh, cc)

    def neighbour(dz, dc):
        zt = z + dz
        good = (zt >= 0) & (zt < nz)
        zt = lax.max(lax.min(zt, nz - 1), 0)
        over = lax.rem(lax.div(zt, half) + side, 2)
        inter = lax.div(cc + 1, nc) if dc > 0 else 0
        core = 1 - lax.min(cc, 1) if dc < 0 else 0
        if dc < 0:
            good = good & ((side == 1) | (cc > 0))
        flip = lax.rem(over + inter, 2)
        tz = flip * (nz - 1 - zt) + (1 - flip) * zt
        sz, sc = (dz + 1) // 2, (dc + 1) // 2
        stay = inter + core
        alone = (over * core == 1) & good
        return dict(good=good & jnp.logical_not(alone), alone=alone, flip=flip,
                    device=owner(tz, lax.rem(kxh + flip + core, 2), cc + dc - inter + core), sz=sz, sc=sc,
                    tsz=flip * sz + (1 - flip) * (1 - sz), tsc=stay * sc + (1 - stay) * (1 - sc))

    dirs = [(dz, dc) for dz in (-1, 0, 1) for dc in (-1, 0, 1) if dz or dc]
    near = {d: neighbour(*d) for d in dirs}

    def load(m):
        at = pl.ds(m * g, g)
        return pltpu.make_async_copy(measured_hbm.at[:, :, at], measured.at[:, :, at], in_sem.at[m])

    load_kernel = pltpu.make_async_copy(kernel_hbm, kernel, in_sem.at[groups])
    load_mask = pltpu.make_async_copy(mask_hbm, mask, in_sem.at[groups + 1])

    def step_group(i):
        m = group_of(h, lax.rem(i, nc))
        return jnp.where(i < nc, groups - 1 - m, m)

    load_mask.start()
    load_kernel.start()
    for i in range(groups):
        load(step_group(i)).start()

    def home_same(cx):
        return {"kz": z, "coil": cx, "kx": kxh}

    def home_far(cx):
        return {"kz": far, "coil": cx, "kx": 1 - kxh}

    def is_self(place):
        return stays & (cc == place)

    barrier = pltpu.get_barrier_semaphore()

    def greet(device):
        pl.semaphore_signal(barrier, inc=1, device_id=device, device_id_type=MESH)

    for i in range(nc):
        greet(owner(far, 1 - h, i))
        greet(home_far(i))

        @pl.when(jnp.logical_not(is_self(i)))
        def _():
            greet(owner(z, h, i))

        @pl.when(jnp.logical_not(stays & (c == i)))
        def _():
            greet(home_same(i))

    for d in range(1, nc):
        greet({"coil": lax.rem(c + d, nc)})
    greet({"kx": 1 - h})
    count = 2 * nc + 2 * (nc - stays.astype(jnp.int32)) + nc
    for d in dirs:
        @pl.when(near[d]["good"])
        def _():
            greet(near[d]["device"])
        count = count + near[d]["good"].astype(jnp.int32)

    def remote(src, dst, send, recv, device):
        return pltpu.make_async_remote_copy(
            src_ref=src, dst_ref=dst, send_sem=send, recv_sem=recv, device_id=device, device_id_type=MESH)

    def same_copy(i, n):
        k = pl.ds(n * CHUNK, CHUNK)
        return remote(hd.at[group_of(h, i), k], rb.at[k, :, 0, c], s_send.at[i, n], s_recv.at[c, n], owner(z, h, i))

    def same_land(cx, n):
        k = pl.ds(n * CHUNK, CHUNK)
        return remote(rb.at[k, :, 0, cx], rb.at[k, :, 0, cx], s_send.at[cx, n], s_recv.at[cx, n], home_same(cx))

    def far_copy(i, n):
        k = pl.ds(planes - (n + 1) * CHUNK, CHUNK)
        return remote(hd.at[groups - 1 - group_of(h, i), k], rb.at[k, :, 1, c], v_send.at[i, n], v_recv.at[c, n], owner(far, 1 - h, i))

    def far_land(cx, n):
        k = pl.ds(planes - (n + 1) * CHUNK, CHUNK)
        return remote(rb.at[k, :, 1, cx], rb.at[k, :, 1, cx], v_send.at[cx, n], v_recv.at[cx, n], home_far(cx))

    def kernel_copy(d):
        return remote(kb.at[c, h], kb.at[c, h], k_send.at[d], k_recv.at[d], {"coil": lax.rem(c + d, nc)})

    def kernel_land(d):
        cx = lax.rem(c + nc - d, nc)
        return remote(kb.at[cx, h], kb.at[cx, h], k_send.at[d], k_recv.at[d], {"coil": cx})

    def kernel_pass(d):
        cx = lax.rem(c + nc - d, nc)
        return remote(kb.at[cx, h], kb.at[cx, h], f_send.at[d], f_recv.at[d], {"kx": 1 - h})

    def kernel_last(d):
        cx = lax.rem(c + nc - d, nc)
        return remote(kb.at[cx, 1 - h], kb.at[cx, 1 - h], f_send.at[d], f_recv.at[d], {"kx": 1 - h})

    mask_self = is_self(c)
    mask_same = remote(hm.at[group_of(h, c)], mb.at[0], m_send.at[0], m_recv.at[0], owner(z, h, c))
    mask_far = remote(hm.at[groups - 1 - group_of(h, c)], mb.at[1], m_send.at[1], m_recv.at[1], owner(far, 1 - h, c))
    mask_same_land = remote(mb.at[0], mb.at[0], m_send.at[0], m_recv.at[0], home_same(cc))
    mask_far_land = remote(mb.at[1], mb.at[1], m_send.at[1], m_recv.at[1], home_far(cc))

    hd_rows = hd.reshape(groups * planes * 2 * coils, lanes)
    fr_rows = fr.reshape(groups * planes * 2 * coils, lanes)

    def pack(m):
        keep = jnp.concatenate([mask[m * g + i] for i in range(g)], 1) == 1
        hm[m] = jnp.where(keep, 1.0, 0.0)

        def one(coil, _):
            for ri in range(2):
                value = jnp.concatenate([measured[ri, coil, m * g + i] for i in range(g)], 1)
                hd_rows[pl.ds(m * planes * 2 * coils + ri * coils + coil, planes, stride=2 * coils), :] = jnp.where(keep, value, 0.0)
            return 0

        lax.fori_loop(0, coils, one, 0, unroll=4)

    load_kernel.wait()

    def fill(t, _):
        both = jnp.concatenate([kernel[t, 0], kernel[t, 1]], 1)
        for i in range(2):
            kb[c, i, t] = both[i * (coils // 2):(i + 1) * (coils // 2)]
        return 0

    lax.fori_loop(0, TAPS, fill, 0)
    load_mask.wait()

    def pack_all(i, _):
        m = step_group(i)
        load(m).wait()
        pack(m)

        @pl.when(i == nc - 1)
        def _():
            pl.semaphore_wait(barrier, count)
            for d in range(1, nc):
                kernel_copy(d).start()
            mask_far.start()

            def launch(i, _):
                far_copy(lax.rem(i, nc), lax.div(i, nc)).start()
                return 0

            lax.fori_loop(0, parts * nc, launch, 0)

        @pl.when((i >= nc) & jnp.logical_not(is_self(i - nc)))
        def _():
            def launch(n, _):
                same_copy(i - nc, n).start()
                return 0

            lax.fori_loop(0, parts, launch, 0)

        return 0

    lax.fori_loop(0, groups, pack_all, 0)

    @pl.when(jnp.logical_not(mask_self))
    def _():
        mask_same.start()

    @pl.when(mask_self)
    def _():
        mb[0] = hm[mine]

    @pl.when(stays)
    def _():
        rb[:, :, 0, c] = hd[mine]

    for step in range(ITERS):
        for b in range(3):
            for k in (0, planes + 1):
                xb[step, b, k] = jnp.zeros(xb.shape[3:], BF16)
            for r in (0, g + 1):
                xb[step, b, :, r] = jnp.zeros((planes + 2, row, wide), BF16)

    for step in range(ITERS):
        for sz in range(2):
            @pl.when(jnp.logical_not(near[(2 * sz - 1, 0)]["good"]))
            def _():
                hz[step, sz] = jnp.zeros(hz.shape[2:], F32)
            for sc in range(2):
                @pl.when(jnp.logical_not(near[(2 * sz - 1, 2 * sc - 1)]["good"]))
                def _():
                    hq[step, sz, sc] = jnp.zeros(hq.shape[3:], F32)
        @pl.when(jnp.logical_not(near[(0, -1)]["good"]))
        def _():
            hg[step, 0] = jnp.zeros(hg.shape[2:], F32)

    for d in range(1, nc):
        kernel_land(d).wait_recv()
        kernel_pass(d).start()
    for d in range(1, nc):
        kernel_last(d).wait_recv()
    lane = lax.broadcasted_iota(jnp.int32, (1, chans), 1)
    first = lax.rem(lax.div(lane, band), 2) == 0
    upper = lane >= 2 * band

    def swap(x):
        return jnp.where(first, pltpu.roll(x, chans - band, 1), pltpu.roll(x, band, 1))

    def sign(s):
        return jnp.where(upper, jnp.where(first, s, -s), 1.0)

    def taken(t):
        return jnp.concatenate([kb[i, j, t] for i in range(nc) for j in range(2)], 0)

    def weights(t, _):
        plain = taken(t)
        turned = swap(taken(TAPS - 1 - t))
        rows = (plain * sign(-1.0), turned * sign(1.0),
                pltpu.roll(plain, 2 * band, 1) * sign(1.0), pltpu.roll(turned, 2 * band, 1) * sign(-1.0))
        for n, value in enumerate(rows):
            hi, lo = split(value)
            w[t, n * band:(n + 1) * band, :] = jnp.concatenate([hi, hi], 1)
            w[t, chans + n * band:chans + (n + 1) * band, :] = jnp.concatenate([lo, jnp.zeros_like(lo)], 1)
        return 0

    lax.fori_loop(0, TAPS, weights, 0)

    turn = reversal(lanes)
    eye = (lax.broadcasted_iota(jnp.int32, (lanes, lanes), 0) == lax.broadcasted_iota(jnp.int32, (lanes, lanes), 1))
    both = jnp.concatenate([jnp.where(eye, 1.0, 0.0).astype(BF16), turn], 1)
    def put(step, x, k, r, n, m):
        rows = n * m * row
        j = lax.rem(lax.broadcasted_iota(jnp.int32, (rows, 1), 0), row)
        for b in range(3):
            y = x
            if b == 0:
                y = jnp.where(j > 0, pltpu.roll(x, 1, 0), 0.0)
            if b == 2:
                y = jnp.where(j < row - 1, pltpu.roll(x, rows - 1, 0), 0.0)
            hi, lo = split(y)
            xb[step, b, pl.ds(k, n), pl.ds(r, m)] = jnp.concatenate([hi, lo], 1).reshape(n, m, row, wide)

    def transpose_in(k):
        kv = planes - 1 - k
        xs, xv = rb[k, :, 0].reshape(2, band, lanes), rb[kv, :, 1].reshape(2, band, lanes)
        none = jnp.zeros((band, lanes), F32)
        ms = jnp.broadcast_to(mb[0, pl.ds(k, 1)], (band, lanes))
        mv = jnp.broadcast_to(mb[1, pl.ds(kv, 1)], (band, lanes))

        def beside(s0, v0, s1, v1):
            return jnp.concatenate([jnp.concatenate(pair, 1) for pair in ((s0, none), (none, v0), (s1, none), (none, v1))], 0)

        hi, lo = split(beside(xs[0], xv[0], xs[1], xv[1]))
        mk = beside(ms, mv, ms, mv).astype(BF16)
        t = lax.dot_general(both, jnp.concatenate([hi, lo, mk], 0), NT, preferred_element_type=F32)
        x = t[:, :chans] + t[:, chans:2 * chans]
        mt[k] = t[:, 2 * chans:]
        st[0, k] = x.reshape(g, row, chans)
        put(0, x, k + 1, 1, 1, g)

    def edge(sc, inner):
        up = eq * sc + (1 - eq) * (1 - sc)
        return up * (g - 1) if inner else up * (g + 1)

    def plane_copy(step, dz):
        v = near[(dz, 0)]
        return remote(st.at[step, planes - 1 if dz > 0 else 0], hz.at[step, v["tsz"]],
                      hz_send.at[step, v["sz"]], hz_recv.at[step, v["tsz"]], v["device"])

    def row_copy(step, dc, n):
        v = near[(0, dc)]
        k = pl.ds(n * CHUNK, CHUNK)
        return remote(st.at[step, k, edge(v["sc"], True)], hg.at[step, v["tsc"], k],
                      hg_send.at[step, v["sc"], n], hg_recv.at[step, v["tsc"], n], v["device"])

    def corner_copy(step, dz, dc):
        v = near[(dz, dc)]
        return remote(st.at[step, planes - 1 if dz > 0 else 0, edge(v["sc"], True)], hq.at[step, v["tsz"], v["tsc"]],
                      hq_send.at[step, v["sz"], v["sc"]], hq_recv.at[step, v["tsz"], v["tsc"]], v["device"])

    def start_halo(step, n):
        for dc in (1, -1):
            @pl.when(near[(0, dc)]["good"])
            def _():
                row_copy(step, dc, n).start()
        for dz in (-1, 1):
            @pl.when(n == (parts - 1 if dz > 0 else 0))
            def _():
                @pl.when(near[(dz, 0)]["good"])
                def _():
                    plane_copy(step, dz).start()
                for dc in (1, -1):
                    @pl.when(near[(dz, dc)]["good"])
                    def _():
                        corner_copy(step, dz, dc).start()
                v = near[(dz, -1)]

                @pl.when(v["alone"])
                def _():
                    hq[step, v["sz"], v["sc"]] = st[step, planes - 1 if dz > 0 else 0, edge(v["sc"], True)]

    def flipped(x, rows):
        hi, lo = split(x)
        y = jnp.dot(reversal(rows), jnp.concatenate([hi, lo], 1), preferred_element_type=F32)
        return swap(y[:, :chans] + y[:, chans:])

    def place_halo(step, d, buf, n, m):
        rows = n * m * row
        x = buf[...].reshape(rows, chans)
        x = jnp.where(near[d]["flip"] == 1, flipped(x, rows), x)
        k = 1 if d[0] == 0 else (planes + 1 if d[0] > 0 else 0)
        r = 1 if d[1] == 0 else edge(near[d]["sc"], False)
        put(step, x, k, r, n, m)

    def product(xs, ws):
        p = lax.dot_general(jnp.concatenate(xs, 1), jnp.concatenate(ws, 1), NT, preferred_element_type=F32)
        return p[:, :chans] + p[:, chans:]

    def inner(step, n):
        p = product([xb[step, (t // 3) % 3, pl.ds(n * CHUNK + t % 3, CHUNK), pl.ds(t // 9, g)].reshape(CHUNK * lanes, wide)
                     for t in range(TAPS)], [w[t] for t in range(TAPS)])
        acc[pl.ds(n * CHUNK, CHUNK)] = p.reshape(CHUNK, g, row, chans)

    def outer(step):
        for dz in (-1, 1):
            v = near[(dz, 0)]
            buf = hz.at[step, v["sz"]]

            @pl.when(v["good"])
            def _():
                remote(buf, buf, hz_send.at[step, v["sz"]], hz_recv.at[step, v["sz"]], v["device"]).wait_recv()

            place_halo(step, (dz, 0), buf, 1, g)
            at, e = (planes - 1, 2) if dz > 0 else (0, 0)
            taps = [9 * a + 3 * b + e for a in range(3) for b in range(3)]
            p = product([xb[step, (t // 3) % 3, at + e, t // 9:t // 9 + g].reshape(lanes, wide) for t in taps],
                        [w[t] for t in taps])
            acc[at] += p.reshape(g, row, chans)
        for dc in (-1, 1):
            v = near[(0, dc)]
            buf = hg.at[step, v["sc"]]

            @pl.when(v["good"])
            def _():
                for n in range(parts):
                    part = buf.at[pl.ds(n * CHUNK, CHUNK)]
                    remote(part, part, hg_send.at[step, v["sc"], n], hg_recv.at[step, v["sc"], n], v["device"]).wait_recv()

            place_halo(step, (0, dc), buf, planes, 1)
            for dz in (-1, 1):
                u = near[(dz, dc)]
                corner = hq.at[step, u["sz"], u["sc"]]

                @pl.when(u["good"])
                def _():
                    remote(corner, corner, hq_send.at[step, u["sz"], u["sc"]], hq_recv.at[step, u["sz"], u["sc"]],
                           u["device"]).wait_recv()

                place_halo(step, (dz, dc), corner, 1, 1)
        for r, a in ((0, 0), (g - 1, 2)):
            taps = [9 * a + t for t in range(9)]
            p = product([xb[step, (t // 3) % 3, t % 3:t % 3 + planes, r + a].reshape(planes * row, wide) for t in taps],
                        [w[t] for t in taps])
            acc[:, r] += p.reshape(planes, row, chans)

    mask_far_land.wait_recv()

    @pl.when(jnp.logical_not(stays & (c == cc)))
    def _():
        mask_same_land.wait_recv()

    def update(step, k):
        x = jnp.where(mt[k] > 0.5, st[0, k].reshape(lanes, chans), acc[k].reshape(lanes, chans))
        st[step, k] = x.reshape(g, row, chans)
        put(step, x, k + 1, 1, 1, g)

    def stage(step, _):
        def chunk(n, _):
            @pl.when((step == 0) & (n < parts))
            def _():
                for cx in range(nc):
                    @pl.when(jnp.logical_not(stays & (c == cx)))
                    def _():
                        same_land(cx, n).wait_recv()

                    far_land(cx, n).wait_recv()
                for i in range(CHUNK):
                    transpose_in(n * CHUNK + i)
                start_halo(step, n)

            @pl.when((step > 0) & (n == 0))
            def _():
                def renew(m, _):
                    for i in range(CHUNK):
                        update(step, m * CHUNK + i)
                    start_halo(step, m)
                    return 0

                lax.fori_loop(0, parts, renew, 0)

            @pl.when(n > 0)
            def _():
                inner(step, n - 1)

            return 0

        lax.fori_loop(0, parts + 1, chunk, 0)
        outer(step)
        return 0

    lax.fori_loop(0, ITERS, stage, 0)

    def same_back(cx, n):
        k = pl.ds(n * CHUNK, CHUNK)
        return remote(ob.at[k, :, 0, cx], fr.at[mine, k], os_send.at[cx, n], os_recv.at[cc, n], home_same(cx))

    def far_back(cx, n):
        k = pl.ds(planes - (n + 1) * CHUNK, CHUNK)
        return remote(ob.at[k, :, 1, cx], fr.at[groups - 1 - mine, k], ov_send.at[cx, n], ov_recv.at[cc, n], home_far(cx))

    turn2 = jnp.concatenate([turn, turn], 1)

    def finish(n, _):
        for i in range(CHUNK):
            k = n * CHUNK + i
            r = acc[k].reshape(lanes, chans)
            hi, lo = split(r)
            back = jnp.dot(turn2, jnp.concatenate([hi, lo], 0), preferred_element_type=F32)
            y = jnp.where(first, r, back).T.reshape(2, 2, nc, coils, lanes)
            ob[k, :, 0] = y[:, 0]
            ob[planes - 1 - k, :, 1] = y[:, 1]
        for cx in range(nc):
            far_back(cx, n).start()
        for cx in range(nc):
            @pl.when(jnp.logical_not(stays & (c == cx)))
            def _():
                same_back(cx, n).start()

        return 0

    lax.fori_loop(0, parts, finish, 0)

    @pl.when(stays)
    def _():
        fr[mine] = ob[:, :, 0, c]

    def unpack(m):
        keep = hm[m] > 0.5

        def one(coil, _):
            for ri in range(2):
                at = pl.ds(m * planes * 2 * coils + ri * coils + coil, planes, stride=2 * coils)
                value = jnp.where(keep, hd_rows[at, :], fr_rows[at, :])
                for i in range(g):
                    out[ri, coil, m * g + i] = value[:, i * row:(i + 1) * row]
            return 0

        lax.fori_loop(0, coils, one, 0, unroll=4)

    def home(i, _):
        place = lax.rem(i, nc)
        m = group_of(h, place)

        def same_home(n, _):
            k = pl.ds(n * CHUNK, CHUNK)
            remote(fr.at[m, k], fr.at[m, k], os_send.at[place, n], os_recv.at[place, n], owner(z, h, place)).wait_recv()
            return 0

        def far_home(n, _):
            k = pl.ds(planes - (n + 1) * CHUNK, CHUNK)
            there = fr.at[groups - 1 - m, k]
            remote(there, there, ov_send.at[place, n], ov_recv.at[place, n], owner(far, 1 - h, place)).wait_recv()
            return 0

        @pl.when((i < nc) & jnp.logical_not(is_self(place)))
        def _():
            lax.fori_loop(0, parts, same_home, 0)

        @pl.when(i >= nc)
        def _():
            lax.fori_loop(0, parts, far_home, 0)

        unpack(jnp.where(i < nc, m, groups - 1 - m))
        return 0

    lax.fori_loop(0, groups, home, 0)

    def sent(n, _):
        for i in range(nc):
            far_copy(i, n).wait_send()
            far_back(i, n).wait_send()

            @pl.when(jnp.logical_not(is_self(i)))
            def _():
                same_copy(i, n).wait_send()

            @pl.when(jnp.logical_not(stays & (c == i)))
            def _():
                same_back(i, n).wait_send()

        return 0

    lax.fori_loop(0, parts, sent, 0)
    for d in range(1, nc):
        kernel_copy(d).wait_send()
        kernel_pass(d).wait_send()
    mask_far.wait_send()

    @pl.when(jnp.logical_not(mask_self))
    def _():
        mask_same.wait_send()

    def passed(step, _):
        for d in dirs:
            @pl.when(near[d]["good"])
            def _():
                if d[1] == 0:
                    plane_copy(step, d[0]).wait_send()
                elif d[0] == 0:
                    for n in range(parts):
                        row_copy(step, d[1], n).wait_send()
                else:
                    corner_copy(step, *d).wait_send()

        return 0

    lax.fori_loop(0, ITERS, passed, 0)


def on_device(sizes, measured, mask, kernel):
    nz, nc = sizes
    _, coils, depth_x, planes, row = measured.shape
    groups = 2 * nc
    g = depth_x // groups
    lanes = g * row
    chans = 4 * nc * coils
    parts = planes // CHUNK
    vmem = pl.BlockSpec(memory_space=pltpu.VMEM)
    dma = pltpu.SemaphoreType.DMA
    return pl.pallas_call(
        functools.partial(body, sizes),
        out_shape=jax.ShapeDtypeStruct(measured.shape, F32),
        in_specs=[pl.BlockSpec(memory_space=pl.ANY)] * 3,
        out_specs=vmem,
        scratch_shapes=[
            pltpu.VMEM(measured.shape, F32),
            pltpu.VMEM(mask.shape, jnp.int32),
            pltpu.VMEM(kernel.shape, F32),
            pltpu.VMEM((groups, planes, 2, coils, lanes), F32),
            pltpu.VMEM((groups, planes, lanes), F32),
            pltpu.VMEM((planes, 2, 2, nc, coils, lanes), F32),
            pltpu.VMEM((2, planes, lanes), F32),
            pltpu.VMEM((nc, 2, TAPS, coils // 2, chans), F32),
            pltpu.VMEM((TAPS, 2 * chans, 2 * chans), BF16),
            pltpu.VMEM((ITERS, planes, g, row, chans), F32),
            pltpu.VMEM((planes, lanes, chans), F32),
            pltpu.VMEM((ITERS, 3, planes + 2, g + 2, row, 2 * chans), BF16),
            pltpu.VMEM((ITERS, 2, g, row, chans), F32),
            pltpu.VMEM((ITERS, 2, planes, row, chans), F32),
            pltpu.VMEM((ITERS, 2, 2, row, chans), F32),
            pltpu.VMEM((planes, g, row, chans), F32),
            pltpu.VMEM((planes, 2, 2, nc, coils, lanes), F32),
            pltpu.VMEM((groups, planes, 2, coils, lanes), F32),
            dma((groups + 2,)),
            dma((nc, parts)), dma((nc, parts)), dma((nc, parts)), dma((nc, parts)),
            dma((nc,)), dma((nc,)), dma((nc,)), dma((nc,)), dma((2,)), dma((2,)),
            dma((ITERS, 2)), dma((ITERS, 2)), dma((ITERS, 2, parts)), dma((ITERS, 2, parts)),
            dma((ITERS, 2, 2)), dma((ITERS, 2, 2)),
            dma((nc, parts)), dma((nc, parts)), dma((nc, parts)), dma((nc, parts)),
        ],
        compiler_params=pltpu.CompilerParams(collective_id=0, has_side_effects=True, vmem_limit_bytes=56 << 20),
    )(measured, mask, kernel)


def solution(mesh):
    placed = (
        P(None, ("grp", "coil"), "kx", "kz", None),
        P(("grp", "kx"), "kz", None),
        P(None, None, "coil", None),
    )
    return jax.shard_map(
        functools.partial(on_device, (mesh.shape["kz"], mesh.shape["coil"])),
        mesh=mesh,
        in_specs=placed,
        out_specs=P(None, ("grp", "coil"), "kx", "kz", None),
        check_vma=False,
    )
```

```python
import functools

import jax
import jax.numpy as jnp
from jax import lax
from jax.experimental import pallas as pl
from jax.experimental.pallas import tpu as pltpu
from jax.sharding import PartitionSpec as P

ITERS = 2
TAPS = 27
CHUNK = 2
VLIM = 40
MESH = pl.DeviceIdType.MESH
F32, BF16 = jnp.float32, jnp.bfloat16
NT = (((1,), (1,)), ((), ()))


def split(x):
    hi = x.astype(BF16)
    return hi, (x - hi.astype(F32)).astype(BF16)


def reversal(n):
    i = lax.broadcasted_iota(jnp.int32, (n, n), 0) + lax.broadcasted_iota(jnp.int32, (n, n), 1)
    return jnp.where(i == n - 1, 1.0, 0.0).astype(BF16)


def body(sizes, measured_hbm, mask_hbm, kernel_hbm, out, measured, mask, kernel, hd, hm, rb, mb, kb, w, st, mt, xb, hz, hg, hq, acc, ob, fr,
         in_sem, s_send, s_recv, v_send, v_recv, k_send, k_recv, f_send, f_recv, m_send, m_recv,
         hz_send, hz_recv, hg_send, hg_recv, hq_send, hq_recv, os_send, os_recv, ov_send, ov_recv):
    nz, nc = sizes
    _, coils, depth_x, planes, row = measured.shape
    half = nz // 2
    groups = 2 * nc
    g = depth_x // groups
    lanes = g * row
    band = nc * coils
    chans = 4 * band
    wide = 2 * chans
    parts = planes // CHUNK

    z, c, h = lax.axis_index("kz"), lax.axis_index("coil"), lax.axis_index("kx")
    side = lax.div(z, half)
    far = nz - 1 - z

    def owner(tz, thalf, place):
        q = lax.rem(thalf + lax.div(tz, half), 2)
        return {"kz": tz, "coil": q * (nc // 2) + lax.div(place, 2), "kx": lax.rem(place, 2)}

    kxh = lax.rem(lax.div(c, nc // 2) + side, 2)
    cc = lax.rem(c, nc // 2) * 2 + h
    stays = kxh == h

    def group_of(khalf, place):
        even = lax.rem(side + khalf + 1, 2)
        return even * place + (1 - even) * (groups - 1 - place)

    eq = lax.rem(side + kxh + 1, 2)
    mine = group_of(kxh, cc)

    def neighbour(dz, dc):
        zt = z + dz
        good = (zt >= 0) & (zt < nz)
        zt = lax.max(lax.min(zt, nz - 1), 0)
        over = lax.rem(lax.div(zt, half) + side, 2)
        inter = lax.div(cc + 1, nc) if dc > 0 else 0
        core = 1 - lax.min(cc, 1) if dc < 0 else 0
        if dc < 0:
            good = good & ((side == 1) | (cc > 0))
        flip = lax.rem(over + inter, 2)
        tz = flip * (nz - 1 - zt) + (1 - flip) * zt
        sz, sc = (dz + 1) // 2, (dc + 1) // 2
        stay = inter + core
        alone = (over * core == 1) & good
        return dict(good=good & jnp.logical_not(alone), alone=alone, flip=flip,
                    device=owner(tz, lax.rem(kxh + flip + core, 2), cc + dc - inter + core), sz=sz, sc=sc,
                    tsz=flip * sz + (1 - flip) * (1 - sz), tsc=stay * sc + (1 - stay) * (1 - sc))

    dirs = [(dz, dc) for dz in (-1, 0, 1) for dc in (-1, 0, 1) if dz or dc]
    near = {d: neighbour(*d) for d in dirs}

    def load(m):
        at = pl.ds(m * g, g)
        return pltpu.make_async_copy(measured_hbm.at[:, :, at], measured.at[:, :, at], in_sem.at[m])

    load_kernel = pltpu.make_async_copy(kernel_hbm, kernel, in_sem.at[groups])
    load_mask = pltpu.make_async_copy(mask_hbm, mask, in_sem.at[groups + 1])

    def step_group(i):
        m = group_of(h, lax.rem(i, nc))
        return jnp.where(i < nc, groups - 1 - m, m)

    load_mask.start()
    load_kernel.start()
    for i in range(groups):
        load(step_group(i)).start()

    def home_same(cx):
        return {"kz": z, "coil": cx, "kx": kxh}

    def home_far(cx):
        return {"kz": far, "coil": cx, "kx": 1 - kxh}

    def is_self(place):
        return stays & (cc == place)

    barrier = pltpu.get_barrier_semaphore()

    def greet(device):
        pl.semaphore_signal(barrier, inc=1, device_id=device, device_id_type=MESH)

    for i in range(nc):
        greet(owner(far, 1 - h, i))
        greet(home_far(i))

        @pl.when(jnp.logical_not(is_self(i)))
        def _():
            greet(owner(z, h, i))

        @pl.when(jnp.logical_not(stays & (c == i)))
        def _():
            greet(home_same(i))

    for d in range(1, nc):
        greet({"coil": lax.rem(c + d, nc)})
    greet({"kx": 1 - h})
    count = 2 * nc + 2 * (nc - stays.astype(jnp.int32)) + nc
    for d in dirs:
        @pl.when(near[d]["good"])
        def _():
            greet(near[d]["device"])
        count = count + near[d]["good"].astype(jnp.int32)

    def remote(src, dst, send, recv, device):
        return pltpu.make_async_remote_copy(
            src_ref=src, dst_ref=dst, send_sem=send, recv_sem=recv, device_id=device, device_id_type=MESH)

    def same_copy(i, n):
        k = pl.ds(n * CHUNK, CHUNK)
        return remote(hd.at[group_of(h, i), k], rb.at[k, :, 0, c], s_send.at[i, n], s_recv.at[c, n], owner(z, h, i))

    def same_land(cx, n):
        k = pl.ds(n * CHUNK, CHUNK)
        return remote(rb.at[k, :, 0, cx], rb.at[k, :, 0, cx], s_send.at[cx, n], s_recv.at[cx, n], home_same(cx))

    def far_copy(i, n):
        k = pl.ds(planes - (n + 1) * CHUNK, CHUNK)
        return remote(hd.at[groups - 1 - group_of(h, i), k], rb.at[k, :, 1, c], v_send.at[i, n], v_recv.at[c, n], owner(far, 1 - h, i))

    def far_land(cx, n):
        k = pl.ds(planes - (n + 1) * CHUNK, CHUNK)
        return remote(rb.at[k, :, 1, cx], rb.at[k, :, 1, cx], v_send.at[cx, n], v_recv.at[cx, n], home_far(cx))

    def kernel_copy(d):
        return remote(kb.at[c, h], kb.at[c, h], k_send.at[d], k_recv.at[d], {"coil": lax.rem(c + d, nc)})

    def kernel_land(d):
        cx = lax.rem(c + nc - d, nc)
        return remote(kb.at[cx, h], kb.at[cx, h], k_send.at[d], k_recv.at[d], {"coil": cx})

    def kernel_pass(d):
        cx = lax.rem(c + nc - d, nc)
        return remote(kb.at[cx, h], kb.at[cx, h], f_send.at[d], f_recv.at[d], {"kx": 1 - h})

    def kernel_last(d):
        cx = lax.rem(c + nc - d, nc)
        return remote(kb.at[cx, 1 - h], kb.at[cx, 1 - h], f_send.at[d], f_recv.at[d], {"kx": 1 - h})

    mask_self = is_self(c)
    mask_same = remote(hm.at[group_of(h, c)], mb.at[0], m_send.at[0], m_recv.at[0], owner(z, h, c))
    mask_far = remote(hm.at[groups - 1 - group_of(h, c)], mb.at[1], m_send.at[1], m_recv.at[1], owner(far, 1 - h, c))
    mask_same_land = remote(mb.at[0], mb.at[0], m_send.at[0], m_recv.at[0], home_same(cc))
    mask_far_land = remote(mb.at[1], mb.at[1], m_send.at[1], m_recv.at[1], home_far(cc))

    def visit(i):
        return jnp.where(i == 0, 0, jnp.where(i == 1, parts - 1, i - 1))

    hd_rows = hd.reshape(groups * planes * 2 * coils, lanes)

    def pack(m):
        keep = jnp.concatenate([mask[m * g + i] for i in range(g)], 1) == 1
        hm[m] = jnp.where(keep, 1.0, 0.0)

        for ri in range(2):
            value = jnp.concatenate([measured[ri, :, m * g + i] for i in range(g)], 2)
            value = jnp.where(keep, value, 0.0)
            for coil in range(coils):
                hd_rows[pl.ds(m * planes * 2 * coils + ri * coils + coil, planes, stride=2 * coils), :] = value[coil]

    load_kernel.wait()

    joined = jnp.concatenate([kernel[:, 0], kernel[:, 1]], 2)
    for i in range(2):
        kb[c, i] = joined[:, i * (coils // 2):(i + 1) * (coils // 2)]

    lane = lax.broadcasted_iota(jnp.int32, (1, chans), 1)
    first = lax.rem(lax.div(lane, band), 2) == 0
    upper = lane >= 2 * band

    def swap(x):
        return jnp.where(first, pltpu.roll(x, chans - band, 1), pltpu.roll(x, band, 1))

    def sign(s):
        return jnp.where(upper, jnp.where(first, s, -s), 1.0)

    def weights(cx):
        def some(n, _):
            plain = jnp.concatenate([kb[cx, j, pl.ds(9 * n, 9)] for j in range(2)], 1).reshape(9 * coils, chans)
            turned = swap(plain)
            rows = (plain * sign(-1.0), turned * sign(1.0),
                    pltpu.roll(plain, 2 * band, 1) * sign(1.0), pltpu.roll(turned, 2 * band, 1) * sign(-1.0))
            for i, value in enumerate(rows):
                hi, lo = split(value)
                at = pl.multiple_of(i * band + cx * coils, coils)
                hi = jnp.concatenate([hi, hi], 1)
                lo = jnp.concatenate([lo, jnp.zeros_like(lo)], 1)
                for t in range(9):
                    tap = TAPS - 1 - (9 * n + t) if i % 2 else 9 * n + t
                    w[tap, pl.ds(at, coils), :] = hi[t * coils:(t + 1) * coils]
                    w[tap, pl.ds(chans + at, coils), :] = lo[t * coils:(t + 1) * coils]
            return 0

        lax.fori_loop(0, TAPS // 9, some, 0)

    for step in range(ITERS):
        for b in range(3):
            for k in (0, planes + 1):
                xb[step, b, k] = jnp.zeros(xb.shape[3:], BF16)
            for r in (0, g + 1):
                xb[step, b, :, r] = jnp.zeros((planes + 2, row, wide), BF16)

    for step in range(ITERS):
        for sz in range(2):
            @pl.when(jnp.logical_not(near[(2 * sz - 1, 0)]["good"]))
            def _():
                hz[step, sz] = jnp.zeros(hz.shape[2:], F32)
            for sc in range(2):
                @pl.when(jnp.logical_not(near[(2 * sz - 1, 2 * sc - 1)]["good"]))
                def _():
                    hq[step, sz, sc] = jnp.zeros(hq.shape[3:], F32)
        @pl.when(jnp.logical_not(near[(0, -1)]["good"]))
        def _():
            hg[step, 0] = jnp.zeros(hg.shape[2:], F32)

    load_mask.wait()

    def pack_all(i, _):
        m = step_group(i)
        load(m).wait()
        pack(m)

        @pl.when(i == nc - 1)
        def _():
            pl.semaphore_wait(barrier, count)
            for d in range(1, nc):
                kernel_copy(d).start()
            mask_far.start()

            def launch(i, _):
                far_copy(lax.rem(i, nc), visit(lax.div(i, nc))).start()
                return 0

            lax.fori_loop(0, parts * nc, launch, 0)

        @pl.when((i >= nc) & jnp.logical_not(is_self(i - nc)))
        def _():
            def launch(n, _):
                same_copy(i - nc, visit(n)).start()
                return 0

            lax.fori_loop(0, parts, launch, 0)

        return 0

    lax.fori_loop(0, groups, pack_all, 0)

    @pl.when(jnp.logical_not(mask_self))
    def _():
        mask_same.start()

    @pl.when(mask_self)
    def _():
        mb[0] = hm[mine]

    @pl.when(stays)
    def _():
        rb[:, :, 0, c] = hd[mine]

    weights(c)
    for d in range(1, nc):
        kernel_land(d).wait_recv()
        kernel_pass(d).start()
    for d in range(1, nc):
        kernel_last(d).wait_recv()
        weights(lax.rem(c + d, nc))

    turn = reversal(lanes)
    eye = (lax.broadcasted_iota(jnp.int32, (lanes, lanes), 0) == lax.broadcasted_iota(jnp.int32, (lanes, lanes), 1))
    both = jnp.concatenate([jnp.where(eye, 1.0, 0.0).astype(BF16), turn], 1)
    def put(step, x, k, r, n, m):
        rows = n * m * row
        j = lax.rem(lax.broadcasted_iota(jnp.int32, (rows, 1), 0), row)
        shifted = (jnp.where(j > 0, pltpu.roll(x, 1, 0), 0.0), x, jnp.where(j < row - 1, pltpu.roll(x, rows - 1, 0), 0.0))
        shifted = [jnp.concatenate(split(y), 1).reshape(n, m, row, wide) for y in shifted]
        for b in range(3):
            xb[step, b, pl.ds(k, n), pl.ds(r, m)] = shifted[b]

    def transpose_in(k0):
        none = jnp.zeros((band, lanes), F32)

        def beside(s0, v0, s1, v1):
            return jnp.concatenate([jnp.concatenate(pair, 1) for pair in ((s0, none), (none, v0), (s1, none), (none, v1))], 0)

        operands = []
        for k in range(CHUNK):
            k = k0 + k
            kv = planes - 1 - k
            xs, xv = rb[k, :, 0].reshape(2, band, lanes), rb[kv, :, 1].reshape(2, band, lanes)
            ms = jnp.broadcast_to(mb[0, pl.ds(k, 1)], (band, lanes))
            mv = jnp.broadcast_to(mb[1, pl.ds(kv, 1)], (band, lanes))
            operands += [*split(beside(xs[0], xv[0], xs[1], xv[1])), beside(ms, mv, ms, mv).astype(BF16)]
        t = lax.dot_general(both, jnp.concatenate(operands, 0), NT, preferred_element_type=F32)
        t = [t[:, i * chans:(i + 1) * chans] for i in range(3 * CHUNK)]
        x = jnp.concatenate([t[3 * i] + t[3 * i + 1] for i in range(CHUNK)], 0)
        mt[pl.ds(k0, CHUNK)] = jnp.concatenate([t[3 * i + 2] for i in range(CHUNK)], 0).reshape(CHUNK, lanes, chans)
        st[0, pl.ds(k0, CHUNK)] = x.reshape(CHUNK, g, row, chans)
        put(0, x, k0 + 1, 1, CHUNK, g)

    def edge(sc, inner):
        up = eq * sc + (1 - eq) * (1 - sc)
        return up * (g - 1) if inner else up * (g + 1)

    def plane_copy(step, dz):
        v = near[(dz, 0)]
        return remote(st.at[step, planes - 1 if dz > 0 else 0], hz.at[step, v["tsz"]],
                      hz_send.at[step, v["sz"]], hz_recv.at[step, v["tsz"]], v["device"])

    def row_copy(step, dc, n):
        v = near[(0, dc)]
        k = pl.ds(n * CHUNK, CHUNK)
        return remote(st.at[step, k, edge(v["sc"], True)], hg.at[step, v["tsc"], k],
                      hg_send.at[step, v["sc"], n], hg_recv.at[step, v["tsc"], n], v["device"])

    def corner_copy(step, dz, dc):
        v = near[(dz, dc)]
        return remote(st.at[step, planes - 1 if dz > 0 else 0, edge(v["sc"], True)], hq.at[step, v["tsz"], v["tsc"]],
                      hq_send.at[step, v["sz"], v["sc"]], hq_recv.at[step, v["tsz"], v["tsc"]], v["device"])

    def start_halo(step, n):
        for dc in (1, -1):
            @pl.when(near[(0, dc)]["good"])
            def _():
                row_copy(step, dc, n).start()
        for dz in (-1, 1):
            @pl.when(n == (parts - 1 if dz > 0 else 0))
            def _():
                @pl.when(near[(dz, 0)]["good"])
                def _():
                    plane_copy(step, dz).start()
                for dc in (1, -1):
                    @pl.when(near[(dz, dc)]["good"])
                    def _():
                        corner_copy(step, dz, dc).start()
                v = near[(dz, -1)]

                @pl.when(v["alone"])
                def _():
                    hq[step, v["sz"], v["sc"]] = st[step, planes - 1 if dz > 0 else 0, edge(v["sc"], True)]

    def flipped(x, rows):
        hi, lo = split(x)
        y = jnp.dot(reversal(rows), jnp.concatenate([hi, lo], 1), preferred_element_type=F32)
        return swap(y[:, :chans] + y[:, chans:])

    def place_halo(step, d, buf, n, m):
        rows = n * m * row
        x = buf[...].reshape(rows, chans)
        x = jnp.where(near[d]["flip"] == 1, flipped(x, rows), x)
        k = 1 if d[0] == 0 else (planes + 1 if d[0] > 0 else 0)
        r = 1 if d[1] == 0 else edge(near[d]["sc"], False)
        put(step, x, k, r, n, m)

    def product(xs, ws):
        p = lax.dot_general(jnp.concatenate(xs, 1), jnp.concatenate(ws, 1), NT, preferred_element_type=F32)
        return p[:, :chans] + p[:, chans:]

    def convolve(step, n):
        return product([xb[step, (t // 3) % 3, pl.ds(n * CHUNK + t % 3, CHUNK), pl.ds(t // 9, g)].reshape(CHUNK * lanes, wide)
                        for t in range(TAPS)], [w[t] for t in range(TAPS)])

    def inner(n):
        acc[pl.ds(n * CHUNK, CHUNK)] = convolve(0, n).reshape(CHUNK, g, row, chans)

    def take_planes(step):
        for dz in (-1, 1):
            v = near[(dz, 0)]
            buf = hz.at[step, v["sz"]]

            @pl.when(v["good"])
            def _():
                remote(buf, buf, hz_send.at[step, v["sz"]], hz_recv.at[step, v["sz"]], v["device"]).wait_recv()

            place_halo(step, (dz, 0), buf, 1, g)

    def take_rows(step):
        for dc in (-1, 1):
            v = near[(0, dc)]
            buf = hg.at[step, v["sc"]]

            @pl.when(v["good"])
            def _():
                for n in range(parts):
                    part = buf.at[pl.ds(n * CHUNK, CHUNK)]
                    remote(part, part, hg_send.at[step, v["sc"], n], hg_recv.at[step, v["sc"], n], v["device"]).wait_recv()

            place_halo(step, (0, dc), buf, planes, 1)
            for dz in (-1, 1):
                u = near[(dz, dc)]
                corner = hq.at[step, u["sz"], u["sc"]]

                @pl.when(u["good"])
                def _():
                    remote(corner, corner, hq_send.at[step, u["sz"], u["sc"]], hq_recv.at[step, u["sz"], u["sc"]],
                           u["device"]).wait_recv()

                place_halo(step, (dz, dc), corner, 1, 1)

    def add_rows():
        for r, a in ((0, 0), (g - 1, 2)):
            taps = [9 * a + t for t in range(9)]
            p = product([xb[0, (t // 3) % 3, t % 3:t % 3 + planes, r + a].reshape(planes * row, wide) for t in taps],
                        [w[t] for t in taps])
            acc[:, r] += p.reshape(planes, row, chans)

    mask_far_land.wait_recv()

    @pl.when(jnp.logical_not(stays & (c == cc)))
    def _():
        mask_same_land.wait_recv()

    def update(step, k):
        k = pl.ds(k, CHUNK)
        rows = CHUNK * lanes
        x = jnp.where(mt[k].reshape(rows, chans) > 0.5, st[0, k].reshape(rows, chans), acc[k].reshape(rows, chans))
        st[step, k] = x.reshape(CHUNK, g, row, chans)
        put(step, x, k.start + 1, 1, CHUNK, g)

    def arrive(i, _):
        n = visit(i)
        for cx in range(nc):
            @pl.when(jnp.logical_not(stays & (c == cx)))
            def _():
                same_land(cx, n).wait_recv()

            far_land(cx, n).wait_recv()
        transpose_in(n * CHUNK)
        start_halo(0, n)

        @pl.when(i > 2)
        def _():
            inner(n - 1)

        return 0

    lax.fori_loop(0, parts, arrive, 0)

    def rest(n, _):
        inner(n)
        return 0

    take_planes(0)
    inner(0)
    lax.fori_loop(parts - 2, parts, rest, 0)
    take_rows(0)
    add_rows()

    def renew(i, _):
        n = visit(i)
        update(1, n * CHUNK)
        start_halo(1, n)
        return 0

    lax.fori_loop(0, parts, renew, 0)
    take_planes(1)
    take_rows(1)

    def same_back(cx, n):
        k = pl.ds(n * CHUNK, CHUNK)
        return remote(ob.at[k, :, 0, cx], fr.at[mine, k], os_send.at[cx, n], os_recv.at[cc, n], home_same(cx))

    def far_back(cx, n):
        k = pl.ds(planes - (n + 1) * CHUNK, CHUNK)
        return remote(ob.at[k, :, 1, cx], fr.at[groups - 1 - mine, k], ov_send.at[cx, n], ov_recv.at[cc, n], home_far(cx))

    turn2 = jnp.concatenate([turn, turn], 1)

    def finish(n, _):
        result = convolve(ITERS - 1, n)
        r = [result[i * lanes:(i + 1) * lanes] for i in range(CHUNK)]
        back = jnp.dot(turn2, jnp.concatenate([jnp.concatenate(split(x), 0) for x in r], 1), preferred_element_type=F32)
        y = [jnp.where(first, r[i], back[:, i * chans:(i + 1) * chans]).T.reshape(2, 2, nc, coils, lanes) for i in range(CHUNK)]
        for i in range(CHUNK):
            k = n * CHUNK + i
            ob[k, :, 0] = y[i][:, 0]
            ob[planes - 1 - k, :, 1] = y[i][:, 1]
        for cx in range(nc):
            far_back(cx, n).start()
        for cx in range(nc):
            @pl.when(jnp.logical_not(stays & (c == cx)))
            def _():
                same_back(cx, n).start()

        return 0

    lax.fori_loop(0, parts, finish, 0)

    @pl.when(stays)
    def _():
        fr[mine] = ob[:, :, 0, c]

    def merge(m):
        keep = [jnp.broadcast_to(hm[m, k:k + 1], (2 * coils, lanes)).reshape(2, coils, lanes) for k in range(planes)]
        out[m] = jnp.stack([jnp.where(keep[k] > 0.5, hd[m, k], fr[m, k]) for k in range(planes)], 0)

    def home(i, _):
        place = lax.rem(i, nc)
        m = group_of(h, place)

        def same_home(n, _):
            k = pl.ds(n * CHUNK, CHUNK)
            remote(fr.at[m, k], fr.at[m, k], os_send.at[place, n], os_recv.at[place, n], owner(z, h, place)).wait_recv()
            return 0

        def far_home(n, _):
            k = pl.ds(planes - (n + 1) * CHUNK, CHUNK)
            there = fr.at[groups - 1 - m, k]
            remote(there, there, ov_send.at[place, n], ov_recv.at[place, n], owner(far, 1 - h, place)).wait_recv()
            return 0

        @pl.when((i < nc) & jnp.logical_not(is_self(place)))
        def _():
            lax.fori_loop(0, parts, same_home, 0)

        @pl.when(i >= nc)
        def _():
            lax.fori_loop(0, parts, far_home, 0)

        merge(jnp.where(i < nc, m, groups - 1 - m))
        return 0

    lax.fori_loop(0, groups, home, 0)

    def sent(n, _):
        for i in range(nc):
            far_copy(i, n).wait_send()
            far_back(i, n).wait_send()

            @pl.when(jnp.logical_not(is_self(i)))
            def _():
                same_copy(i, n).wait_send()

            @pl.when(jnp.logical_not(stays & (c == i)))
            def _():
                same_back(i, n).wait_send()

        return 0

    lax.fori_loop(0, parts, sent, 0)
    for d in range(1, nc):
        kernel_copy(d).wait_send()
        kernel_pass(d).wait_send()
    mask_far.wait_send()

    @pl.when(jnp.logical_not(mask_self))
    def _():
        mask_same.wait_send()

    def passed(step, _):
        for d in dirs:
            @pl.when(near[d]["good"])
            def _():
                if d[1] == 0:
                    plane_copy(step, d[0]).wait_send()
                elif d[0] == 0:
                    for n in range(parts):
                        row_copy(step, d[1], n).wait_send()
                else:
                    corner_copy(step, *d).wait_send()

        return 0

    lax.fori_loop(0, ITERS, passed, 0)


def unpack(packed, out_hbm, out, sem):
    groups, planes, _, coils, lanes = packed.shape
    row = out.shape[4]
    g = lanes // row
    rows = packed.reshape(groups * planes * 2 * coils, lanes)

    def store(m):
        at = pl.ds(m * g, g)
        return pltpu.make_async_copy(out.at[:, :, at], out_hbm.at[:, :, at], sem.at[m])

    def group(m, _):
        for ri in range(2):
            value = jnp.stack([rows[pl.ds(m * planes * 2 * coils + ri * coils + coil, planes, stride=2 * coils), :]
                               for coil in range(coils)], 0)
            for i in range(g):
                out[ri, :, m * g + i] = value[:, :, i * row:(i + 1) * row]
        store(m).start()
        return 0

    lax.fori_loop(0, groups, group, 0)
    for m in range(groups):
        store(m).wait()


def on_device(sizes, measured, mask, kernel):
    nz, nc = sizes
    _, coils, depth_x, planes, row = measured.shape
    groups = 2 * nc
    g = depth_x // groups
    lanes = g * row
    chans = 4 * nc * coils
    parts = planes // CHUNK
    vmem = pl.BlockSpec(memory_space=pltpu.VMEM)
    dma = pltpu.SemaphoreType.DMA
    packed = pl.pallas_call(
        functools.partial(body, sizes),
        out_shape=jax.ShapeDtypeStruct((groups, planes, 2, coils, lanes), F32),
        in_specs=[pl.BlockSpec(memory_space=pltpu.HBM)] * 3,
        out_specs=vmem,
        scratch_shapes=[
            pltpu.VMEM(measured.shape, F32),
            pltpu.VMEM(mask.shape, jnp.int32),
            pltpu.VMEM(kernel.shape, F32),
            pltpu.VMEM((groups, planes, 2, coils, lanes), F32),
            pltpu.VMEM((groups, planes, lanes), F32),
            pltpu.VMEM((planes, 2, 2, nc, coils, lanes), F32),
            pltpu.VMEM((2, planes, lanes), F32),
            pltpu.VMEM((nc, 2, TAPS, coils // 2, chans), F32),
            pltpu.VMEM((TAPS, 2 * chans, 2 * chans), BF16),
            pltpu.VMEM((ITERS, planes, g, row, chans), F32),
            pltpu.VMEM((planes, lanes, chans), F32),
            pltpu.VMEM((ITERS, 3, planes + 2, g + 2, row, 2 * chans), BF16),
            pltpu.VMEM((ITERS, 2, g, row, chans), F32),
            pltpu.VMEM((ITERS, 2, planes, row, chans), F32),
            pltpu.VMEM((ITERS, 2, 2, row, chans), F32),
            pltpu.VMEM((planes, g, row, chans), F32),
            pltpu.VMEM((planes, 2, 2, nc, coils, lanes), F32),
            pltpu.VMEM((groups, planes, 2, coils, lanes), F32),
            dma((groups + 2,)),
            dma((nc, parts)), dma((nc, parts)), dma((nc, parts)), dma((nc, parts)),
            dma((nc,)), dma((nc,)), dma((nc,)), dma((nc,)), dma((2,)), dma((2,)),
            dma((ITERS, 2)), dma((ITERS, 2)), dma((ITERS, 2, parts)), dma((ITERS, 2, parts)),
            dma((ITERS, 2, 2)), dma((ITERS, 2, 2)),
            dma((nc, parts)), dma((nc, parts)), dma((nc, parts)), dma((nc, parts)),
        ],
        compiler_params=pltpu.CompilerParams(collective_id=0, has_side_effects=True, vmem_limit_bytes=VLIM << 20),
    )(*(pltpu.with_memory_space_constraint(x, pltpu.HBM) for x in (measured, mask, kernel)))
    return pl.pallas_call(
        unpack,
        out_shape=jax.ShapeDtypeStruct(measured.shape, F32),
        in_specs=[vmem],
        out_specs=pl.BlockSpec(memory_space=pl.ANY),
        scratch_shapes=[pltpu.VMEM(measured.shape, F32), dma((groups,))],
        compiler_params=pltpu.CompilerParams(vmem_limit_bytes=16 << 20),
    )(packed)


def solution(mesh):
    placed = (
        P(None, ("grp", "coil"), "kx", "kz", None),
        P(("grp", "kx"), "kz", None),
        P(None, None, "coil", None),
    )
    return jax.shard_map(
        functools.partial(on_device, (mesh.shape["kz"], mesh.shape["coil"])),
        mesh=mesh,
        in_specs=placed,
        out_specs=P(None, ("grp", "coil"), "kx", "kz", None),
        check_vma=False,
    )
```

```python
import functools

import jax
import jax.numpy as jnp
from jax import lax
from jax.experimental import pallas as pl
from jax.experimental.pallas import tpu as pltpu
from jax.sharding import PartitionSpec as P

ITERS = 2
TAPS = 27
CHUNK = 2
VLIM = 40
MESH = pl.DeviceIdType.MESH
F32, BF16 = jnp.float32, jnp.bfloat16
NT = (((1,), (1,)), ((), ()))


def split(x):
    hi = x.astype(BF16)
    return hi, (x - hi.astype(F32)).astype(BF16)


def reversal(n):
    i = lax.broadcasted_iota(jnp.int32, (n, n), 0) + lax.broadcasted_iota(jnp.int32, (n, n), 1)
    return jnp.where(i == n - 1, 1.0, 0.0).astype(BF16)


def body(sizes, measured_hbm, mask_hbm, kernel_hbm, out, measured, mask, kernel, hd, hm, rb, mb, kb, w, st, mt, xb, hz, hg, hq, acc, ob, fr,
         in_sem, s_send, s_recv, v_send, v_recv, k_send, k_recv, f_send, f_recv, m_send, m_recv,
         hz_send, hz_recv, hg_send, hg_recv, hq_send, hq_recv, os_send, os_recv, ov_send, ov_recv):
    nz, nc = sizes
    _, coils, depth_x, planes, row = measured.shape
    half = nz // 2
    groups = 2 * nc
    g = depth_x // groups
    halves = g // 2
    plane = g * row
    lanes = 2 * CHUNK * row
    band = nc * coils
    chans = 4 * band
    wide = 2 * chans
    parts = planes // CHUNK

    z, c, h = lax.axis_index("kz"), lax.axis_index("coil"), lax.axis_index("kx")
    side = lax.div(z, half)
    far = nz - 1 - z

    def owner(tz, thalf, place):
        q = lax.rem(thalf + lax.div(tz, half), 2)
        return {"kz": tz, "coil": q * (nc // 2) + lax.div(place, 2), "kx": lax.rem(place, 2)}

    kxh = lax.rem(lax.div(c, nc // 2) + side, 2)
    cc = lax.rem(c, nc // 2) * 2 + h
    stays = kxh == h

    def group_of(khalf, place):
        even = lax.rem(side + khalf + 1, 2)
        return even * place + (1 - even) * (groups - 1 - place)

    eq = lax.rem(side + kxh + 1, 2)
    mine = group_of(kxh, cc)

    def neighbour(dz, dc):
        zt = z + dz
        good = (zt >= 0) & (zt < nz)
        zt = lax.max(lax.min(zt, nz - 1), 0)
        over = lax.rem(lax.div(zt, half) + side, 2)
        inter = lax.div(cc + 1, nc) if dc > 0 else 0
        core = 1 - lax.min(cc, 1) if dc < 0 else 0
        if dc < 0:
            good = good & ((side == 1) | (cc > 0))
        flip = lax.rem(over + inter, 2)
        tz = flip * (nz - 1 - zt) + (1 - flip) * zt
        sz, sc = (dz + 1) // 2, (dc + 1) // 2
        stay = inter + core
        alone = (over * core == 1) & good
        return dict(good=good & jnp.logical_not(alone), alone=alone, flip=flip,
                    device=owner(tz, lax.rem(kxh + flip + core, 2), cc + dc - inter + core), sz=sz, sc=sc,
                    tsz=flip * sz + (1 - flip) * (1 - sz), tsc=stay * sc + (1 - stay) * (1 - sc))

    dirs = [(dz, dc) for dz in (-1, 0, 1) for dc in (-1, 0, 1) if dz or dc]
    near = {d: neighbour(*d) for d in dirs}

    def load(m):
        at = pl.ds(m * g, g)
        return pltpu.make_async_copy(measured_hbm.at[:, :, at], measured.at[:, :, at], in_sem.at[m])

    load_kernel = pltpu.make_async_copy(kernel_hbm, kernel, in_sem.at[groups])
    load_mask = pltpu.make_async_copy(mask_hbm, mask, in_sem.at[groups + 1])

    def step_group(i):
        m = group_of(h, lax.rem(i, nc))
        return jnp.where(i < nc, groups - 1 - m, m)

    load_mask.start()
    load_kernel.start()
    for i in range(groups):
        load(step_group(i)).start()

    def home_same(cx):
        return {"kz": z, "coil": cx, "kx": kxh}

    def home_far(cx):
        return {"kz": far, "coil": cx, "kx": 1 - kxh}

    def is_self(place):
        return stays & (cc == place)

    barrier = pltpu.get_barrier_semaphore()

    def greet(device):
        pl.semaphore_signal(barrier, inc=1, device_id=device, device_id_type=MESH)

    for i in range(nc):
        greet(owner(far, 1 - h, i))
        greet(home_far(i))

        @pl.when(jnp.logical_not(is_self(i)))
        def _():
            greet(owner(z, h, i))

        @pl.when(jnp.logical_not(stays & (c == i)))
        def _():
            greet(home_same(i))

    for d in range(1, nc):
        greet({"coil": lax.rem(c + d, nc)})
    greet({"kx": 1 - h})
    count = 2 * nc + 2 * (nc - stays.astype(jnp.int32)) + nc
    for d in dirs:
        @pl.when(near[d]["good"])
        def _():
            greet(near[d]["device"])
        count = count + near[d]["good"].astype(jnp.int32)

    def remote(src, dst, send, recv, device):
        return pltpu.make_async_remote_copy(
            src_ref=src, dst_ref=dst, send_sem=send, recv_sem=recv, device_id=device, device_id_type=MESH)

    def slot(n, q):
        return n * CHUNK + q

    def back_slot(n, q):
        return (parts - 1 - n) * CHUNK + q

    def same_copy(i, n, q):
        k = slot(n, q)
        return remote(hd.at[group_of(h, i), k], rb.at[k, :, 0, c], s_send.at[i, k], s_recv.at[c, k], owner(z, h, i))

    def same_land(cx, n, q):
        k = slot(n, q)
        return remote(rb.at[k, :, 0, cx], rb.at[k, :, 0, cx], s_send.at[cx, k], s_recv.at[cx, k], home_same(cx))

    def far_copy(i, n, q):
        k = back_slot(n, q)
        return remote(hd.at[groups - 1 - group_of(h, i), k], rb.at[k, :, 1, c], v_send.at[i, k], v_recv.at[c, k], owner(far, 1 - h, i))

    def far_land(cx, n, q):
        k = back_slot(n, q)
        return remote(rb.at[k, :, 1, cx], rb.at[k, :, 1, cx], v_send.at[cx, k], v_recv.at[cx, k], home_far(cx))

    def kernel_copy(d):
        return remote(kb.at[c, h], kb.at[c, h], k_send.at[d], k_recv.at[d], {"coil": lax.rem(c + d, nc)})

    def kernel_land(d):
        cx = lax.rem(c + nc - d, nc)
        return remote(kb.at[cx, h], kb.at[cx, h], k_send.at[d], k_recv.at[d], {"coil": cx})

    def kernel_pass(d):
        cx = lax.rem(c + nc - d, nc)
        return remote(kb.at[cx, h], kb.at[cx, h], f_send.at[d], f_recv.at[d], {"kx": 1 - h})

    def kernel_last(d):
        cx = lax.rem(c + nc - d, nc)
        return remote(kb.at[cx, 1 - h], kb.at[cx, 1 - h], f_send.at[d], f_recv.at[d], {"kx": 1 - h})

    mask_self = is_self(c)
    mask_same = remote(hm.at[group_of(h, c)], mb.at[0], m_send.at[0], m_recv.at[0], owner(z, h, c))
    mask_far = remote(hm.at[groups - 1 - group_of(h, c)], mb.at[1], m_send.at[1], m_recv.at[1], owner(far, 1 - h, c))
    mask_same_land = remote(mb.at[0], mb.at[0], m_send.at[0], m_recv.at[0], home_same(cc))
    mask_far_land = remote(mb.at[1], mb.at[1], m_send.at[1], m_recv.at[1], home_far(cc))

    def visit(i):
        return jnp.where(i == 0, 0, jnp.where(i == 1, parts - 1, i - 1))

    hd_rows = hd.reshape(groups * planes * 2 * coils, lanes)

    def weave(tile):
        a = jnp.concatenate([tile(0), tile(g - 1)], -1)
        axis = a.ndim - 2
        even = jnp.concatenate([a, pltpu.roll(a, planes - 1, axis)], -1)
        if halves == 1:
            return even
        b = jnp.concatenate([tile(1), tile(g - 2)], -1)
        odd = jnp.concatenate([pltpu.roll(b, 1, axis), b], -1)
        return jnp.where(lax.rem(lax.broadcasted_iota(jnp.int32, even.shape, axis), 2) == 0, even, odd)

    def pack(m):
        keep = weave(lambda i: mask[m * g + i]) == 1
        hm[m] = jnp.where(keep, 1.0, 0.0)
        for ri in range(2):
            value = jnp.where(keep, weave(lambda i: measured[ri, :, m * g + i]), 0.0)
            for coil in range(coils):
                hd_rows[pl.ds(m * planes * 2 * coils + ri * coils + coil, planes, stride=2 * coils), :] = value[coil]

    load_kernel.wait()

    joined = jnp.concatenate([kernel[:, 0], kernel[:, 1]], 2)
    for i in range(2):
        kb[c, i] = joined[:, i * (coils // 2):(i + 1) * (coils // 2)]

    lane = lax.broadcasted_iota(jnp.int32, (1, chans), 1)
    first = lax.rem(lax.div(lane, band), 2) == 0
    upper = lane >= 2 * band

    def swap(x):
        return jnp.where(first, pltpu.roll(x, chans - band, 1), pltpu.roll(x, band, 1))

    def sign(s):
        return jnp.where(upper, jnp.where(first, s, -s), 1.0)

    def weights(cx):
        def some(n, _):
            plain = jnp.concatenate([kb[cx, j, pl.ds(9 * n, 9)] for j in range(2)], 1).reshape(9 * coils, chans)
            turned = swap(plain)
            rows = (plain * sign(-1.0), turned * sign(1.0),
                    pltpu.roll(plain, 2 * band, 1) * sign(1.0), pltpu.roll(turned, 2 * band, 1) * sign(-1.0))
            for i, value in enumerate(rows):
                hi, lo = split(value)
                at = pl.multiple_of(i * band + cx * coils, coils)
                hi = jnp.concatenate([hi, hi], 1)
                lo = jnp.concatenate([lo, jnp.zeros_like(lo)], 1)
                for t in range(9):
                    tap = TAPS - 1 - (9 * n + t) if i % 2 else 9 * n + t
                    w[tap, pl.ds(at, coils), :] = hi[t * coils:(t + 1) * coils]
                    w[tap, pl.ds(chans + at, coils), :] = lo[t * coils:(t + 1) * coils]
            return 0

        lax.fori_loop(0, TAPS // 9, some, 0)

    for step in range(ITERS):
        for b in range(3):
            for k in (0, planes + 1):
                xb[step, b, k] = jnp.zeros(xb.shape[3:], BF16)
            for r in (0, g + 1):
                xb[step, b, :, r] = jnp.zeros((planes + 2, row, wide), BF16)

    for step in range(ITERS):
        for sz in range(2):
            @pl.when(jnp.logical_not(near[(2 * sz - 1, 0)]["good"]))
            def _():
                hz[step, sz] = jnp.zeros(hz.shape[2:], F32)
            for sc in range(2):
                @pl.when(jnp.logical_not(near[(2 * sz - 1, 2 * sc - 1)]["good"]))
                def _():
                    hq[step, sz, sc] = jnp.zeros(hq.shape[3:], F32)
        @pl.when(jnp.logical_not(near[(0, -1)]["good"]))
        def _():
            hg[step, 0] = jnp.zeros(hg.shape[2:], F32)

    load_mask.wait()

    def pack_all(i, _):
        m = step_group(i)
        load(m).wait()
        pack(m)

        @pl.when(i == nc - 1)
        def _():
            pl.semaphore_wait(barrier, count)
            for d in range(1, nc):
                kernel_copy(d).start()
            mask_far.start()

            for q in range(halves):
                def launch(i, _):
                    far_copy(lax.rem(i, nc), visit(lax.div(i, nc)), q).start()
                    return 0

                lax.fori_loop(0, parts * nc, launch, 0)

        @pl.when((i >= nc) & jnp.logical_not(is_self(i - nc)))
        def _():
            for q in range(halves):
                def launch(n, _):
                    same_copy(i - nc, visit(n), q).start()
                    return 0

                lax.fori_loop(0, parts, launch, 0)

        return 0

    lax.fori_loop(0, groups, pack_all, 0)

    @pl.when(jnp.logical_not(mask_self))
    def _():
        mask_same.start()

    @pl.when(mask_self)
    def _():
        mb[0] = hm[mine]

    @pl.when(stays)
    def _():
        rb[:, :, 0, c] = hd[mine]

    weights(c)
    for d in range(1, nc):
        kernel_land(d).wait_recv()
        kernel_pass(d).start()
    for d in range(1, nc):
        kernel_last(d).wait_recv()
        weights(lax.rem(c + d, nc))

    turn = reversal(lanes)
    eye = (lax.broadcasted_iota(jnp.int32, (lanes, lanes), 0) == lax.broadcasted_iota(jnp.int32, (lanes, lanes), 1))
    both = jnp.concatenate([jnp.where(eye, 1.0, 0.0).astype(BF16), turn], 1)
    def put(step, x, k, n, at):
        rows = n * len(at) * row
        j = lax.rem(lax.broadcasted_iota(jnp.int32, (rows, 1), 0), row)
        shifted = (jnp.where(j > 0, pltpu.roll(x, 1, 0), 0.0), x, jnp.where(j < row - 1, pltpu.roll(x, rows - 1, 0), 0.0))
        shifted = [jnp.concatenate(split(y), 1).reshape(n, len(at), row, wide) for y in shifted]
        for b in range(3):
            for i, r in enumerate(at):
                xb[step, b, pl.ds(k, n), r] = shifted[b][:, i]

    def pair(q):
        return q, g - 1 - q

    def transpose_in(n, q):
        none = jnp.zeros((band, lanes), F32)

        def beside(s0, v0, s1, v1):
            return jnp.concatenate([jnp.concatenate(both, 1) for both in ((s0, none), (none, v0), (s1, none), (none, v1))], 0)

        ks, kv = slot(n, q), back_slot(n, q)
        xs, xv = rb[ks, :, 0].reshape(2, band, lanes), rb[kv, :, 1].reshape(2, band, lanes)
        ms = jnp.broadcast_to(mb[0, pl.ds(ks, 1)], (band, lanes))
        mv = jnp.broadcast_to(mb[1, pl.ds(kv, 1)], (band, lanes))
        operand = [*split(beside(xs[0], xv[0], xs[1], xv[1])), beside(ms, mv, ms, mv).astype(BF16)]
        t = lax.dot_general(both, jnp.concatenate(operand, 0), NT, preferred_element_type=F32)
        x = t[:, :chans] + t[:, chans:2 * chans]
        kept = t[:, 2 * chans:].reshape(CHUNK, 2, row, chans)
        here = x.reshape(CHUNK, 2, row, chans)
        k = pl.ds(n * CHUNK, CHUNK)
        for i, r in enumerate(pair(q)):
            mt[k, r] = kept[:, i]
            st[0, k, r] = here[:, i]
        put(0, x, n * CHUNK + 1, CHUNK, [r + 1 for r in pair(q)])

    def edge(sc, inner):
        up = eq * sc + (1 - eq) * (1 - sc)
        return up * (g - 1) if inner else up * (g + 1)

    def plane_copy(step, dz):
        v = near[(dz, 0)]
        return remote(st.at[step, planes - 1 if dz > 0 else 0], hz.at[step, v["tsz"]],
                      hz_send.at[step, v["sz"]], hz_recv.at[step, v["tsz"]], v["device"])

    def row_copy(step, dc, n):
        v = near[(0, dc)]
        k = pl.ds(n * CHUNK, CHUNK)
        return remote(st.at[step, k, edge(v["sc"], True)], hg.at[step, v["tsc"], k],
                      hg_send.at[step, v["sc"], n], hg_recv.at[step, v["tsc"], n], v["device"])

    def corner_copy(step, dz, dc):
        v = near[(dz, dc)]
        return remote(st.at[step, planes - 1 if dz > 0 else 0, edge(v["sc"], True)], hq.at[step, v["tsz"], v["tsc"]],
                      hq_send.at[step, v["sz"], v["sc"]], hq_recv.at[step, v["tsz"], v["tsc"]], v["device"])

    def send_plane(step, dz):
        @pl.when(near[(dz, 0)]["good"])
        def _():
            plane_copy(step, dz).start()

    def send_rows(step, n):
        for dc in (1, -1):
            @pl.when(near[(0, dc)]["good"])
            def _():
                row_copy(step, dc, n).start()
        for dz in (-1, 1):
            @pl.when(n == (parts - 1 if dz > 0 else 0))
            def _():
                for dc in (1, -1):
                    @pl.when(near[(dz, dc)]["good"])
                    def _():
                        corner_copy(step, dz, dc).start()
                v = near[(dz, -1)]

                @pl.when(v["alone"])
                def _():
                    hq[step, v["sz"], v["sc"]] = st[step, planes - 1 if dz > 0 else 0, edge(v["sc"], True)]

    def send_planes(step, n):
        for dz in (-1, 1):
            @pl.when(n == (parts - 1 if dz > 0 else 0))
            def _():
                send_plane(step, dz)

    def flipped(x, rows):
        hi, lo = split(x)
        y = jnp.dot(reversal(rows), jnp.concatenate([hi, lo], 1), preferred_element_type=F32)
        return swap(y[:, :chans] + y[:, chans:])

    def place_halo(step, d, buf, n, m):
        rows = n * m * row
        x = buf[...].reshape(rows, chans)
        x = jnp.where(near[d]["flip"] == 1, flipped(x, rows), x)
        k = 1 if d[0] == 0 else (planes + 1 if d[0] > 0 else 0)
        put(step, x, k, n, range(1, g + 1) if d[1] == 0 else [edge(near[d]["sc"], False)])

    def product(xs, ws):
        p = lax.dot_general(jnp.concatenate(xs, 1), jnp.concatenate(ws, 1), NT, preferred_element_type=F32)
        return p[:, :chans] + p[:, chans:]

    def convolve(step, n):
        return product([xb[step, (t // 3) % 3, pl.ds(n * CHUNK + t % 3, CHUNK), pl.ds(t // 9, g)].reshape(CHUNK * plane, wide)
                        for t in range(TAPS)], [w[t] for t in range(TAPS)])

    def take_planes(step):
        for dz in (-1, 1):
            v = near[(dz, 0)]
            buf = hz.at[step, v["sz"]]

            @pl.when(v["good"])
            def _():
                remote(buf, buf, hz_send.at[step, v["sz"]], hz_recv.at[step, v["sz"]], v["device"]).wait_recv()

            place_halo(step, (dz, 0), buf, 1, g)

    def take_rows(step):
        for dc in (-1, 1):
            v = near[(0, dc)]
            buf = hg.at[step, v["sc"]]

            @pl.when(v["good"])
            def _():
                for n in range(parts):
                    part = buf.at[pl.ds(n * CHUNK, CHUNK)]
                    remote(part, part, hg_send.at[step, v["sc"], n], hg_recv.at[step, v["sc"], n], v["device"]).wait_recv()

            place_halo(step, (0, dc), buf, planes, 1)
            for dz in (-1, 1):
                u = near[(dz, dc)]
                corner = hq.at[step, u["sz"], u["sc"]]

                @pl.when(u["good"])
                def _():
                    remote(corner, corner, hq_send.at[step, u["sz"], u["sc"]], hq_recv.at[step, u["sz"], u["sc"]],
                           u["device"]).wait_recv()

                place_halo(step, (dz, dc), corner, 1, 1)

    def add_rows(step):
        for r, a in ((0, 0), (g - 1, 2)):
            taps = [9 * a + t for t in range(9)]
            p = product([xb[step, (t // 3) % 3, t % 3:t % 3 + planes, r + a].reshape(planes * row, wide) for t in taps],
                        [w[t] for t in taps])
            acc[:, r] += p.reshape(planes, row, chans)

    mask_far_land.wait_recv()

    @pl.when(jnp.logical_not(stays & (c == cc)))
    def _():
        mask_same_land.wait_recv()

    def landed(n, q):
        for cx in range(nc):
            @pl.when(jnp.logical_not(stays & (c == cx)))
            def _():
                same_land(cx, n, q).wait_recv()

            far_land(cx, n, q).wait_recv()

    def arrive_edges(i, _):
        n = visit(i)
        landed(n, 0)
        transpose_in(n, 0)
        send_rows(0, n)
        return 0

    lax.fori_loop(0, parts, arrive_edges, 0)

    def arrive_rest(i, _):
        n = visit(i)
        for q in range(1, halves):
            landed(n, q)
            transpose_in(n, q)
        send_planes(0, n)
        return 0

    lax.fori_loop(0, parts, arrive_rest, 0)

    for step in range(ITERS - 1):
        take_rows(step)
        take_planes(step)

        def iterate(i, _):
            n = visit(i)
            k = pl.ds(n * CHUNK, CHUNK)
            rows = CHUNK * plane
            result = convolve(step, n)
            x = jnp.where(mt[k].reshape(rows, chans) > 0.5, st[0, k].reshape(rows, chans), result)
            st[step + 1, k] = x.reshape(CHUNK, g, row, chans)
            put(step + 1, x, n * CHUNK + 1, CHUNK, range(1, g + 1))
            send_rows(step + 1, n)
            send_planes(step + 1, n)
            return 0

        lax.fori_loop(0, parts, iterate, 0)

    def same_back(cx, n, q):
        k = slot(n, q)
        return remote(ob.at[k, :, 0, cx], fr.at[mine, k], os_send.at[cx, k], os_recv.at[cc, k], home_same(cx))

    def far_back(cx, n, q):
        k = back_slot(n, q)
        return remote(ob.at[k, :, 1, cx], fr.at[groups - 1 - mine, k], ov_send.at[cx, k], ov_recv.at[cc, k], home_far(cx))

    turn2 = jnp.concatenate([turn, turn], 1)

    def finish(x, n, q):
        r = jnp.stack([x[:, i] for i in pair(q)], 1).reshape(lanes, chans)
        back = jnp.dot(turn2, jnp.concatenate(split(r), 0), preferred_element_type=F32)
        y = jnp.where(first, r, back).T.reshape(2, 2, nc, coils, lanes)
        ob[slot(n, q), :, 0] = y[:, 0]
        ob[back_slot(n, q), :, 1] = y[:, 1]
        for cx in range(nc):
            far_back(cx, n, q).start()
        for cx in range(nc):
            @pl.when(jnp.logical_not(stays & (c == cx)))
            def _():
                same_back(cx, n, q).start()

    def ahead(i, _):
        n = jnp.where(i < parts - 2, i + 1, jnp.where(i == parts - 2, 0, parts - 1))

        @pl.when(i == parts - 2)
        def _():
            take_planes(ITERS - 1)

        result = convolve(ITERS - 1, n).reshape(CHUNK, g, row, chans)
        acc[pl.ds(n * CHUNK, CHUNK)] = result
        for q in range(1, halves):
            finish(result, n, q)
        return 0

    lax.fori_loop(0, parts, ahead, 0)
    take_rows(ITERS - 1)
    add_rows(ITERS - 1)

    def edges(i, _):
        n = visit(i)
        finish(acc[pl.ds(n * CHUNK, CHUNK)], n, 0)
        return 0

    lax.fori_loop(0, parts, edges, 0)

    @pl.when(stays)
    def _():
        fr[mine] = ob[:, :, 0, c]

    def merge(m):
        keep = [jnp.broadcast_to(hm[m, k:k + 1], (2 * coils, lanes)).reshape(2, coils, lanes) for k in range(planes)]
        out[m] = jnp.stack([jnp.where(keep[k] > 0.5, hd[m, k], fr[m, k]) for k in range(planes)], 0)

    def home(i, _):
        place = lax.rem(i, nc)
        m = group_of(h, place)

        def same_home(n, _):
            for q in range(halves):
                there = fr.at[m, slot(n, q)]
                k = slot(n, q)
                remote(there, there, os_send.at[place, k], os_recv.at[place, k], owner(z, h, place)).wait_recv()
            return 0

        def far_home(n, _):
            for q in range(halves):
                k = back_slot(n, q)
                there = fr.at[groups - 1 - m, k]
                remote(there, there, ov_send.at[place, k], ov_recv.at[place, k], owner(far, 1 - h, place)).wait_recv()
            return 0

        @pl.when((i < nc) & jnp.logical_not(is_self(place)))
        def _():
            lax.fori_loop(0, parts, same_home, 0)

        @pl.when(i >= nc)
        def _():
            lax.fori_loop(0, parts, far_home, 0)

        merge(jnp.where(i < nc, m, groups - 1 - m))
        return 0

    lax.fori_loop(0, groups, home, 0)

    def sent(n, _):
        for q in range(halves):
            for i in range(nc):
                far_copy(i, n, q).wait_send()
                far_back(i, n, q).wait_send()

                @pl.when(jnp.logical_not(is_self(i)))
                def _():
                    same_copy(i, n, q).wait_send()

                @pl.when(jnp.logical_not(stays & (c == i)))
                def _():
                    same_back(i, n, q).wait_send()

        return 0

    lax.fori_loop(0, parts, sent, 0)
    for d in range(1, nc):
        kernel_copy(d).wait_send()
        kernel_pass(d).wait_send()
    mask_far.wait_send()

    @pl.when(jnp.logical_not(mask_self))
    def _():
        mask_same.wait_send()

    def passed(step, _):
        for d in dirs:
            @pl.when(near[d]["good"])
            def _():
                if d[1] == 0:
                    plane_copy(step, d[0]).wait_send()
                elif d[0] == 0:
                    for n in range(parts):
                        row_copy(step, d[1], n).wait_send()
                else:
                    corner_copy(step, *d).wait_send()

        return 0

    lax.fori_loop(0, ITERS, passed, 0)


def unpack(packed, out_hbm, out, sem):
    groups, planes, _, coils, lanes = packed.shape
    row = out.shape[4]
    g = out.shape[2] // groups
    rows = packed.reshape(groups * planes * 2 * coils, lanes)
    even = lax.rem(lax.broadcasted_iota(jnp.int32, (coils, planes, 2 * row), 1), 2) == 0

    def store(m):
        at = pl.ds(m * g, g)
        return pltpu.make_async_copy(out.at[:, :, at], out_hbm.at[:, :, at], sem.at[m])

    def group(m, _):
        for ri in range(2):
            value = jnp.stack([rows[pl.ds(m * planes * 2 * coils + ri * coils + coil, planes, stride=2 * coils), :]
                               for coil in range(coils)], 0)
            left, right = value[:, :, :2 * row], value[:, :, 2 * row:]
            for q in range(g // 2):
                tile = jnp.where(even, left if q == 0 else pltpu.roll(left, planes - 1, 1), right if q else pltpu.roll(right, 1, 1))
                out[ri, :, m * g + q] = tile[:, :, :row]
                out[ri, :, m * g + g - 1 - q] = tile[:, :, row:]
        store(m).start()
        return 0

    lax.fori_loop(0, groups, group, 0)
    for m in range(groups):
        store(m).wait()


def on_device(sizes, measured, mask, kernel):
    nz, nc = sizes
    _, coils, depth_x, planes, row = measured.shape
    groups = 2 * nc
    g = depth_x // groups
    lanes = 2 * CHUNK * row
    chans = 4 * nc * coils
    parts = planes // CHUNK
    vmem = pl.BlockSpec(memory_space=pltpu.VMEM)
    dma = pltpu.SemaphoreType.DMA
    packed = pl.pallas_call(
        functools.partial(body, sizes),
        out_shape=jax.ShapeDtypeStruct((groups, planes, 2, coils, lanes), F32),
        in_specs=[pl.BlockSpec(memory_space=pltpu.HBM)] * 3,
        out_specs=vmem,
        scratch_shapes=[
            pltpu.VMEM(measured.shape, F32),
            pltpu.VMEM(mask.shape, jnp.int32),
            pltpu.VMEM(kernel.shape, F32),
            pltpu.VMEM((groups, planes, 2, coils, lanes), F32),
            pltpu.VMEM((groups, planes, lanes), F32),
            pltpu.VMEM((planes, 2, 2, nc, coils, lanes), F32),
            pltpu.VMEM((2, planes, lanes), F32),
            pltpu.VMEM((nc, 2, TAPS, coils // 2, chans), F32),
            pltpu.VMEM((TAPS, 2 * chans, 2 * chans), BF16),
            pltpu.VMEM((ITERS, planes, g, row, chans), F32),
            pltpu.VMEM((planes, g, row, chans), F32),
            pltpu.VMEM((ITERS, 3, planes + 2, g + 2, row, 2 * chans), BF16),
            pltpu.VMEM((ITERS, 2, g, row, chans), F32),
            pltpu.VMEM((ITERS, 2, planes, row, chans), F32),
            pltpu.VMEM((ITERS, 2, 2, row, chans), F32),
            pltpu.VMEM((planes, g, row, chans), F32),
            pltpu.VMEM((planes, 2, 2, nc, coils, lanes), F32),
            pltpu.VMEM((groups, planes, 2, coils, lanes), F32),
            dma((groups + 2,)),
            dma((nc, planes)), dma((nc, planes)), dma((nc, planes)), dma((nc, planes)),
            dma((nc,)), dma((nc,)), dma((nc,)), dma((nc,)), dma((2,)), dma((2,)),
            dma((ITERS, 2)), dma((ITERS, 2)), dma((ITERS, 2, parts)), dma((ITERS, 2, parts)),
            dma((ITERS, 2, 2)), dma((ITERS, 2, 2)),
            dma((nc, planes)), dma((nc, planes)), dma((nc, planes)), dma((nc, planes)),
        ],
        compiler_params=pltpu.CompilerParams(collective_id=0, has_side_effects=True, vmem_limit_bytes=VLIM << 20),
    )(*(pltpu.with_memory_space_constraint(x, pltpu.HBM) for x in (measured, mask, kernel)))
    return pl.pallas_call(
        unpack,
        out_shape=jax.ShapeDtypeStruct(measured.shape, F32),
        in_specs=[vmem],
        out_specs=pl.BlockSpec(memory_space=pl.ANY),
        scratch_shapes=[pltpu.VMEM(measured.shape, F32), dma((groups,))],
        compiler_params=pltpu.CompilerParams(vmem_limit_bytes=16 << 20),
    )(packed)


def solution(mesh):
    placed = (
        P(None, ("grp", "coil"), "kx", "kz", None),
        P(("grp", "kx"), "kz", None),
        P(None, None, "coil", None),
    )
    return jax.shard_map(
        functools.partial(on_device, (mesh.shape["kz"], mesh.shape["coil"])),
        mesh=mesh,
        in_specs=placed,
        out_specs=P(None, ("grp", "coil"), "kx", "kz", None),
        check_vma=False,
    )
```

```python
import functools

import jax
import jax.numpy as jnp
from jax import lax
from jax.experimental import pallas as pl
from jax.experimental.pallas import tpu as pltpu
from jax.sharding import PartitionSpec as P

ITERS = 2
TAPS = 27
CHUNK = 2
VLIM = 40
MESH = pl.DeviceIdType.MESH
F32, BF16 = jnp.float32, jnp.bfloat16
NT = (((1,), (1,)), ((), ()))


def split(x):
    hi = x.astype(BF16)
    return hi, (x - hi.astype(F32)).astype(BF16)


def reversal(n):
    i = lax.broadcasted_iota(jnp.int32, (n, n), 0) + lax.broadcasted_iota(jnp.int32, (n, n), 1)
    return jnp.where(i == n - 1, 1.0, 0.0).astype(BF16)


def body(sizes, measured_hbm, mask_hbm, kernel_hbm, out, measured, mask, kernel, hd, hm, rb, mb, kb, w, st, mt, xb, hz, hg, hq, acc, ob, fr,
         in_sem, s_send, s_recv, v_send, v_recv, k_send, k_recv, f_send, f_recv, m_send, m_recv,
         hz_send, hz_recv, hg_send, hg_recv, hq_send, hq_recv, os_send, os_recv, ov_send, ov_recv):
    nz, nc = sizes
    _, coils, depth_x, planes, row = measured.shape
    half = nz // 2
    groups = 2 * nc
    g = depth_x // groups
    halves = g // 2
    plane = g * row
    lanes = 2 * CHUNK * row
    band = nc * coils
    chans = 4 * band
    wide = 2 * chans
    parts = planes // CHUNK

    z, c, h = lax.axis_index("kz"), lax.axis_index("coil"), lax.axis_index("kx")
    side = lax.div(z, half)
    far = nz - 1 - z

    def owner(tz, thalf, place):
        q = lax.rem(thalf + lax.div(tz, half), 2)
        return {"kz": tz, "coil": q * (nc // 2) + lax.div(place, 2), "kx": lax.rem(place, 2)}

    kxh = lax.rem(lax.div(c, nc // 2) + side, 2)
    cc = lax.rem(c, nc // 2) * 2 + h
    stays = kxh == h

    def group_of(khalf, place):
        even = lax.rem(side + khalf + 1, 2)
        return even * place + (1 - even) * (groups - 1 - place)

    eq = lax.rem(side + kxh + 1, 2)
    mine = group_of(kxh, cc)

    def neighbour(dz, dc):
        zt = z + dz
        good = (zt >= 0) & (zt < nz)
        zt = lax.max(lax.min(zt, nz - 1), 0)
        over = lax.rem(lax.div(zt, half) + side, 2)
        inter = lax.div(cc + 1, nc) if dc > 0 else 0
        core = 1 - lax.min(cc, 1) if dc < 0 else 0
        if dc < 0:
            good = good & ((side == 1) | (cc > 0))
        flip = lax.rem(over + inter, 2)
        tz = flip * (nz - 1 - zt) + (1 - flip) * zt
        sz, sc = (dz + 1) // 2, (dc + 1) // 2
        stay = inter + core
        alone = (over * core == 1) & good
        return dict(good=good & jnp.logical_not(alone), alone=alone, flip=flip,
                    device=owner(tz, lax.rem(kxh + flip + core, 2), cc + dc - inter + core), sz=sz, sc=sc,
                    tsz=flip * sz + (1 - flip) * (1 - sz), tsc=stay * sc + (1 - stay) * (1 - sc))

    dirs = [(dz, dc) for dz in (-1, 0, 1) for dc in (-1, 0, 1) if dz or dc]
    near = {d: neighbour(*d) for d in dirs}

    def load(m):
        at = pl.ds(m * g, g)
        return pltpu.make_async_copy(measured_hbm.at[:, :, at], measured.at[:, :, at], in_sem.at[m])

    load_kernel = pltpu.make_async_copy(kernel_hbm, kernel, in_sem.at[groups])
    load_mask = pltpu.make_async_copy(mask_hbm, mask, in_sem.at[groups + 1])

    def step_group(i):
        m = group_of(h, lax.rem(i, nc))
        return jnp.where(i < nc, groups - 1 - m, m)

    load_mask.start()
    load_kernel.start()
    for i in range(groups):
        load(step_group(i)).start()

    def home_same(cx):
        return {"kz": z, "coil": cx, "kx": kxh}

    def home_far(cx):
        return {"kz": far, "coil": cx, "kx": 1 - kxh}

    def is_self(place):
        return stays & (cc == place)

    barrier = pltpu.get_barrier_semaphore()

    def greet(device):
        pl.semaphore_signal(barrier, inc=1, device_id=device, device_id_type=MESH)

    for i in range(nc):
        greet(owner(far, 1 - h, i))
        greet(home_far(i))

        @pl.when(jnp.logical_not(is_self(i)))
        def _():
            greet(owner(z, h, i))

        @pl.when(jnp.logical_not(stays & (c == i)))
        def _():
            greet(home_same(i))

    for d in range(1, nc):
        greet({"coil": lax.rem(c + d, nc)})
    greet({"kx": 1 - h})
    count = 2 * nc + 2 * (nc - stays.astype(jnp.int32)) + nc
    for d in dirs:
        @pl.when(near[d]["good"])
        def _():
            greet(near[d]["device"])
        count = count + near[d]["good"].astype(jnp.int32)

    def remote(src, dst, send, recv, device):
        return pltpu.make_async_remote_copy(
            src_ref=src, dst_ref=dst, send_sem=send, recv_sem=recv, device_id=device, device_id_type=MESH)

    def slot(n, q):
        return n * CHUNK + q

    def back_slot(n, q):
        return (parts - 1 - n) * CHUNK + q

    def same_copy(i, n, q):
        k = slot(n, q)
        return remote(hd.at[group_of(h, i), k], rb.at[k, :, 0, c], s_send.at[i, k], s_recv.at[c, k], owner(z, h, i))

    def same_land(cx, n, q):
        k = slot(n, q)
        return remote(rb.at[k, :, 0, cx], rb.at[k, :, 0, cx], s_send.at[cx, k], s_recv.at[cx, k], home_same(cx))

    def far_copy(i, n, q):
        k = back_slot(n, q)
        return remote(hd.at[groups - 1 - group_of(h, i), k], rb.at[k, :, 1, c], v_send.at[i, k], v_recv.at[c, k], owner(far, 1 - h, i))

    def far_land(cx, n, q):
        k = back_slot(n, q)
        return remote(rb.at[k, :, 1, cx], rb.at[k, :, 1, cx], v_send.at[cx, k], v_recv.at[cx, k], home_far(cx))

    def kernel_copy(d):
        return remote(kb.at[c, h], kb.at[c, h], k_send.at[d], k_recv.at[d], {"coil": lax.rem(c + d, nc)})

    def kernel_land(d):
        cx = lax.rem(c + nc - d, nc)
        return remote(kb.at[cx, h], kb.at[cx, h], k_send.at[d], k_recv.at[d], {"coil": cx})

    def kernel_pass(d):
        cx = lax.rem(c + nc - d, nc)
        return remote(kb.at[cx, h], kb.at[cx, h], f_send.at[d], f_recv.at[d], {"kx": 1 - h})

    def kernel_last(d):
        cx = lax.rem(c + nc - d, nc)
        return remote(kb.at[cx, 1 - h], kb.at[cx, 1 - h], f_send.at[d], f_recv.at[d], {"kx": 1 - h})

    mask_self = is_self(c)
    mask_same = remote(hm.at[group_of(h, c)], mb.at[0], m_send.at[0], m_recv.at[0], owner(z, h, c))
    mask_far = remote(hm.at[groups - 1 - group_of(h, c)], mb.at[1], m_send.at[1], m_recv.at[1], owner(far, 1 - h, c))
    mask_same_land = remote(mb.at[0], mb.at[0], m_send.at[0], m_recv.at[0], home_same(cc))
    mask_far_land = remote(mb.at[1], mb.at[1], m_send.at[1], m_recv.at[1], home_far(cc))

    def visit(i):
        return jnp.where(i == 0, 0, jnp.where(i == 1, parts - 1, i - 1))

    hd_rows = hd.reshape(groups * planes * 2 * coils, lanes)

    def weave(tile):
        a = jnp.concatenate([tile(0), tile(g - 1)], -1)
        axis = a.ndim - 2
        even = jnp.concatenate([a, pltpu.roll(a, planes - 1, axis)], -1)
        if halves == 1:
            return even
        b = jnp.concatenate([tile(1), tile(g - 2)], -1)
        odd = jnp.concatenate([pltpu.roll(b, 1, axis), b], -1)
        return jnp.where(lax.rem(lax.broadcasted_iota(jnp.int32, even.shape, axis), 2) == 0, even, odd)

    def pack(m):
        keep = weave(lambda i: mask[m * g + i]) == 1
        hm[m] = jnp.where(keep, 1.0, 0.0)
        for ri in range(2):
            value = jnp.where(keep, weave(lambda i: measured[ri, :, m * g + i]), 0.0)
            for coil in range(coils):
                hd_rows[pl.ds(m * planes * 2 * coils + ri * coils + coil, planes, stride=2 * coils), :] = value[coil]

    load_kernel.wait()

    joined = jnp.concatenate([kernel[:, 0], kernel[:, 1]], 2)
    for i in range(2):
        kb[c, i] = joined[:, i * (coils // 2):(i + 1) * (coils // 2)]

    lane = lax.broadcasted_iota(jnp.int32, (1, chans), 1)
    first = lax.rem(lax.div(lane, band), 2) == 0
    upper = lane >= 2 * band

    def swap(x):
        return jnp.where(first, pltpu.roll(x, chans - band, 1), pltpu.roll(x, band, 1))

    def sign(s):
        return jnp.where(upper, jnp.where(first, s, -s), 1.0)

    def weights(cx):
        def some(n, _):
            plain = jnp.concatenate([kb[cx, j, pl.ds(9 * n, 9)] for j in range(2)], 1).reshape(9 * coils, chans)
            turned = swap(plain)
            rows = (plain * sign(-1.0), turned * sign(1.0),
                    pltpu.roll(plain, 2 * band, 1) * sign(1.0), pltpu.roll(turned, 2 * band, 1) * sign(-1.0))
            for i, value in enumerate(rows):
                hi, lo = split(value)
                at = pl.multiple_of(i * band + cx * coils, coils)
                hi = jnp.concatenate([hi, hi], 1)
                lo = jnp.concatenate([lo, jnp.zeros_like(lo)], 1)
                for t in range(9):
                    tap = TAPS - 1 - (9 * n + t) if i % 2 else 9 * n + t
                    w[tap, pl.ds(at, coils), :] = hi[t * coils:(t + 1) * coils]
                    w[tap, pl.ds(chans + at, coils), :] = lo[t * coils:(t + 1) * coils]
            return 0

        lax.fori_loop(0, TAPS // 9, some, 0)

    for step in range(ITERS):
        for b in range(3):
            for k in (0, planes + 1):
                xb[step, b, k] = jnp.zeros(xb.shape[3:], BF16)
            for r in (0, g + 1):
                xb[step, b, :, r] = jnp.zeros((planes + 2, row, wide), BF16)

    for step in range(ITERS):
        for sz in range(2):
            @pl.when(jnp.logical_not(near[(2 * sz - 1, 0)]["good"]))
            def _():
                hz[step, sz] = jnp.zeros(hz.shape[2:], F32)
            for sc in range(2):
                @pl.when(jnp.logical_not(near[(2 * sz - 1, 2 * sc - 1)]["good"]))
                def _():
                    hq[step, sz, sc] = jnp.zeros(hq.shape[3:], F32)
        @pl.when(jnp.logical_not(near[(0, -1)]["good"]))
        def _():
            hg[step, 0] = jnp.zeros(hg.shape[2:], F32)

    load_mask.wait()

    def pack_all(i, _):
        m = step_group(i)
        load(m).wait()
        pack(m)

        @pl.when(i == nc - 1)
        def _():
            pl.semaphore_wait(barrier, count)
            for d in range(1, nc):
                kernel_copy(d).start()
            mask_far.start()

            for q in range(halves):
                def launch(i, _):
                    far_copy(lax.rem(i, nc), visit(lax.div(i, nc)), q).start()
                    return 0

                lax.fori_loop(0, parts * nc, launch, 0)

        @pl.when((i >= nc) & jnp.logical_not(is_self(i - nc)))
        def _():
            for q in range(halves):
                def launch(n, _):
                    same_copy(i - nc, visit(n), q).start()
                    return 0

                lax.fori_loop(0, parts, launch, 0)

        return 0

    lax.fori_loop(0, groups, pack_all, 0)

    @pl.when(jnp.logical_not(mask_self))
    def _():
        mask_same.start()

    @pl.when(mask_self)
    def _():
        mb[0] = hm[mine]

    @pl.when(stays)
    def _():
        rb[:, :, 0, c] = hd[mine]

    weights(c)
    for d in range(1, nc):
        kernel_land(d).wait_recv()
        kernel_pass(d).start()
    for d in range(1, nc):
        kernel_last(d).wait_recv()
        weights(lax.rem(c + d, nc))

    turn = reversal(lanes)
    eye = (lax.broadcasted_iota(jnp.int32, (lanes, lanes), 0) == lax.broadcasted_iota(jnp.int32, (lanes, lanes), 1))
    both = jnp.concatenate([jnp.where(eye, 1.0, 0.0).astype(BF16), turn], 1)
    def put(step, x, k, n, at):
        rows = n * len(at) * row
        j = lax.rem(lax.broadcasted_iota(jnp.int32, (rows, 1), 0), row)
        shifted = (jnp.where(j > 0, pltpu.roll(x, 1, 0), 0.0), x, jnp.where(j < row - 1, pltpu.roll(x, rows - 1, 0), 0.0))
        shifted = [jnp.concatenate(split(y), 1).reshape(n, len(at), row, wide) for y in shifted]
        for b in range(3):
            for i, r in enumerate(at):
                xb[step, b, pl.ds(k, n), r] = shifted[b][:, i]

    def pair(q):
        return q, g - 1 - q

    def transpose_in(n, q):
        none = jnp.zeros((band, lanes), F32)

        def beside(s0, v0, s1, v1):
            return jnp.concatenate([jnp.concatenate(both, 1) for both in ((s0, none), (none, v0), (s1, none), (none, v1))], 0)

        ks, kv = slot(n, q), back_slot(n, q)
        xs, xv = rb[ks, :, 0].reshape(2, band, lanes), rb[kv, :, 1].reshape(2, band, lanes)
        ms = jnp.broadcast_to(mb[0, pl.ds(ks, 1)], (band, lanes))
        mv = jnp.broadcast_to(mb[1, pl.ds(kv, 1)], (band, lanes))
        operand = [*split(beside(xs[0], xv[0], xs[1], xv[1])), beside(ms, mv, ms, mv).astype(BF16)]
        t = lax.dot_general(both, jnp.concatenate(operand, 0), NT, preferred_element_type=F32)
        x = t[:, :chans] + t[:, chans:2 * chans]
        kept = t[:, 2 * chans:].reshape(CHUNK, 2, row, chans)
        here = x.reshape(CHUNK, 2, row, chans)
        k = pl.ds(n * CHUNK, CHUNK)
        for i, r in enumerate((q, g - 1 - q)):
            mt[k, r] = kept[:, i]
            st[0, k, r] = here[:, i]
        put(0, x, n * CHUNK + 1, CHUNK, [q + 1, g - q])

    def edge(sc, inner):
        up = eq * sc + (1 - eq) * (1 - sc)
        return up * (g - 1) if inner else up * (g + 1)

    def plane_copy(step, dz):
        v = near[(dz, 0)]
        return remote(st.at[step, planes - 1 if dz > 0 else 0], hz.at[step, v["tsz"]],
                      hz_send.at[step, v["sz"]], hz_recv.at[step, v["tsz"]], v["device"])

    def row_copy(step, dc, n):
        v = near[(0, dc)]
        k = pl.ds(n * CHUNK, CHUNK)
        return remote(st.at[step, k, edge(v["sc"], True)], hg.at[step, v["tsc"], k],
                      hg_send.at[step, v["sc"], n], hg_recv.at[step, v["tsc"], n], v["device"])

    def corner_copy(step, dz, dc):
        v = near[(dz, dc)]
        return remote(st.at[step, planes - 1 if dz > 0 else 0, edge(v["sc"], True)], hq.at[step, v["tsz"], v["tsc"]],
                      hq_send.at[step, v["sz"], v["sc"]], hq_recv.at[step, v["tsz"], v["tsc"]], v["device"])

    def send_plane(step, dz):
        @pl.when(near[(dz, 0)]["good"])
        def _():
            plane_copy(step, dz).start()

    def send_rows(step, n):
        for dc in (1, -1):
            @pl.when(near[(0, dc)]["good"])
            def _():
                row_copy(step, dc, n).start()
        for dz in (-1, 1):
            @pl.when(n == (parts - 1 if dz > 0 else 0))
            def _():
                for dc in (1, -1):
                    @pl.when(near[(dz, dc)]["good"])
                    def _():
                        corner_copy(step, dz, dc).start()
                v = near[(dz, -1)]

                @pl.when(v["alone"])
                def _():
                    hq[step, v["sz"], v["sc"]] = st[step, planes - 1 if dz > 0 else 0, edge(v["sc"], True)]

    def send_planes(step, n):
        for dz in (-1, 1):
            @pl.when(n == (parts - 1 if dz > 0 else 0))
            def _():
                send_plane(step, dz)

    def flipped(x, rows):
        hi, lo = split(x)
        y = jnp.dot(reversal(rows), jnp.concatenate([hi, lo], 1), preferred_element_type=F32)
        return swap(y[:, :chans] + y[:, chans:])

    def place_halo(step, flip, buf, k, n, at):
        rows = n * len(at) * row
        x = buf[...].reshape(rows, chans)
        if flip is not None:
            x = jnp.where(flip == 1, flipped(x, rows), x)
        put(step, x, k, n, at)

    def product(xs, ws):
        p = lax.dot_general(jnp.concatenate(xs, 1), jnp.concatenate(ws, 1), NT, preferred_element_type=F32)
        return p[:, :chans] + p[:, chans:]

    def convolve(step, n):
        return product([xb[step, (t // 3) % 3, pl.ds(n * CHUNK + t % 3, CHUNK), pl.ds(t // 9, g)].reshape(CHUNK * plane, wide)
                        for t in range(TAPS)], [w[t] for t in range(TAPS)])

    def take_planes(step):
        for dz in (-1, 1):
            v = near[(dz, 0)]
            buf = hz.at[step, v["sz"]]

            @pl.when(v["good"])
            def _():
                remote(buf, buf, hz_send.at[step, v["sz"]], hz_recv.at[step, v["sz"]], v["device"]).wait_recv()

        for dz in (-1, 1):
            v = near[(dz, 0)]
            place_halo(step, v["flip"], hz.at[step, v["sz"]], v["sz"] * (planes + 1), 1, range(1, g + 1))

    def take_rows(step):
        for dc in (-1, 1):
            v = near[(0, dc)]
            buf = hg.at[step, v["sc"]]

            @pl.when(v["good"])
            def _():
                def land(n, _):
                    part = buf.at[pl.ds(n * CHUNK, CHUNK)]
                    remote(part, part, hg_send.at[step, v["sc"], n], hg_recv.at[step, v["sc"], n], v["device"]).wait_recv()
                    return 0

                lax.fori_loop(0, parts, land, 0)

            for dz in (-1, 1):
                u = near[(dz, dc)]
                corner = hq.at[step, u["sz"], u["sc"]]

                @pl.when(u["good"])
                def _():
                    remote(corner, corner, hq_send.at[step, u["sz"], u["sc"]], hq_recv.at[step, u["sz"], u["sc"]],
                           u["device"]).wait_recv()

        for dc in (-1, 1):
            v = near[(0, dc)]
            at = [edge(v["sc"], False)]
            place_halo(step, v["flip"] if dc > 0 else None, hg.at[step, v["sc"]], 1, planes, at)
            for dz in (-1, 1):
                u = near[(dz, dc)]
                place_halo(step, u["flip"], hq.at[step, u["sz"], u["sc"]], u["sz"] * (planes + 1), 1, at)

    def add_rows(step):
        for r, a in ((0, 0), (g - 1, 2)):
            taps = [9 * a + t for t in range(9)]
            p = product([xb[step, (t // 3) % 3, t % 3:t % 3 + planes, r + a].reshape(planes * row, wide) for t in taps],
                        [w[t] for t in taps])
            acc[:, r] += p.reshape(planes, row, chans)

    mask_far_land.wait_recv()

    @pl.when(jnp.logical_not(stays & (c == cc)))
    def _():
        mask_same_land.wait_recv()

    def landed(n, q):
        for cx in range(nc):
            @pl.when(jnp.logical_not(stays & (c == cx)))
            def _():
                same_land(cx, n, q).wait_recv()

            far_land(cx, n, q).wait_recv()

    def arrive(i, _):
        n, q = visit(lax.rem(i, parts)), lax.div(i, parts)
        landed(n, q)
        transpose_in(n, q)

        @pl.when(q == 0)
        def _():
            send_rows(0, n)

        @pl.when(q == halves - 1)
        def _():
            send_planes(0, n)

        return 0

    lax.fori_loop(0, parts * halves, arrive, 0)

    for step in range(ITERS - 1):
        take_rows(step)
        take_planes(step)

        def iterate(i, _):
            n = visit(i)
            k = pl.ds(n * CHUNK, CHUNK)
            rows = CHUNK * plane
            result = convolve(step, n)
            x = jnp.where(mt[k].reshape(rows, chans) > 0.5, st[0, k].reshape(rows, chans), result)
            st[step + 1, k] = x.reshape(CHUNK, g, row, chans)
            put(step + 1, x, n * CHUNK + 1, CHUNK, range(1, g + 1))
            send_rows(step + 1, n)
            send_planes(step + 1, n)
            return 0

        lax.fori_loop(0, parts, iterate, 0)

    def same_back(cx, n, q):
        k = slot(n, q)
        return remote(ob.at[k, :, 0, cx], fr.at[mine, k], os_send.at[cx, k], os_recv.at[cc, k], home_same(cx))

    def far_back(cx, n, q):
        k = back_slot(n, q)
        return remote(ob.at[k, :, 1, cx], fr.at[groups - 1 - mine, k], ov_send.at[cx, k], ov_recv.at[cc, k], home_far(cx))

    turn2 = jnp.concatenate([turn, turn], 1)

    def finish(x, n, q):
        r = jnp.stack([x[:, i] for i in pair(q)], 1).reshape(lanes, chans)
        back = jnp.dot(turn2, jnp.concatenate(split(r), 0), preferred_element_type=F32)
        y = jnp.where(first, r, back).T.reshape(2, 2, nc, coils, lanes)
        ob[slot(n, q), :, 0] = y[:, 0]
        ob[back_slot(n, q), :, 1] = y[:, 1]
        for cx in range(nc):
            far_back(cx, n, q).start()
        for cx in range(nc):
            @pl.when(jnp.logical_not(stays & (c == cx)))
            def _():
                same_back(cx, n, q).start()

    def ahead(i, _):
        n = jnp.where(i < parts - 2, i + 1, jnp.where(i == parts - 2, 0, parts - 1))

        @pl.when(i == parts - 2)
        def _():
            take_planes(ITERS - 1)

        result = convolve(ITERS - 1, n).reshape(CHUNK, g, row, chans)
        acc[pl.ds(n * CHUNK, CHUNK)] = result
        for q in range(1, halves):
            finish(result, n, q)
        return 0

    lax.fori_loop(0, parts, ahead, 0)
    take_rows(ITERS - 1)
    add_rows(ITERS - 1)

    def edges(i, _):
        n = visit(i)
        finish(acc[pl.ds(n * CHUNK, CHUNK)], n, 0)
        return 0

    lax.fori_loop(0, parts, edges, 0)

    @pl.when(stays)
    def _():
        fr[mine] = ob[:, :, 0, c]

    def merge(m):
        keep = [jnp.broadcast_to(hm[m, k:k + 1], (2 * coils, lanes)).reshape(2, coils, lanes) for k in range(planes)]
        out[m] = jnp.stack([jnp.where(keep[k] > 0.5, hd[m, k], fr[m, k]) for k in range(planes)], 0)

    def home(i, _):
        place = lax.rem(i, nc)
        m = group_of(h, place)

        def same_home(n, _):
            for q in range(halves):
                there = fr.at[m, slot(n, q)]
                k = slot(n, q)
                remote(there, there, os_send.at[place, k], os_recv.at[place, k], owner(z, h, place)).wait_recv()
            return 0

        def far_home(n, _):
            for q in range(halves):
                k = back_slot(n, q)
                there = fr.at[groups - 1 - m, k]
                remote(there, there, ov_send.at[place, k], ov_recv.at[place, k], owner(far, 1 - h, place)).wait_recv()
            return 0

        @pl.when((i < nc) & jnp.logical_not(is_self(place)))
        def _():
            lax.fori_loop(0, parts, same_home, 0)

        @pl.when(i >= nc)
        def _():
            lax.fori_loop(0, parts, far_home, 0)

        merge(jnp.where(i < nc, m, groups - 1 - m))
        return 0

    lax.fori_loop(0, groups, home, 0)

    def sent(n, _):
        for q in range(halves):
            for i in range(nc):
                far_copy(i, n, q).wait_send()
                far_back(i, n, q).wait_send()

                @pl.when(jnp.logical_not(is_self(i)))
                def _():
                    same_copy(i, n, q).wait_send()

                @pl.when(jnp.logical_not(stays & (c == i)))
                def _():
                    same_back(i, n, q).wait_send()

        return 0

    lax.fori_loop(0, parts, sent, 0)
    for d in range(1, nc):
        kernel_copy(d).wait_send()
        kernel_pass(d).wait_send()
    mask_far.wait_send()

    @pl.when(jnp.logical_not(mask_self))
    def _():
        mask_same.wait_send()

    def passed(step, _):
        for d in dirs:
            @pl.when(near[d]["good"])
            def _():
                if d[1] == 0:
                    plane_copy(step, d[0]).wait_send()
                elif d[0] == 0:
                    for n in range(parts):
                        row_copy(step, d[1], n).wait_send()
                else:
                    corner_copy(step, *d).wait_send()

        return 0

    lax.fori_loop(0, ITERS, passed, 0)


def unpack(packed, out_hbm, out, sem):
    groups, planes, _, coils, lanes = packed.shape
    row = out.shape[4]
    g = out.shape[2] // groups
    rows = packed.reshape(groups * planes * 2 * coils, lanes)
    even = lax.rem(lax.broadcasted_iota(jnp.int32, (coils, planes, 2 * row), 1), 2) == 0

    def store(m):
        at = pl.ds(m * g, g)
        return pltpu.make_async_copy(out.at[:, :, at], out_hbm.at[:, :, at], sem.at[m])

    def group(m, _):
        for ri in range(2):
            value = jnp.stack([rows[pl.ds(m * planes * 2 * coils + ri * coils + coil, planes, stride=2 * coils), :]
                               for coil in range(coils)], 0)
            left, right = value[:, :, :2 * row], value[:, :, 2 * row:]
            for q in range(g // 2):
                tile = jnp.where(even, left if q == 0 else pltpu.roll(left, planes - 1, 1), right if q else pltpu.roll(right, 1, 1))
                out[ri, :, m * g + q] = tile[:, :, :row]
                out[ri, :, m * g + g - 1 - q] = tile[:, :, row:]
        store(m).start()
        return 0

    lax.fori_loop(0, groups, group, 0)
    for m in range(groups):
        store(m).wait()


def on_device(sizes, measured, mask, kernel):
    nz, nc = sizes
    _, coils, depth_x, planes, row = measured.shape
    groups = 2 * nc
    g = depth_x // groups
    lanes = 2 * CHUNK * row
    chans = 4 * nc * coils
    parts = planes // CHUNK
    vmem = pl.BlockSpec(memory_space=pltpu.VMEM)
    dma = pltpu.SemaphoreType.DMA
    packed = pl.pallas_call(
        functools.partial(body, sizes),
        out_shape=jax.ShapeDtypeStruct((groups, planes, 2, coils, lanes), F32),
        in_specs=[pl.BlockSpec(memory_space=pltpu.HBM)] * 3,
        out_specs=vmem,
        scratch_shapes=[
            pltpu.VMEM(measured.shape, F32),
            pltpu.VMEM(mask.shape, jnp.int32),
            pltpu.VMEM(kernel.shape, F32),
            pltpu.VMEM((groups, planes, 2, coils, lanes), F32),
            pltpu.VMEM((groups, planes, lanes), F32),
            pltpu.VMEM((planes, 2, 2, nc, coils, lanes), F32),
            pltpu.VMEM((2, planes, lanes), F32),
            pltpu.VMEM((nc, 2, TAPS, coils // 2, chans), F32),
            pltpu.VMEM((TAPS, 2 * chans, 2 * chans), BF16),
            pltpu.VMEM((ITERS, planes, g, row, chans), F32),
            pltpu.VMEM((planes, g, row, chans), F32),
            pltpu.VMEM((ITERS, 3, planes + 2, g + 2, row, 2 * chans), BF16),
            pltpu.VMEM((ITERS, 2, g, row, chans), F32),
            pltpu.VMEM((ITERS, 2, planes, row, chans), F32),
            pltpu.VMEM((ITERS, 2, 2, row, chans), F32),
            pltpu.VMEM((planes, g, row, chans), F32),
            pltpu.VMEM((planes, 2, 2, nc, coils, lanes), F32),
            pltpu.VMEM((groups, planes, 2, coils, lanes), F32),
            dma((groups + 2,)),
            dma((nc, planes)), dma((nc, planes)), dma((nc, planes)), dma((nc, planes)),
            dma((nc,)), dma((nc,)), dma((nc,)), dma((nc,)), dma((2,)), dma((2,)),
            dma((ITERS, 2)), dma((ITERS, 2)), dma((ITERS, 2, parts)), dma((ITERS, 2, parts)),
            dma((ITERS, 2, 2)), dma((ITERS, 2, 2)),
            dma((nc, planes)), dma((nc, planes)), dma((nc, planes)), dma((nc, planes)),
        ],
        compiler_params=pltpu.CompilerParams(collective_id=0, has_side_effects=True, vmem_limit_bytes=VLIM << 20),
    )(*(pltpu.with_memory_space_constraint(x, pltpu.HBM) for x in (measured, mask, kernel)))
    return pl.pallas_call(
        unpack,
        out_shape=jax.ShapeDtypeStruct(measured.shape, F32),
        in_specs=[vmem],
        out_specs=pl.BlockSpec(memory_space=pl.ANY),
        scratch_shapes=[pltpu.VMEM(measured.shape, F32), dma((groups,))],
        compiler_params=pltpu.CompilerParams(vmem_limit_bytes=16 << 20),
    )(packed)


def solution(mesh):
    placed = (
        P(None, ("grp", "coil"), "kx", "kz", None),
        P(("grp", "kx"), "kz", None),
        P(None, None, "coil", None),
    )
    return jax.shard_map(
        functools.partial(on_device, (mesh.shape["kz"], mesh.shape["coil"])),
        mesh=mesh,
        in_specs=placed,
        out_specs=P(None, ("grp", "coil"), "kx", "kz", None),
        check_vma=False,
    )
```

```python
import functools

import jax
import jax.numpy as jnp
from jax import lax
from jax.experimental import pallas as pl
from jax.experimental.pallas import tpu as pltpu
from jax.sharding import PartitionSpec as P

ITERS = 2
TAPS = 27
CHUNK = 2
VLIM = 40
MESH = pl.DeviceIdType.MESH
F32, BF16 = jnp.float32, jnp.bfloat16
NT = (((1,), (1,)), ((), ()))


def split(x):
    hi = x.astype(BF16)
    return hi, (x - hi.astype(F32)).astype(BF16)


def reversal(n):
    i = lax.broadcasted_iota(jnp.int32, (n, n), 0) + lax.broadcasted_iota(jnp.int32, (n, n), 1)
    return jnp.where(i == n - 1, 1.0, 0.0).astype(BF16)


def body(sizes, measured_hbm, mask_hbm, kernel_hbm, out, measured, mask, kernel, hd, hm, rb, mb, kb, w, st, mt, xb, hz, hg, hq, acc, ob, fr,
         in_sem, s_send, s_recv, v_send, v_recv, k_send, k_recv, f_send, f_recv, m_send, m_recv,
         hz_send, hz_recv, hg_send, hg_recv, hq_send, hq_recv, os_send, os_recv, ov_send, ov_recv):
    nz, nc = sizes
    _, coils, depth_x, planes, row = measured.shape
    half = nz // 2
    groups = 2 * nc
    g = depth_x // groups
    halves = g // 2
    plane = g * row
    lanes = 2 * CHUNK * row
    band = nc * coils
    chans = 4 * band
    wide = 2 * chans
    parts = planes // CHUNK

    z, c, h = lax.axis_index("kz"), lax.axis_index("coil"), lax.axis_index("kx")
    side = lax.div(z, half)
    far = nz - 1 - z

    def owner(tz, thalf, place):
        q = lax.rem(thalf + lax.div(tz, half), 2)
        return {"kz": tz, "coil": q * (nc // 2) + lax.div(place, 2), "kx": lax.rem(place, 2)}

    kxh = lax.rem(lax.div(c, nc // 2) + side, 2)
    cc = lax.rem(c, nc // 2) * 2 + h
    stays = kxh == h

    def group_of(khalf, place):
        even = lax.rem(side + khalf + 1, 2)
        return even * place + (1 - even) * (groups - 1 - place)

    eq = lax.rem(side + kxh + 1, 2)
    mine = group_of(kxh, cc)

    def neighbour(dz, dc):
        zt = z + dz
        good = (zt >= 0) & (zt < nz)
        zt = lax.max(lax.min(zt, nz - 1), 0)
        over = lax.rem(lax.div(zt, half) + side, 2)
        inter = lax.div(cc + 1, nc) if dc > 0 else 0
        core = 1 - lax.min(cc, 1) if dc < 0 else 0
        if dc < 0:
            good = good & ((side == 1) | (cc > 0))
        flip = lax.rem(over + inter, 2)
        tz = flip * (nz - 1 - zt) + (1 - flip) * zt
        sz, sc = (dz + 1) // 2, (dc + 1) // 2
        stay = inter + core
        alone = (over * core == 1) & good
        return dict(good=good & jnp.logical_not(alone), alone=alone, flip=flip,
                    device=owner(tz, lax.rem(kxh + flip + core, 2), cc + dc - inter + core), sz=sz, sc=sc,
                    tsz=flip * sz + (1 - flip) * (1 - sz), tsc=stay * sc + (1 - stay) * (1 - sc))

    dirs = [(dz, dc) for dz in (-1, 0, 1) for dc in (-1, 0, 1) if dz or dc]
    near = {d: neighbour(*d) for d in dirs}

    def load(m):
        at = pl.ds(m * g, g)
        return pltpu.make_async_copy(measured_hbm.at[:, :, at], measured.at[:, :, at], in_sem.at[m])

    load_kernel = pltpu.make_async_copy(kernel_hbm, kernel, in_sem.at[groups])
    load_mask = pltpu.make_async_copy(mask_hbm, mask, in_sem.at[groups + 1])

    def step_group(i):
        m = group_of(h, lax.rem(i, nc))
        return jnp.where(i < nc, groups - 1 - m, m)

    def home_same(cx):
        return {"kz": z, "coil": cx, "kx": kxh}

    def home_far(cx):
        return {"kz": far, "coil": cx, "kx": 1 - kxh}

    def is_self(place):
        return stays & (cc == place)

    barrier = pltpu.get_barrier_semaphore()

    def greet(device):
        pl.semaphore_signal(barrier, inc=1, device_id=device, device_id_type=MESH)

    for i in range(nc):
        greet(owner(far, 1 - h, i))
        greet(home_far(i))

        @pl.when(jnp.logical_not(is_self(i)))
        def _():
            greet(owner(z, h, i))

        @pl.when(jnp.logical_not(stays & (c == i)))
        def _():
            greet(home_same(i))

    for d in range(1, nc):
        greet({"coil": lax.rem(c + d, nc)})
    greet({"kx": 1 - h})
    count = 2 * nc + 2 * (nc - stays.astype(jnp.int32)) + nc
    for d in dirs:
        @pl.when(near[d]["good"])
        def _():
            greet(near[d]["device"])
        count = count + near[d]["good"].astype(jnp.int32)

    load_mask.start()
    load_kernel.start()
    for i in range(groups):
        load(step_group(i)).start()

    def remote(src, dst, send, recv, device):
        return pltpu.make_async_remote_copy(
            src_ref=src, dst_ref=dst, send_sem=send, recv_sem=recv, device_id=device, device_id_type=MESH)

    def slot(n, q):
        return n * CHUNK + q

    def back_slot(n, q):
        return (parts - 1 - n) * CHUNK + q

    def same_copy(i, n, q):
        k = slot(n, q)
        return remote(hd.at[group_of(h, i), k], rb.at[k, :, 0, c], s_send.at[i, k], s_recv.at[c, k], owner(z, h, i))

    def same_land(cx, n, q):
        k = slot(n, q)
        return remote(rb.at[k, :, 0, cx], rb.at[k, :, 0, cx], s_send.at[cx, k], s_recv.at[cx, k], home_same(cx))

    def far_copy(i, n, q):
        k = back_slot(n, q)
        return remote(hd.at[groups - 1 - group_of(h, i), k], rb.at[k, :, 1, c], v_send.at[i, k], v_recv.at[c, k], owner(far, 1 - h, i))

    def far_land(cx, n, q):
        k = back_slot(n, q)
        return remote(rb.at[k, :, 1, cx], rb.at[k, :, 1, cx], v_send.at[cx, k], v_recv.at[cx, k], home_far(cx))

    def kernel_copy(d):
        return remote(kb.at[c, h], kb.at[c, h], k_send.at[d], k_recv.at[d], {"coil": lax.rem(c + d, nc)})

    def kernel_land(d):
        cx = lax.rem(c + nc - d, nc)
        return remote(kb.at[cx, h], kb.at[cx, h], k_send.at[d], k_recv.at[d], {"coil": cx})

    def kernel_pass(d):
        cx = lax.rem(c + nc - d, nc)
        return remote(kb.at[cx, h], kb.at[cx, h], f_send.at[d], f_recv.at[d], {"kx": 1 - h})

    def kernel_last(d):
        cx = lax.rem(c + nc - d, nc)
        return remote(kb.at[cx, 1 - h], kb.at[cx, 1 - h], f_send.at[d], f_recv.at[d], {"kx": 1 - h})

    mask_self = is_self(c)
    mask_same = remote(hm.at[group_of(h, c)], mb.at[0], m_send.at[0], m_recv.at[0], owner(z, h, c))
    mask_far = remote(hm.at[groups - 1 - group_of(h, c)], mb.at[1], m_send.at[1], m_recv.at[1], owner(far, 1 - h, c))
    mask_same_land = remote(mb.at[0], mb.at[0], m_send.at[0], m_recv.at[0], home_same(cc))
    mask_far_land = remote(mb.at[1], mb.at[1], m_send.at[1], m_recv.at[1], home_far(cc))

    def visit(i):
        return jnp.where(i == 0, 0, jnp.where(i == 1, parts - 1, i - 1))

    hd_rows = hd.reshape(groups * planes * 2 * coils, lanes)

    def weave(tile):
        a = jnp.concatenate([tile(0), tile(g - 1)], -1)
        axis = a.ndim - 2
        even = jnp.concatenate([a, pltpu.roll(a, planes - 1, axis)], -1)
        if halves == 1:
            return even
        b = jnp.concatenate([tile(1), tile(g - 2)], -1)
        odd = jnp.concatenate([pltpu.roll(b, 1, axis), b], -1)
        return jnp.where(lax.rem(lax.broadcasted_iota(jnp.int32, even.shape, axis), 2) == 0, even, odd)

    def pack(m):
        keep = weave(lambda i: mask[m * g + i]) == 1
        hm[m] = jnp.where(keep, 1.0, 0.0)
        for ri in range(2):
            value = jnp.where(keep, weave(lambda i: measured[ri, :, m * g + i]), 0.0)
            for coil in range(coils):
                hd_rows[pl.ds(m * planes * 2 * coils + ri * coils + coil, planes, stride=2 * coils), :] = value[coil]

    load_kernel.wait()

    joined = jnp.concatenate([kernel[:, 0], kernel[:, 1]], 2)
    for i in range(2):
        kb[c, i] = joined[:, i * (coils // 2):(i + 1) * (coils // 2)]

    lane = lax.broadcasted_iota(jnp.int32, (1, chans), 1)
    first = lax.rem(lax.div(lane, band), 2) == 0
    upper = lane >= 2 * band

    def swap(x):
        return jnp.where(first, pltpu.roll(x, chans - band, 1), pltpu.roll(x, band, 1))

    def sign(s):
        return jnp.where(upper, jnp.where(first, s, -s), 1.0)

    def weights(cx):
        def some(n, _):
            plain = jnp.concatenate([kb[cx, j, pl.ds(9 * n, 9)] for j in range(2)], 1).reshape(9 * coils, chans)
            turned = swap(plain)
            rows = (plain * sign(-1.0), turned * sign(1.0),
                    pltpu.roll(plain, 2 * band, 1) * sign(1.0), pltpu.roll(turned, 2 * band, 1) * sign(-1.0))
            for i, value in enumerate(rows):
                hi, lo = split(value)
                at = pl.multiple_of(i * band + cx * coils, coils)
                hi = jnp.concatenate([hi, hi], 1)
                lo = jnp.concatenate([lo, jnp.zeros_like(lo)], 1)
                for t in range(9):
                    tap = TAPS - 1 - (9 * n + t) if i % 2 else 9 * n + t
                    w[tap, pl.ds(at, coils), :] = hi[t * coils:(t + 1) * coils]
                    w[tap, pl.ds(chans + at, coils), :] = lo[t * coils:(t + 1) * coils]
            return 0

        lax.fori_loop(0, TAPS // 9, some, 0)

    for step in range(ITERS):
        for b in range(3):
            for k in (0, planes + 1):
                xb[step, b, k] = jnp.zeros(xb.shape[3:], BF16)
            for r in (0, g + 1):
                xb[step, b, :, r] = jnp.zeros((planes + 2, row, wide), BF16)

    for step in range(ITERS):
        for sz in range(2):
            @pl.when(jnp.logical_not(near[(2 * sz - 1, 0)]["good"]))
            def _():
                hz[step, sz] = jnp.zeros(hz.shape[2:], F32)
            for sc in range(2):
                @pl.when(jnp.logical_not(near[(2 * sz - 1, 2 * sc - 1)]["good"]))
                def _():
                    hq[step, sz, sc] = jnp.zeros(hq.shape[3:], F32)
        @pl.when(jnp.logical_not(near[(0, -1)]["good"]))
        def _():
            hg[step, 0] = jnp.zeros(hg.shape[2:], F32)

    load_mask.wait()

    def pack_all(i, _):
        m = step_group(i)
        load(m).wait()
        pack(m)

        @pl.when(i == nc - 1)
        def _():
            pl.semaphore_wait(barrier, count)
            for d in range(1, nc):
                kernel_copy(d).start()
            mask_far.start()

            for q in range(halves):
                def launch(i, _):
                    far_copy(lax.rem(i, nc), visit(lax.div(i, nc)), q).start()
                    return 0

                lax.fori_loop(0, parts * nc, launch, 0)

        @pl.when((i >= nc) & jnp.logical_not(is_self(i - nc)))
        def _():
            for q in range(halves):
                def launch(n, _):
                    same_copy(i - nc, visit(n), q).start()
                    return 0

                lax.fori_loop(0, parts, launch, 0)

        return 0

    lax.fori_loop(0, groups, pack_all, 0)

    @pl.when(jnp.logical_not(mask_self))
    def _():
        mask_same.start()

    @pl.when(mask_self)
    def _():
        mb[0] = hm[mine]

    @pl.when(stays)
    def _():
        rb[:, :, 0, c] = hd[mine]

    weights(c)
    for d in range(1, nc):
        kernel_land(d).wait_recv()
        kernel_pass(d).start()
    for d in range(1, nc):
        kernel_last(d).wait_recv()
        weights(lax.rem(c + d, nc))

    turns = {n: reversal(n) for n in sorted({lanes, plane, planes * row, row})}
    turn = turns[lanes]
    eye = (lax.broadcasted_iota(jnp.int32, (lanes, lanes), 0) == lax.broadcasted_iota(jnp.int32, (lanes, lanes), 1))
    both = jnp.concatenate([jnp.where(eye, 1.0, 0.0).astype(BF16), turn], 1)
    def put(step, x, k, n, at):
        rows = n * len(at) * row
        j = lax.rem(lax.broadcasted_iota(jnp.int32, (rows, 1), 0), row)
        shifted = (jnp.where(j > 0, pltpu.roll(x, 1, 0), 0.0), x, jnp.where(j < row - 1, pltpu.roll(x, rows - 1, 0), 0.0))
        shifted = [jnp.concatenate(split(y), 1).reshape(n, len(at), row, wide) for y in shifted]
        for b in range(3):
            for i, r in enumerate(at):
                xb[step, b, pl.ds(k, n), r] = shifted[b][:, i]

    def pair(q):
        return q, g - 1 - q

    def transpose_in(n, q):
        none = jnp.zeros((band, lanes), F32)

        def beside(s0, v0, s1, v1):
            return jnp.concatenate([jnp.concatenate(both, 1) for both in ((s0, none), (none, v0), (s1, none), (none, v1))], 0)

        ks, kv = slot(n, q), back_slot(n, q)
        xs, xv = rb[ks, :, 0].reshape(2, band, lanes), rb[kv, :, 1].reshape(2, band, lanes)
        ms = jnp.broadcast_to(mb[0, pl.ds(ks, 1)], (band, lanes))
        mv = jnp.broadcast_to(mb[1, pl.ds(kv, 1)], (band, lanes))
        operand = [*split(beside(xs[0], xv[0], xs[1], xv[1])), beside(ms, mv, ms, mv).astype(BF16)]
        t = lax.dot_general(both, jnp.concatenate(operand, 0), NT, preferred_element_type=F32)
        x = t[:, :chans] + t[:, chans:2 * chans]
        kept = t[:, 2 * chans:].reshape(CHUNK, 2, row, chans)
        here = x.reshape(CHUNK, 2, row, chans)
        k = pl.ds(n * CHUNK, CHUNK)
        for i, r in enumerate((q, g - 1 - q)):
            mt[k, r] = kept[:, i]
            st[0, k, r] = here[:, i]
        put(0, x, n * CHUNK + 1, CHUNK, [q + 1, g - q])

    def edge(sc, inner):
        up = eq * sc + (1 - eq) * (1 - sc)
        return up * (g - 1) if inner else up * (g + 1)

    def plane_copy(step, dz):
        v = near[(dz, 0)]
        return remote(st.at[step, planes - 1 if dz > 0 else 0], hz.at[step, v["tsz"]],
                      hz_send.at[step, v["sz"]], hz_recv.at[step, v["tsz"]], v["device"])

    def row_copy(step, dc, n):
        v = near[(0, dc)]
        k = pl.ds(n * CHUNK, CHUNK)
        return remote(st.at[step, k, edge(v["sc"], True)], hg.at[step, v["tsc"], k],
                      hg_send.at[step, v["sc"], n], hg_recv.at[step, v["tsc"], n], v["device"])

    def corner_copy(step, dz, dc):
        v = near[(dz, dc)]
        return remote(st.at[step, planes - 1 if dz > 0 else 0, edge(v["sc"], True)], hq.at[step, v["tsz"], v["tsc"]],
                      hq_send.at[step, v["sz"], v["sc"]], hq_recv.at[step, v["tsz"], v["tsc"]], v["device"])

    def send_plane(step, dz):
        @pl.when(near[(dz, 0)]["good"])
        def _():
            plane_copy(step, dz).start()

    def send_rows(step, n):
        for dc in (1, -1):
            @pl.when(near[(0, dc)]["good"])
            def _():
                row_copy(step, dc, n).start()
        for dz in (-1, 1):
            @pl.when(n == (parts - 1 if dz > 0 else 0))
            def _():
                for dc in (1, -1):
                    @pl.when(near[(dz, dc)]["good"])
                    def _():
                        corner_copy(step, dz, dc).start()
                v = near[(dz, -1)]

                @pl.when(v["alone"])
                def _():
                    hq[step, v["sz"], v["sc"]] = st[step, planes - 1 if dz > 0 else 0, edge(v["sc"], True)]

    def send_planes(step, n):
        for dz in (-1, 1):
            @pl.when(n == (parts - 1 if dz > 0 else 0))
            def _():
                send_plane(step, dz)

    def flipped(x, rows):
        hi, lo = split(x)
        y = jnp.dot(turns[rows], jnp.concatenate([hi, lo], 1), preferred_element_type=F32)
        return swap(y[:, :chans] + y[:, chans:])

    def place_halo(step, flip, buf, k, n, at):
        rows = n * len(at) * row
        x = buf[...].reshape(rows, chans)
        if flip is not None:
            x = jnp.where(flip == 1, flipped(x, rows), x)
        put(step, x, k, n, at)

    def product(xs, ws):
        p = lax.dot_general(jnp.concatenate(xs, 1), jnp.concatenate(ws, 1), NT, preferred_element_type=F32)
        return p[:, :chans] + p[:, chans:]

    def convolve(step, n):
        return product([xb[step, (t // 3) % 3, pl.ds(n * CHUNK + t % 3, CHUNK), pl.ds(t // 9, g)].reshape(CHUNK * plane, wide)
                        for t in range(TAPS)], [w[t] for t in range(TAPS)])

    def take_planes(step):
        for dz in (-1, 1):
            v = near[(dz, 0)]
            buf = hz.at[step, v["sz"]]

            @pl.when(v["good"])
            def _():
                remote(buf, buf, hz_send.at[step, v["sz"]], hz_recv.at[step, v["sz"]], v["device"]).wait_recv()

        for dz in (-1, 1):
            v = near[(dz, 0)]
            place_halo(step, v["flip"], hz.at[step, v["sz"]], v["sz"] * (planes + 1), 1, range(1, g + 1))

    def take_rows(step):
        for dc in (-1, 1):
            v = near[(0, dc)]
            buf = hg.at[step, v["sc"]]

            @pl.when(v["good"])
            def _():
                def land(n, _):
                    part = buf.at[pl.ds(n * CHUNK, CHUNK)]
                    remote(part, part, hg_send.at[step, v["sc"], n], hg_recv.at[step, v["sc"], n], v["device"]).wait_recv()
                    return 0

                lax.fori_loop(0, parts, land, 0)

            for dz in (-1, 1):
                u = near[(dz, dc)]
                corner = hq.at[step, u["sz"], u["sc"]]

                @pl.when(u["good"])
                def _():
                    remote(corner, corner, hq_send.at[step, u["sz"], u["sc"]], hq_recv.at[step, u["sz"], u["sc"]],
                           u["device"]).wait_recv()

        for dc in (-1, 1):
            v = near[(0, dc)]
            at = [edge(v["sc"], False)]
            place_halo(step, v["flip"] if dc > 0 else None, hg.at[step, v["sc"]], 1, planes, at)
            for dz in (-1, 1):
                u = near[(dz, dc)]
                place_halo(step, u["flip"], hq.at[step, u["sz"], u["sc"]], u["sz"] * (planes + 1), 1, at)

    def add_rows(step):
        for r, a in ((0, 0), (g - 1, 2)):
            taps = [9 * a + t for t in range(9)]
            p = product([xb[step, (t // 3) % 3, t % 3:t % 3 + planes, r + a].reshape(planes * row, wide) for t in taps],
                        [w[t] for t in taps])
            acc[:, r] += p.reshape(planes, row, chans)

    mask_far_land.wait_recv()

    @pl.when(jnp.logical_not(stays & (c == cc)))
    def _():
        mask_same_land.wait_recv()

    def landed(n, q):
        for cx in range(nc):
            @pl.when(jnp.logical_not(stays & (c == cx)))
            def _():
                same_land(cx, n, q).wait_recv()

            far_land(cx, n, q).wait_recv()

    def arrive(i, _):
        n, q = visit(lax.rem(i, parts)), lax.div(i, parts)
        landed(n, q)
        transpose_in(n, q)

        @pl.when(q == 0)
        def _():
            send_rows(0, n)

        @pl.when(q == halves - 1)
        def _():
            send_planes(0, n)

        return 0

    lax.fori_loop(0, parts * halves, arrive, 0)

    for step in range(ITERS - 1):
        take_rows(step)
        take_planes(step)

        def iterate(i, _):
            n = visit(i)
            k = pl.ds(n * CHUNK, CHUNK)
            rows = CHUNK * plane
            result = convolve(step, n)
            x = jnp.where(mt[k].reshape(rows, chans) > 0.5, st[0, k].reshape(rows, chans), result)
            st[step + 1, k] = x.reshape(CHUNK, g, row, chans)
            put(step + 1, x, n * CHUNK + 1, CHUNK, range(1, g + 1))
            send_rows(step + 1, n)
            send_planes(step + 1, n)
            return 0

        lax.fori_loop(0, parts, iterate, 0)

    def same_back(cx, n, q):
        k = slot(n, q)
        return remote(ob.at[k, :, 0, cx], fr.at[mine, k], os_send.at[cx, k], os_recv.at[cc, k], home_same(cx))

    def far_back(cx, n, q):
        k = back_slot(n, q)
        return remote(ob.at[k, :, 1, cx], fr.at[groups - 1 - mine, k], ov_send.at[cx, k], ov_recv.at[cc, k], home_far(cx))

    turn2 = jnp.concatenate([turn, turn], 1)

    def finish(x, n, q):
        r = jnp.stack([x[:, i] for i in pair(q)], 1).reshape(lanes, chans)
        back = jnp.dot(turn2, jnp.concatenate(split(r), 0), preferred_element_type=F32)
        y = jnp.where(first, r, back).T.reshape(2, 2, nc, coils, lanes)
        ob[slot(n, q), :, 0] = y[:, 0]
        ob[back_slot(n, q), :, 1] = y[:, 1]
        for cx in range(nc):
            far_back(cx, n, q).start()
        for cx in range(nc):
            @pl.when(jnp.logical_not(stays & (c == cx)))
            def _():
                same_back(cx, n, q).start()

    def ahead(i, _):
        n = jnp.where(i < parts - 2, i + 1, jnp.where(i == parts - 2, 0, parts - 1))

        @pl.when(i == parts - 2)
        def _():
            take_planes(ITERS - 1)

        result = convolve(ITERS - 1, n).reshape(CHUNK, g, row, chans)
        acc[pl.ds(n * CHUNK, CHUNK)] = result
        for q in range(1, halves):
            finish(result, n, q)
        return 0

    lax.fori_loop(0, parts, ahead, 0)
    take_rows(ITERS - 1)
    add_rows(ITERS - 1)

    def edges(i, _):
        n = visit(i)
        finish(acc[pl.ds(n * CHUNK, CHUNK)], n, 0)
        return 0

    lax.fori_loop(0, parts, edges, 0)

    @pl.when(stays)
    def _():
        fr[mine] = ob[:, :, 0, c]

    def merge(m):
        keep = [jnp.broadcast_to(hm[m, k:k + 1], (2 * coils, lanes)).reshape(2, coils, lanes) for k in range(planes)]
        out[m] = jnp.stack([jnp.where(keep[k] > 0.5, hd[m, k], fr[m, k]) for k in range(planes)], 0)

    def home(i, _):
        place = lax.rem(i, nc)
        m = group_of(h, place)

        def same_home(n, _):
            for q in range(halves):
                there = fr.at[m, slot(n, q)]
                k = slot(n, q)
                remote(there, there, os_send.at[place, k], os_recv.at[place, k], owner(z, h, place)).wait_recv()
            return 0

        def far_home(n, _):
            for q in range(halves):
                k = back_slot(n, q)
                there = fr.at[groups - 1 - m, k]
                remote(there, there, ov_send.at[place, k], ov_recv.at[place, k], owner(far, 1 - h, place)).wait_recv()
            return 0

        @pl.when((i < nc) & jnp.logical_not(is_self(place)))
        def _():
            lax.fori_loop(0, parts, same_home, 0)

        @pl.when(i >= nc)
        def _():
            lax.fori_loop(0, parts, far_home, 0)

        merge(jnp.where(i < nc, m, groups - 1 - m))
        return 0

    def sent(n, _):
        for q in range(halves):
            for i in range(nc):
                far_copy(i, n, q).wait_send()

                @pl.when(jnp.logical_not(is_self(i)))
                def _():
                    same_copy(i, n, q).wait_send()

        return 0

    lax.fori_loop(0, parts, sent, 0)
    for d in range(1, nc):
        kernel_copy(d).wait_send()
        kernel_pass(d).wait_send()
    mask_far.wait_send()

    @pl.when(jnp.logical_not(mask_self))
    def _():
        mask_same.wait_send()

    def passed(step, _):
        for d in dirs:
            @pl.when(near[d]["good"])
            def _():
                if d[1] == 0:
                    plane_copy(step, d[0]).wait_send()
                elif d[0] == 0:
                    for n in range(parts):
                        row_copy(step, d[1], n).wait_send()
                else:
                    corner_copy(step, *d).wait_send()

        return 0

    lax.fori_loop(0, ITERS, passed, 0)

    def returned(n, _):
        for q in range(halves):
            for i in range(nc):
                far_back(i, n, q).wait_send()

                @pl.when(jnp.logical_not(stays & (c == i)))
                def _():
                    same_back(i, n, q).wait_send()

        return 0

    def gather(i, _):
        @pl.when(i == nc)
        def _():
            lax.fori_loop(0, parts, returned, 0)

        return home(i, 0)

    lax.fori_loop(0, groups, gather, 0)


def unpack(packed, out_hbm, out, sem):
    groups, planes, _, coils, lanes = packed.shape
    row = out.shape[4]
    g = out.shape[2] // groups
    rows = packed.reshape(groups * planes * 2 * coils, lanes)
    even = lax.rem(lax.broadcasted_iota(jnp.int32, (coils, planes, 2 * row), 1), 2) == 0

    def store(m):
        at = pl.ds(m * g, g)
        return pltpu.make_async_copy(out.at[:, :, at], out_hbm.at[:, :, at], sem.at[m])

    def group(m, _):
        for ri in range(2):
            value = jnp.stack([rows[pl.ds(m * planes * 2 * coils + ri * coils + coil, planes, stride=2 * coils), :]
                               for coil in range(coils)], 0)
            left, right = value[:, :, :2 * row], value[:, :, 2 * row:]
            for q in range(g // 2):
                tile = jnp.where(even, left if q == 0 else pltpu.roll(left, planes - 1, 1), right if q else pltpu.roll(right, 1, 1))
                out[ri, :, m * g + q] = tile[:, :, :row]
                out[ri, :, m * g + g - 1 - q] = tile[:, :, row:]
        store(m).start()
        return 0

    lax.fori_loop(0, groups, group, 0)
    for m in range(groups):
        store(m).wait()


def on_device(sizes, measured, mask, kernel):
    nz, nc = sizes
    _, coils, depth_x, planes, row = measured.shape
    groups = 2 * nc
    g = depth_x // groups
    lanes = 2 * CHUNK * row
    chans = 4 * nc * coils
    parts = planes // CHUNK
    vmem = pl.BlockSpec(memory_space=pltpu.VMEM)
    dma = pltpu.SemaphoreType.DMA
    packed = pl.pallas_call(
        functools.partial(body, sizes),
        out_shape=jax.ShapeDtypeStruct((groups, planes, 2, coils, lanes), F32),
        in_specs=[pl.BlockSpec(memory_space=pltpu.HBM)] * 3,
        out_specs=vmem,
        scratch_shapes=[
            pltpu.VMEM(measured.shape, F32),
            pltpu.VMEM(mask.shape, jnp.int32),
            pltpu.VMEM(kernel.shape, F32),
            pltpu.VMEM((groups, planes, 2, coils, lanes), F32),
            pltpu.VMEM((groups, planes, lanes), F32),
            pltpu.VMEM((planes, 2, 2, nc, coils, lanes), F32),
            pltpu.VMEM((2, planes, lanes), F32),
            pltpu.VMEM((nc, 2, TAPS, coils // 2, chans), F32),
            pltpu.VMEM((TAPS, 2 * chans, 2 * chans), BF16),
            pltpu.VMEM((ITERS, planes, g, row, chans), F32),
            pltpu.VMEM((planes, g, row, chans), F32),
            pltpu.VMEM((ITERS, 3, planes + 2, g + 2, row, 2 * chans), BF16),
            pltpu.VMEM((ITERS, 2, g, row, chans), F32),
            pltpu.VMEM((ITERS, 2, planes, row, chans), F32),
            pltpu.VMEM((ITERS, 2, 2, row, chans), F32),
            pltpu.VMEM((planes, g, row, chans), F32),
            pltpu.VMEM((planes, 2, 2, nc, coils, lanes), F32),
            pltpu.VMEM((groups, planes, 2, coils, lanes), F32),
            dma((groups + 2,)),
            dma((nc, planes)), dma((nc, planes)), dma((nc, planes)), dma((nc, planes)),
            dma((nc,)), dma((nc,)), dma((nc,)), dma((nc,)), dma((2,)), dma((2,)),
            dma((ITERS, 2)), dma((ITERS, 2)), dma((ITERS, 2, parts)), dma((ITERS, 2, parts)),
            dma((ITERS, 2, 2)), dma((ITERS, 2, 2)),
            dma((nc, planes)), dma((nc, planes)), dma((nc, planes)), dma((nc, planes)),
        ],
        compiler_params=pltpu.CompilerParams(collective_id=0, has_side_effects=True, vmem_limit_bytes=VLIM << 20),
    )(*(pltpu.with_memory_space_constraint(x, pltpu.HBM) for x in (measured, mask, kernel)))
    return pl.pallas_call(
        unpack,
        out_shape=jax.ShapeDtypeStruct(measured.shape, F32),
        in_specs=[vmem],
        out_specs=pl.BlockSpec(memory_space=pl.ANY),
        scratch_shapes=[pltpu.VMEM(measured.shape, F32), dma((groups,))],
        compiler_params=pltpu.CompilerParams(vmem_limit_bytes=16 << 20),
    )(packed)


def solution(mesh):
    placed = (
        P(None, ("grp", "coil"), "kx", "kz", None),
        P(("grp", "kx"), "kz", None),
        P(None, None, "coil", None),
    )
    return jax.shard_map(
        functools.partial(on_device, (mesh.shape["kz"], mesh.shape["coil"])),
        mesh=mesh,
        in_specs=placed,
        out_specs=P(None, ("grp", "coil"), "kx", "kz", None),
        check_vma=False,
    )
```

```python
import functools

import jax
import jax.numpy as jnp
from jax import lax
from jax.experimental import pallas as pl
from jax.experimental.pallas import tpu as pltpu
from jax.sharding import PartitionSpec as P

ITERS = 2
TAPS = 27
CHUNK = 2
VLIM = 40
MESH = pl.DeviceIdType.MESH
F32, BF16 = jnp.float32, jnp.bfloat16
NT = (((1,), (1,)), ((), ()))


def split(x):
    hi = x.astype(BF16)
    return hi, (x - hi.astype(F32)).astype(BF16)


def reversal(n):
    i = lax.broadcasted_iota(jnp.int32, (n, n), 0) + lax.broadcasted_iota(jnp.int32, (n, n), 1)
    return jnp.where(i == n - 1, 1.0, 0.0).astype(BF16)


def body(sizes, measured_hbm, mask_hbm, kernel_hbm, out, measured, mask, kernel, hd, hm, rb, mb, kb, w, st, mt, xb, hz, hg, hq, acc, ob, fr,
         in_sem, s_send, s_recv, v_send, v_recv, k_send, k_recv, f_send, f_recv, m_send, m_recv,
         hz_send, hz_recv, hg_send, hg_recv, hq_send, hq_recv, os_send, os_recv, ov_send, ov_recv):
    nz, nc = sizes
    _, coils, depth_x, planes, row = measured.shape
    half = nz // 2
    groups = 2 * nc
    g = depth_x // groups
    halves = g // 2
    plane = g * row
    lanes = 2 * CHUNK * row
    band = nc * coils
    chans = 4 * band
    wide = 2 * chans
    parts = planes // CHUNK

    z, c, h = lax.axis_index("kz"), lax.axis_index("coil"), lax.axis_index("kx")
    side = lax.div(z, half)
    far = nz - 1 - z

    def owner(tz, thalf, place):
        q = lax.rem(thalf + lax.div(tz, half), 2)
        return {"kz": tz, "coil": q * (nc // 2) + lax.div(place, 2), "kx": lax.rem(place, 2)}

    kxh = lax.rem(lax.div(c, nc // 2) + side, 2)
    cc = lax.rem(c, nc // 2) * 2 + h
    stays = kxh == h

    def group_of(khalf, place):
        even = lax.rem(side + khalf + 1, 2)
        return even * place + (1 - even) * (groups - 1 - place)

    eq = lax.rem(side + kxh + 1, 2)
    mine = group_of(kxh, cc)

    def neighbour(dz, dc):
        zt = z + dz
        good = (zt >= 0) & (zt < nz)
        zt = lax.max(lax.min(zt, nz - 1), 0)
        over = lax.rem(lax.div(zt, half) + side, 2)
        inter = lax.div(cc + 1, nc) if dc > 0 else 0
        core = 1 - lax.min(cc, 1) if dc < 0 else 0
        if dc < 0:
            good = good & ((side == 1) | (cc > 0))
        flip = lax.rem(over + inter, 2)
        tz = flip * (nz - 1 - zt) + (1 - flip) * zt
        sz, sc = (dz + 1) // 2, (dc + 1) // 2
        stay = inter + core
        alone = (over * core == 1) & good
        return dict(good=good & jnp.logical_not(alone), alone=alone, flip=flip,
                    device=owner(tz, lax.rem(kxh + flip + core, 2), cc + dc - inter + core), sz=sz, sc=sc,
                    tsz=flip * sz + (1 - flip) * (1 - sz), tsc=stay * sc + (1 - stay) * (1 - sc))

    dirs = [(dz, dc) for dz in (-1, 0, 1) for dc in (-1, 0, 1) if dz or dc]
    near = {d: neighbour(*d) for d in dirs}

    def load(m):
        at = pl.ds(m * g, g)
        return pltpu.make_async_copy(measured_hbm.at[:, :, at], measured.at[:, :, at], in_sem.at[m])

    load_kernel = pltpu.make_async_copy(kernel_hbm, kernel, in_sem.at[groups])
    load_mask = pltpu.make_async_copy(mask_hbm, mask, in_sem.at[groups + 1])

    def step_group(i):
        m = group_of(h, lax.rem(i, nc))
        return jnp.where(i < nc, groups - 1 - m, m)

    def home_same(cx):
        return {"kz": z, "coil": cx, "kx": kxh}

    def home_far(cx):
        return {"kz": far, "coil": cx, "kx": 1 - kxh}

    def is_self(place):
        return stays & (cc == place)

    barrier = pltpu.get_barrier_semaphore()

    def greet(device):
        pl.semaphore_signal(barrier, inc=1, device_id=device, device_id_type=MESH)

    for i in range(nc):
        greet(owner(far, 1 - h, i))
        greet(home_far(i))

        @pl.when(jnp.logical_not(is_self(i)))
        def _():
            greet(owner(z, h, i))

        @pl.when(jnp.logical_not(stays & (c == i)))
        def _():
            greet(home_same(i))

    for d in range(1, nc):
        greet({"coil": lax.rem(c + d, nc)})
    greet({"kx": 1 - h})
    count = 2 * nc + 2 * (nc - stays.astype(jnp.int32)) + nc
    for d in dirs:
        @pl.when(near[d]["good"])
        def _():
            greet(near[d]["device"])
        count = count + near[d]["good"].astype(jnp.int32)

    load_mask.start()
    load_kernel.start()
    for i in range(groups):
        load(step_group(i)).start()

    def remote(src, dst, send, recv, device):
        return pltpu.make_async_remote_copy(
            src_ref=src, dst_ref=dst, send_sem=send, recv_sem=recv, device_id=device, device_id_type=MESH)

    def slot(n, q):
        return n * CHUNK + q

    def back_slot(n, q):
        return (parts - 1 - n) * CHUNK + q

    def same_copy(i, n, q):
        k = slot(n, q)
        return remote(hd.at[group_of(h, i), k], rb.at[k, :, 0, c], s_send.at[i, k], s_recv.at[c, k], owner(z, h, i))

    def same_land(cx, n, q):
        k = slot(n, q)
        return remote(rb.at[k, :, 0, cx], rb.at[k, :, 0, cx], s_send.at[cx, k], s_recv.at[cx, k], home_same(cx))

    def far_copy(i, n, q):
        k = back_slot(n, q)
        return remote(hd.at[groups - 1 - group_of(h, i), k], rb.at[k, :, 1, c], v_send.at[i, k], v_recv.at[c, k], owner(far, 1 - h, i))

    def far_land(cx, n, q):
        k = back_slot(n, q)
        return remote(rb.at[k, :, 1, cx], rb.at[k, :, 1, cx], v_send.at[cx, k], v_recv.at[cx, k], home_far(cx))

    def kernel_copy(d):
        return remote(kb.at[c, h], kb.at[c, h], k_send.at[d], k_recv.at[d], {"coil": lax.rem(c + d, nc)})

    def kernel_land(d):
        cx = lax.rem(c + nc - d, nc)
        return remote(kb.at[cx, h], kb.at[cx, h], k_send.at[d], k_recv.at[d], {"coil": cx})

    def kernel_pass(d):
        cx = lax.rem(c + nc - d, nc)
        return remote(kb.at[cx, h], kb.at[cx, h], f_send.at[d], f_recv.at[d], {"kx": 1 - h})

    def kernel_last(d):
        cx = lax.rem(c + nc - d, nc)
        return remote(kb.at[cx, 1 - h], kb.at[cx, 1 - h], f_send.at[d], f_recv.at[d], {"kx": 1 - h})

    mask_self = is_self(c)
    mask_same = remote(hm.at[group_of(h, c)], mb.at[0], m_send.at[0], m_recv.at[0], owner(z, h, c))
    mask_far = remote(hm.at[groups - 1 - group_of(h, c)], mb.at[1], m_send.at[1], m_recv.at[1], owner(far, 1 - h, c))
    mask_same_land = remote(mb.at[0], mb.at[0], m_send.at[0], m_recv.at[0], home_same(cc))
    mask_far_land = remote(mb.at[1], mb.at[1], m_send.at[1], m_recv.at[1], home_far(cc))

    def visit(i):
        return jnp.where(i == 0, 0, jnp.where(i == 1, parts - 1, i - 1))

    hd_rows = hd.reshape(groups * planes * 2 * coils, lanes)

    def weave(tile):
        a = jnp.concatenate([tile(0), tile(g - 1)], -1)
        axis = a.ndim - 2
        even = jnp.concatenate([a, pltpu.roll(a, planes - 1, axis)], -1)
        if halves == 1:
            return even
        b = jnp.concatenate([tile(1), tile(g - 2)], -1)
        odd = jnp.concatenate([pltpu.roll(b, 1, axis), b], -1)
        return jnp.where(lax.rem(lax.broadcasted_iota(jnp.int32, even.shape, axis), 2) == 0, even, odd)

    def pack(m):
        keep = weave(lambda i: mask[m * g + i]) == 1
        hm[m] = jnp.where(keep, 1.0, 0.0)
        for ri in range(2):
            value = jnp.where(keep, weave(lambda i: measured[ri, :, m * g + i]), 0.0)
            for coil in range(coils):
                hd_rows[pl.ds(m * planes * 2 * coils + ri * coils + coil, planes, stride=2 * coils), :] = value[coil]

    load_kernel.wait()

    joined = jnp.concatenate([kernel[:, 0], kernel[:, 1]], 2)
    for i in range(2):
        kb[c, i] = joined[:, i * (coils // 2):(i + 1) * (coils // 2)]

    lane = lax.broadcasted_iota(jnp.int32, (1, chans), 1)
    first = lax.rem(lax.div(lane, band), 2) == 0
    upper = lane >= 2 * band

    def swap(x):
        return jnp.where(first, pltpu.roll(x, chans - band, 1), pltpu.roll(x, band, 1))

    def sign(s):
        return jnp.where(upper, jnp.where(first, s, -s), 1.0)

    def weights(cx):
        def some(n, _):
            plain = jnp.concatenate([kb[cx, j, pl.ds(9 * n, 9)] for j in range(2)], 1).reshape(9 * coils, chans)
            turned = swap(plain)
            rows = (plain * sign(-1.0), turned * sign(1.0),
                    pltpu.roll(plain, 2 * band, 1) * sign(1.0), pltpu.roll(turned, 2 * band, 1) * sign(-1.0))
            for i, value in enumerate(rows):
                hi, lo = split(value)
                at = pl.multiple_of(i * band + cx * coils, coils)
                hi = jnp.concatenate([hi, hi], 1)
                lo = jnp.concatenate([lo, jnp.zeros_like(lo)], 1)
                for t in range(9):
                    tap = TAPS - 1 - (9 * n + t) if i % 2 else 9 * n + t
                    w[tap, pl.ds(at, coils), :] = hi[t * coils:(t + 1) * coils]
                    w[tap, pl.ds(chans + at, coils), :] = lo[t * coils:(t + 1) * coils]
            return 0

        lax.fori_loop(0, TAPS // 9, some, 0)

    for step in range(ITERS):
        for b in range(3):
            for k in (0, planes + 1):
                xb[step, b, k] = jnp.zeros(xb.shape[3:], BF16)
            for r in (0, g + 1):
                xb[step, b, :, r] = jnp.zeros((planes + 2, row, wide), BF16)

    for step in range(ITERS):
        for sz in range(2):
            @pl.when(jnp.logical_not(near[(2 * sz - 1, 0)]["good"]))
            def _():
                hz[step, sz] = jnp.zeros(hz.shape[2:], F32)
            for sc in range(2):
                @pl.when(jnp.logical_not(near[(2 * sz - 1, 2 * sc - 1)]["good"]))
                def _():
                    hq[step, sz, sc] = jnp.zeros(hq.shape[3:], F32)
        @pl.when(jnp.logical_not(near[(0, -1)]["good"]))
        def _():
            hg[step, 0] = jnp.zeros(hg.shape[2:], F32)

    load_mask.wait()

    def pack_all(i, _):
        m = step_group(i)
        load(m).wait()
        pack(m)

        @pl.when(i == nc - 1)
        def _():
            pl.semaphore_wait(barrier, count)
            for d in range(1, nc):
                kernel_copy(d).start()
            mask_far.start()

            for q in range(halves):
                def launch(i, _):
                    far_copy(lax.rem(i, nc), visit(lax.div(i, nc)), q).start()
                    return 0

                lax.fori_loop(0, parts * nc, launch, 0)

        @pl.when((i >= nc) & jnp.logical_not(is_self(i - nc)))
        def _():
            for q in range(halves):
                def launch(n, _):
                    same_copy(i - nc, visit(n), q).start()
                    return 0

                lax.fori_loop(0, parts, launch, 0)

        return 0

    lax.fori_loop(0, groups, pack_all, 0)

    @pl.when(jnp.logical_not(mask_self))
    def _():
        mask_same.start()

    @pl.when(mask_self)
    def _():
        mb[0] = hm[mine]

    @pl.when(stays)
    def _():
        rb[:, :, 0, c] = hd[mine]

    weights(c)
    for d in range(1, nc):
        kernel_land(d).wait_recv()
        kernel_pass(d).start()
    for d in range(1, nc):
        kernel_last(d).wait_recv()
        weights(lax.rem(c + d, nc))

    turns = {n: reversal(n) for n in sorted({lanes, plane, planes * row, row})}
    turn = turns[lanes]
    eye = (lax.broadcasted_iota(jnp.int32, (lanes, lanes), 0) == lax.broadcasted_iota(jnp.int32, (lanes, lanes), 1))
    both = jnp.concatenate([jnp.where(eye, 1.0, 0.0).astype(BF16), turn], 1)
    def put(step, x, k, n, at):
        rows = n * len(at) * row
        j = lax.rem(lax.broadcasted_iota(jnp.int32, (rows, 1), 0), row)
        shifted = (jnp.where(j > 0, pltpu.roll(x, 1, 0), 0.0), x, jnp.where(j < row - 1, pltpu.roll(x, rows - 1, 0), 0.0))
        shifted = [jnp.concatenate(split(y), 1).reshape(n, len(at), row, wide) for y in shifted]
        for b in range(3):
            for i, r in enumerate(at):
                xb[step, b, pl.ds(k, n), r] = shifted[b][:, i]

    def pair(q):
        return q, g - 1 - q

    def transpose_in(n, q):
        none = jnp.zeros((band, lanes), F32)

        def beside(s0, v0, s1, v1):
            return jnp.concatenate([jnp.concatenate(both, 1) for both in ((s0, none), (none, v0), (s1, none), (none, v1))], 0)

        ks, kv = slot(n, q), back_slot(n, q)
        xs, xv = rb[ks, :, 0].reshape(2, band, lanes), rb[kv, :, 1].reshape(2, band, lanes)
        ms = jnp.broadcast_to(mb[0, pl.ds(ks, 1)], (band, lanes))
        mv = jnp.broadcast_to(mb[1, pl.ds(kv, 1)], (band, lanes))
        operand = [*split(beside(xs[0], xv[0], xs[1], xv[1])), beside(ms, mv, ms, mv).astype(BF16)]
        t = lax.dot_general(both, jnp.concatenate(operand, 0), NT, preferred_element_type=F32)
        x = t[:, :chans] + t[:, chans:2 * chans]
        kept = t[:, 2 * chans:].reshape(CHUNK, 2, row, chans)
        here = x.reshape(CHUNK, 2, row, chans)
        k = pl.ds(n * CHUNK, CHUNK)
        for i, r in enumerate((q, g - 1 - q)):
            mt[k, r] = kept[:, i]
            st[0, k, r] = here[:, i]
        put(0, x, n * CHUNK + 1, CHUNK, [q + 1, g - q])

    def edge(sc, inner):
        up = eq * sc + (1 - eq) * (1 - sc)
        return up * (g - 1) if inner else up * (g + 1)

    def plane_copy(step, dz):
        v = near[(dz, 0)]
        return remote(st.at[step, planes - 1 if dz > 0 else 0], hz.at[step, v["tsz"]],
                      hz_send.at[step, v["sz"]], hz_recv.at[step, v["tsz"]], v["device"])

    def row_copy(step, dc, n):
        v = near[(0, dc)]
        k = pl.ds(n * CHUNK, CHUNK)
        return remote(st.at[step, k, edge(v["sc"], True)], hg.at[step, v["tsc"], k],
                      hg_send.at[step, v["sc"], n], hg_recv.at[step, v["tsc"], n], v["device"])

    def corner_copy(step, dz, dc):
        v = near[(dz, dc)]
        return remote(st.at[step, planes - 1 if dz > 0 else 0, edge(v["sc"], True)], hq.at[step, v["tsz"], v["tsc"]],
                      hq_send.at[step, v["sz"], v["sc"]], hq_recv.at[step, v["tsz"], v["tsc"]], v["device"])

    def send_plane(step, dz):
        @pl.when(near[(dz, 0)]["good"])
        def _():
            plane_copy(step, dz).start()

    def send_rows(step, n):
        for dc in (1, -1):
            @pl.when(near[(0, dc)]["good"])
            def _():
                row_copy(step, dc, n).start()
        for dz in (-1, 1):
            @pl.when(n == (parts - 1 if dz > 0 else 0))
            def _():
                for dc in (1, -1):
                    @pl.when(near[(dz, dc)]["good"])
                    def _():
                        corner_copy(step, dz, dc).start()
                v = near[(dz, -1)]

                @pl.when(v["alone"])
                def _():
                    hq[step, v["sz"], v["sc"]] = st[step, planes - 1 if dz > 0 else 0, edge(v["sc"], True)]

    def send_planes(step, n):
        for dz in (-1, 1):
            @pl.when(n == (parts - 1 if dz > 0 else 0))
            def _():
                send_plane(step, dz)

    def flipped(x, rows):
        hi, lo = split(x)
        y = jnp.dot(turns[rows], jnp.concatenate([hi, lo], 1), preferred_element_type=F32)
        return swap(y[:, :chans] + y[:, chans:])

    def place_halo(step, flip, buf, k, n, at):
        rows = n * len(at) * row
        x = buf[...].reshape(rows, chans)
        if flip is not None:
            x = jnp.where(flip == 1, flipped(x, rows), x)
        put(step, x, k, n, at)

    def product(xs, ws):
        p = lax.dot_general(jnp.concatenate(xs, 1), jnp.concatenate(ws, 1), NT, preferred_element_type=F32)
        return p[:, :chans] + p[:, chans:]

    def convolve(step, n):
        return product([xb[step, (t // 3) % 3, pl.ds(n * CHUNK + t % 3, CHUNK), pl.ds(t // 9, g)].reshape(CHUNK * plane, wide)
                        for t in range(TAPS)], [w[t] for t in range(TAPS)])

    def take_planes(step):
        for dz in (-1, 1):
            v = near[(dz, 0)]
            buf = hz.at[step, v["sz"]]

            @pl.when(v["good"])
            def _():
                remote(buf, buf, hz_send.at[step, v["sz"]], hz_recv.at[step, v["sz"]], v["device"]).wait_recv()

        for dz in (-1, 1):
            v = near[(dz, 0)]
            place_halo(step, v["flip"], hz.at[step, v["sz"]], v["sz"] * (planes + 1), 1, range(1, g + 1))

    def take_rows(step):
        for dc in (-1, 1):
            v = near[(0, dc)]
            buf = hg.at[step, v["sc"]]

            @pl.when(v["good"])
            def _():
                def land(n, _):
                    part = buf.at[pl.ds(n * CHUNK, CHUNK)]
                    remote(part, part, hg_send.at[step, v["sc"], n], hg_recv.at[step, v["sc"], n], v["device"]).wait_recv()
                    return 0

                lax.fori_loop(0, parts, land, 0)

            for dz in (-1, 1):
                u = near[(dz, dc)]
                corner = hq.at[step, u["sz"], u["sc"]]

                @pl.when(u["good"])
                def _():
                    remote(corner, corner, hq_send.at[step, u["sz"], u["sc"]], hq_recv.at[step, u["sz"], u["sc"]],
                           u["device"]).wait_recv()

        for dc in (-1, 1):
            v = near[(0, dc)]
            at = [edge(v["sc"], False)]
            place_halo(step, v["flip"] if dc > 0 else None, hg.at[step, v["sc"]], 1, planes, at)
            for dz in (-1, 1):
                u = near[(dz, dc)]
                place_halo(step, u["flip"], hq.at[step, u["sz"], u["sc"]], u["sz"] * (planes + 1), 1, at)

    def add_rows(step):
        for r, a in ((0, 0), (g - 1, 2)):
            taps = [9 * a + t for t in range(9)]
            p = product([xb[step, (t // 3) % 3, t % 3:t % 3 + planes, r + a].reshape(planes * row, wide) for t in taps],
                        [w[t] for t in taps])
            acc[:, r] += p.reshape(planes, row, chans)

    mask_far_land.wait_recv()

    @pl.when(jnp.logical_not(stays & (c == cc)))
    def _():
        mask_same_land.wait_recv()

    def landed(n, q):
        for cx in range(nc):
            @pl.when(jnp.logical_not(stays & (c == cx)))
            def _():
                same_land(cx, n, q).wait_recv()

            far_land(cx, n, q).wait_recv()

    def arrive(i, _):
        n, q = visit(lax.rem(i, parts)), lax.div(i, parts)
        landed(n, q)
        transpose_in(n, q)

        @pl.when(q == 0)
        def _():
            send_rows(0, n)

        @pl.when(q == halves - 1)
        def _():
            send_planes(0, n)

        return 0

    lax.fori_loop(0, parts * halves, arrive, 0)

    for step in range(ITERS - 1):
        take_rows(step)
        take_planes(step)

        def iterate(i, _):
            n = visit(i)
            k = pl.ds(n * CHUNK, CHUNK)
            rows = CHUNK * plane
            result = convolve(step, n)
            x = jnp.where(mt[k].reshape(rows, chans) > 0.5, st[0, k].reshape(rows, chans), result)
            st[step + 1, k] = x.reshape(CHUNK, g, row, chans)
            put(step + 1, x, n * CHUNK + 1, CHUNK, range(1, g + 1))
            send_rows(step + 1, n)
            send_planes(step + 1, n)
            return 0

        lax.fori_loop(0, parts, iterate, 0)

    def same_back(cx, n, q):
        k = slot(n, q)
        return remote(ob.at[k, :, 0, cx], fr.at[mine, k], os_send.at[cx, k], os_recv.at[cc, k], home_same(cx))

    def far_back(cx, n, q):
        k = back_slot(n, q)
        return remote(ob.at[k, :, 1, cx], fr.at[groups - 1 - mine, k], ov_send.at[cx, k], ov_recv.at[cc, k], home_far(cx))

    turn2 = jnp.concatenate([turn, turn], 1)

    def finish(x, n, q):
        r = jnp.stack([x[:, i] for i in pair(q)], 1).reshape(lanes, chans)
        back = jnp.dot(turn2, jnp.concatenate(split(r), 0), preferred_element_type=F32)
        y = jnp.where(first, r, back).T.reshape(2, 2, nc, coils, lanes)
        ob[back_slot(n, q), :, 1] = y[:, 1]
        for cx in range(nc):
            far_back(cx, n, q).start()
        ob[slot(n, q), :, 0] = y[:, 0]
        for cx in range(nc):
            @pl.when(jnp.logical_not(stays & (c == cx)))
            def _():
                same_back(cx, n, q).start()

    def ahead(i, _):
        n = jnp.where(i < parts - 2, i + 1, jnp.where(i == parts - 2, 0, parts - 1))

        @pl.when(i == parts - 2)
        def _():
            take_planes(ITERS - 1)

        result = convolve(ITERS - 1, n).reshape(CHUNK, g, row, chans)
        acc[pl.ds(n * CHUNK, CHUNK)] = result
        for q in range(1, halves):
            finish(result, n, q)
        return 0

    lax.fori_loop(0, parts, ahead, 0)
    take_rows(ITERS - 1)
    add_rows(ITERS - 1)

    def edges(i, _):
        n = visit(i)
        finish(acc[pl.ds(n * CHUNK, CHUNK)], n, 0)
        return 0

    lax.fori_loop(0, parts, edges, 0)

    @pl.when(stays)
    def _():
        fr[mine] = ob[:, :, 0, c]

    def merge(m):
        keep = [jnp.broadcast_to(hm[m, k:k + 1], (2 * coils, lanes)).reshape(2, coils, lanes) for k in range(planes)]
        out[m] = jnp.stack([jnp.where(keep[k] > 0.5, hd[m, k], fr[m, k]) for k in range(planes)], 0)

    def home(i, _):
        place = lax.rem(i, nc)
        m = group_of(h, place)

        def same_home(n, _):
            for q in range(halves):
                there = fr.at[m, slot(n, q)]
                k = slot(n, q)
                remote(there, there, os_send.at[place, k], os_recv.at[place, k], owner(z, h, place)).wait_recv()
            return 0

        def far_home(n, _):
            for q in range(halves):
                k = back_slot(n, q)
                there = fr.at[groups - 1 - m, k]
                remote(there, there, ov_send.at[place, k], ov_recv.at[place, k], owner(far, 1 - h, place)).wait_recv()
            return 0

        @pl.when((i < nc) & jnp.logical_not(is_self(place)))
        def _():
            lax.fori_loop(0, parts, same_home, 0)

        @pl.when(i >= nc)
        def _():
            lax.fori_loop(0, parts, far_home, 0)

        merge(jnp.where(i < nc, m, groups - 1 - m))
        return 0

    def sent(n, _):
        for q in range(halves):
            for i in range(nc):
                far_copy(i, n, q).wait_send()

                @pl.when(jnp.logical_not(is_self(i)))
                def _():
                    same_copy(i, n, q).wait_send()

        return 0

    lax.fori_loop(0, parts, sent, 0)
    for d in range(1, nc):
        kernel_copy(d).wait_send()
        kernel_pass(d).wait_send()
    mask_far.wait_send()

    @pl.when(jnp.logical_not(mask_self))
    def _():
        mask_same.wait_send()

    def passed(step, _):
        for d in dirs:
            @pl.when(near[d]["good"])
            def _():
                if d[1] == 0:
                    plane_copy(step, d[0]).wait_send()
                elif d[0] == 0:
                    for n in range(parts):
                        row_copy(step, d[1], n).wait_send()
                else:
                    corner_copy(step, *d).wait_send()

        return 0

    lax.fori_loop(0, ITERS, passed, 0)

    def returned(n, _):
        for q in range(halves):
            for i in range(nc):
                far_back(i, n, q).wait_send()

                @pl.when(jnp.logical_not(stays & (c == i)))
                def _():
                    same_back(i, n, q).wait_send()

        return 0

    def gather(i, _):
        @pl.when(i == nc)
        def _():
            lax.fori_loop(0, parts, returned, 0)

        return home(i, 0)

    lax.fori_loop(0, groups, gather, 0)


def unpack(packed, out_hbm, out, sem):
    groups, planes, _, coils, lanes = packed.shape
    row = out.shape[4]
    g = out.shape[2] // groups
    rows = packed.reshape(groups * planes * 2 * coils, lanes)
    even = lax.rem(lax.broadcasted_iota(jnp.int32, (coils, planes, 2 * row), 1), 2) == 0

    def store(m):
        at = pl.ds(m * g, g)
        return pltpu.make_async_copy(out.at[:, :, at], out_hbm.at[:, :, at], sem.at[m])

    def group(m, _):
        for ri in range(2):
            value = jnp.stack([rows[pl.ds(m * planes * 2 * coils + ri * coils + coil, planes, stride=2 * coils), :]
                               for coil in range(coils)], 0)
            left, right = value[:, :, :2 * row], value[:, :, 2 * row:]
            for q in range(g // 2):
                tile = jnp.where(even, left if q == 0 else pltpu.roll(left, planes - 1, 1), right if q else pltpu.roll(right, 1, 1))
                out[ri, :, m * g + q] = tile[:, :, :row]
                out[ri, :, m * g + g - 1 - q] = tile[:, :, row:]
        store(m).start()
        return 0

    lax.fori_loop(0, groups, group, 0)
    for m in range(groups):
        store(m).wait()


def on_device(sizes, measured, mask, kernel):
    nz, nc = sizes
    _, coils, depth_x, planes, row = measured.shape
    groups = 2 * nc
    g = depth_x // groups
    lanes = 2 * CHUNK * row
    chans = 4 * nc * coils
    parts = planes // CHUNK
    vmem = pl.BlockSpec(memory_space=pltpu.VMEM)
    dma = pltpu.SemaphoreType.DMA
    packed = pl.pallas_call(
        functools.partial(body, sizes),
        out_shape=jax.ShapeDtypeStruct((groups, planes, 2, coils, lanes), F32),
        in_specs=[pl.BlockSpec(memory_space=pltpu.HBM)] * 3,
        out_specs=vmem,
        scratch_shapes=[
            pltpu.VMEM(measured.shape, F32),
            pltpu.VMEM(mask.shape, jnp.int32),
            pltpu.VMEM(kernel.shape, F32),
            pltpu.VMEM((groups, planes, 2, coils, lanes), F32),
            pltpu.VMEM((groups, planes, lanes), F32),
            pltpu.VMEM((planes, 2, 2, nc, coils, lanes), F32),
            pltpu.VMEM((2, planes, lanes), F32),
            pltpu.VMEM((nc, 2, TAPS, coils // 2, chans), F32),
            pltpu.VMEM((TAPS, 2 * chans, 2 * chans), BF16),
            pltpu.VMEM((ITERS, planes, g, row, chans), F32),
            pltpu.VMEM((planes, g, row, chans), F32),
            pltpu.VMEM((ITERS, 3, planes + 2, g + 2, row, 2 * chans), BF16),
            pltpu.VMEM((ITERS, 2, g, row, chans), F32),
            pltpu.VMEM((ITERS, 2, planes, row, chans), F32),
            pltpu.VMEM((ITERS, 2, 2, row, chans), F32),
            pltpu.VMEM((planes, g, row, chans), F32),
            pltpu.VMEM((planes, 2, 2, nc, coils, lanes), F32),
            pltpu.VMEM((groups, planes, 2, coils, lanes), F32),
            dma((groups + 2,)),
            dma((nc, planes)), dma((nc, planes)), dma((nc, planes)), dma((nc, planes)),
            dma((nc,)), dma((nc,)), dma((nc,)), dma((nc,)), dma((2,)), dma((2,)),
            dma((ITERS, 2)), dma((ITERS, 2)), dma((ITERS, 2, parts)), dma((ITERS, 2, parts)),
            dma((ITERS, 2, 2)), dma((ITERS, 2, 2)),
            dma((nc, planes)), dma((nc, planes)), dma((nc, planes)), dma((nc, planes)),
        ],
        compiler_params=pltpu.CompilerParams(collective_id=0, has_side_effects=True, vmem_limit_bytes=VLIM << 20),
    )(*(pltpu.with_memory_space_constraint(x, pltpu.HBM) for x in (measured, mask, kernel)))
    return pl.pallas_call(
        unpack,
        out_shape=jax.ShapeDtypeStruct(measured.shape, F32),
        in_specs=[vmem],
        out_specs=pl.BlockSpec(memory_space=pl.ANY),
        scratch_shapes=[pltpu.VMEM(measured.shape, F32), dma((groups,))],
        compiler_params=pltpu.CompilerParams(vmem_limit_bytes=16 << 20),
    )(packed)


def solution(mesh):
    placed = (
        P(None, ("grp", "coil"), "kx", "kz", None),
        P(("grp", "kx"), "kz", None),
        P(None, None, "coil", None),
    )
    return jax.shard_map(
        functools.partial(on_device, (mesh.shape["kz"], mesh.shape["coil"])),
        mesh=mesh,
        in_specs=placed,
        out_specs=P(None, ("grp", "coil"), "kx", "kz", None),
        check_vma=False,
    )
```
